128 devices in a mesh: ctx: 32 (over y, z_lo, x), head: 4 (over z_hi, core).
Axes of the slice: x: 4, y: 4, z: 4 (z_hi: 2, z_lo: 2; z = z_hi * 2 + z_lo), core: 2. Of those that a mesh axis runs over, the one named last changes fastest.
Arguments:
- kda_inputs: bfloat16 [3, 4096, 4096], P(None, 'ctx', 'head'), may hold values from -4 to 4
- gate_log: float32 [4096, 4096], P('ctx', 'head'), may hold values from -2.2 to 0
- beta: float32 [4096, 32], P('ctx', 'head'), may hold values from 0.1 to 0.9
- conv_weight: float32 [3, 4, 4096], P(None, None, 'head'), may hold values from -3 to 3
- kda_out_weight: bfloat16 [4096, 2304], P('head'), may hold values from -3 to 3
- residual: bfloat16 [4096, 2304], P('ctx'), may hold values from -3 to 3
- norm_gain: float32 [2304], replicated, may hold values from 0.1 to 1.9
- latent_weight: bfloat16 [2304, 512], replicated, may hold values from -0.125 to 0.125
- latent_gain: float32 [512], replicated, may hold values from 0.1 to 1.9
- query_weight: bfloat16 [2304, 2048], P(None, 'head'), may hold values from -0.27083333 to 0.27083333
- up_weight: bfloat16 [512, 2, 2048], P(None, None, 'head'), may hold values from -0.5745243 to 0.5745243
Outputs:
- stream_out: bfloat16 [4096, 2304], P('ctx')
- attention_out: bfloat16 [4096, 2048], P('ctx', 'head')
The draws below stay inside these ranges and needn't reach their ends.
All inputs are finite; a program needn't handle non-finite values.
Results may differ from the reference program's by a relative error of at most 0.04.
Values may be sent and summed in bfloat16 or wider, within the bound.
A program may use at most 128 MiB of HBM per device.

```python
import math
import jax
import jax.numpy as jnp
from jax import lax

D = 2304
HK = 32
DK = 128
CONV = 4
LAT = 512
HM = 16
DH = 128
TOK_DEV = 128
SEQUENCE_TOKENS = 4096


def draw_gate_log(key, part):
    channel_count = HK * DK
    blocks = SEQUENCE_TOKENS // TOK_DEV
    collected_keys = jax.random.split(key, 7)
    fast_share = 0.5
    chooser = jax.random.uniform(collected_keys[0], (channel_count,), jnp.float32)
    slow_rate = jnp.exp(jax.random.uniform(collected_keys[1], (channel_count,), jnp.float32, math.log(0.03), math.log(0.3))) / SEQUENCE_TOKENS
    fast_rate = jnp.exp(jax.random.uniform(collected_keys[2], (channel_count,), jnp.float32, math.log(1.0 / 50.0), math.log(1.0 / 30.0)))
    base_rate = jnp.where(chooser < fast_share, fast_rate, slow_rate)
    block_factor = jnp.exp(jax.random.uniform(collected_keys[3], (blocks, 1, channel_count), jnp.float32, -math.log(2.0), math.log(2.0)))
    roughness = jax.random.uniform(collected_keys[4], (blocks, TOK_DEV, channel_count), jnp.float32, 0.5, 1.5)
    log_decay_rates = -(base_rate * block_factor * roughness).reshape(SEQUENCE_TOKENS, channel_count)
    segment_rows = jax.random.randint(collected_keys[5], (3,), 0, SEQUENCE_TOKENS)
    segment_decay_total = jnp.log(jax.random.uniform(collected_keys[6], (3, channel_count), jnp.float32, 0.5, 0.8))
    token_positions = jnp.arange(SEQUENCE_TOKENS)[:, None]
    for segment_index in range(3):
        log_decay_rates = log_decay_rates + jnp.where(token_positions == segment_rows[segment_index], segment_decay_total[segment_index][None, :], 0.0)
    return log_decay_rates


def draw_kda_inputs(key, part):
    channel_count = HK * DK
    entries = jnp.clip(jax.random.normal(jax.random.fold_in(key, 3), (3, SEQUENCE_TOKENS, channel_count), jnp.float32), -4.0, 4.0)
    head_keys = jax.random.split(jax.random.fold_in(key, 4), HK)
    ranking = jax.vmap(lambda head_key: jax.random.permutation(head_key, DK))(head_keys)
    strong = ranking < DK // 8
    faint_scale = math.sqrt(3.0 * (DK // 8) / SEQUENCE_TOKENS)
    key_scale = jnp.where(strong, 1.0, faint_scale).astype(jnp.float32).reshape(channel_count)
    part_scale = jnp.stack([jnp.ones_like(key_scale), key_scale, jnp.ones_like(key_scale)])
    return (entries * part_scale[:, None, :]).astype(jnp.bfloat16)


def head_strength(key, strongest):
    ranking = jax.random.permutation(jax.random.fold_in(key, 71), HM)
    return jnp.float32(strongest) ** (ranking.astype(jnp.float32) / (HM - 1))


def draw_query_weight(key, part):
    strongest = 8.0
    entries = jnp.clip(jax.random.normal(jax.random.fold_in(key, 5), (D, HM * DH), jnp.float32), -3.0, 3.0)
    column_scale = jnp.repeat(jnp.sqrt(head_strength(key, strongest)), DH)
    return (entries * column_scale[None, :] / math.sqrt(D)).astype(jnp.bfloat16)


def draw_up_weight(key, part):
    strongest = 8.0
    entries = jnp.clip(jax.random.normal(jax.random.fold_in(key, 6), (LAT, 2, HM * DH), jnp.float32), -3.0, 3.0)
    key_scale = jnp.repeat(jnp.sqrt(head_strength(key, strongest)), DH)
    both_scales = jnp.stack([key_scale, jnp.ones_like(key_scale)])
    return (entries * both_scales[None, :, :] / math.sqrt(LAT)).astype(jnp.bfloat16)


def level_of(stream_key, shape, cuts, low, high):
    loudness = 1.0
    for dim, parts in cuts:
        steps = jax.random.uniform(jax.random.fold_in(jax.random.fold_in(stream_key, 6), dim), (parts,), jnp.float32, low / len(cuts), high / len(cuts))
        loudness = loudness * jnp.repeat(jnp.exp(steps), shape[dim] // parts).reshape((-1,) + (1,) * (len(shape) - 1 - dim))
    return loudness


def scatter_about(rng, shape, deviation, bound, shards=(), kind=jnp.bfloat16):
    result = jax.random.normal(rng, shape, jnp.float32) * deviation
    if len(shards) > 0:
        result = level_of(rng, shape, shards, -0.22, 0.18) * result
    return jnp.clip(result, min=-bound, max=bound).astype(kind)


def setup_inputs(seed: int = 0) -> dict:
    keys = jax.random.split(jax.random.key(seed), 12)
    return {
        "kda_inputs": draw_kda_inputs(jax.random.fold_in(keys[11], 71), 0),
        "gate_log": draw_gate_log(jax.random.fold_in(keys[11], 71), 0),
        "beta": jnp.clip(0.1 + 0.79999997 * jax.random.uniform(keys[2], (SEQUENCE_TOKENS, HK), jnp.float32) ** level_of(keys[2], (SEQUENCE_TOKENS, HK), ((0, 32), (1, 4)), -0.2, 0.2), 0.1, 0.9),
        "conv_weight": scatter_about(keys[3], (3, CONV, HK * DK), 0.5, 3.0, ((2, 4),), jnp.float32),
        "kda_out_weight": scatter_about(keys[4], (HK * DK, D), (HK // 8) ** -0.5, 3.0, ((0, 4),)),
        "residual": scatter_about(keys[5], (SEQUENCE_TOKENS, D), 0.5, 3.0, ((0, 32),)),
        "norm_gain": jnp.clip(1.0 + 0.18 * jax.random.normal(keys[6], (D,), jnp.float32), 0.1, 1.9),
        "latent_weight": scatter_about(keys[7], (D, LAT), D ** -0.5, 0.125),
        "latent_gain": jnp.clip(1.0 + 0.18 * jax.random.normal(keys[8], (LAT,), jnp.float32), 0.1, 1.9),
        "query_weight": draw_query_weight(jax.random.fold_in(keys[11], 71), 0),
        "up_weight": draw_up_weight(jax.random.fold_in(keys[11], 71), 0),
    }


eps_norm = 1e-06
highest_precision = lax.Precision.HIGHEST

def rounded(values):
    return lax.optimization_barrier(values.astype(jnp.bfloat16))

def short_conv(signal, weights):
    widened = signal.astype(jnp.float32)
    length = widened.shape[0]
    padded = jnp.concatenate([jnp.zeros((CONV - 1, widened.shape[1]), jnp.float32), widened], axis=0)
    running = jnp.zeros_like(widened)
    for tap_index in range(CONV):
        running = running + weights[tap_index] * padded[tap_index:tap_index + length]
    return jax.nn.silu(running)

def unit_heads(activated):
    grouped = activated.reshape(activated.shape[0], -1, DK)
    scaled = grouped * lax.rsqrt(lax.optimization_barrier(jnp.sum(grouped * grouped, axis=-1, keepdims=True)) + eps_norm)
    return scaled.reshape(activated.shape)

def prepare(stream, norm_gain, latent_weight, latent_gain):
    widened = stream.astype(jnp.float32)
    normed = (widened * lax.rsqrt(lax.optimization_barrier(jnp.mean(widened * widened, axis=-1, keepdims=True)) + eps_norm) * norm_gain).astype(jnp.bfloat16)
    latent_pre = jnp.dot(normed, latent_weight, preferred_element_type=jnp.float32)
    latent = (latent_pre * lax.rsqrt(lax.optimization_barrier(jnp.mean(latent_pre * latent_pre, axis=-1, keepdims=True)) + eps_norm) * latent_gain).astype(jnp.bfloat16)
    return (normed, latent)

def attend_block(query_block, first_row, group_keys, group_values):
    query_positions = first_row + jnp.arange(query_block.shape[0], dtype=jnp.int32)
    key_positions = jnp.arange(group_keys.shape[0], dtype=jnp.int32)
    scores = jnp.einsum('qhd,khd->hqk', query_block, group_keys, precision=highest_precision) * DH ** (-0.5)
    allowed = key_positions[None, :] <= query_positions[:, None]
    peak = lax.optimization_barrier(jnp.max(jnp.where(allowed, scores, -jnp.inf), axis=-1, keepdims=True))
    weights = jnp.where(allowed, jnp.exp(scores - peak), 0.0)
    totals = lax.optimization_barrier(jnp.sum(weights, axis=-1))
    mixed = jnp.einsum('hqk,khd->qhd', rounded(weights).astype(jnp.float32), group_values, precision=highest_precision)
    return (mixed / jnp.transpose(totals)[:, :, None]).astype(jnp.bfloat16)

def reference(kda_inputs, gate_log, beta, conv_weight, kda_out_weight, residual, norm_gain, latent_weight, latent_gain, query_weight, up_weight):
    activated = [short_conv(kda_inputs[branch], conv_weight[branch]) for branch in range(3)]
    kda_query = rounded(unit_heads(activated[0]) * DK ** (-0.5)).astype(jnp.float32)
    kda_key = rounded(unit_heads(activated[1])).astype(jnp.float32)
    kda_value = rounded(activated[2]).astype(jnp.float32)
    decays = jnp.exp(gate_log)

    def advance(recurrent_state, inputs_row):
        current_query_row, current_key_row, value_row, decay_row, rate_row = inputs_row
        decayed_state = decay_row[:, :, None] * recurrent_state
        predicted_value = jnp.einsum('sa,sau->su', current_key_row, decayed_state, precision=highest_precision)
        recurrent_state = decayed_state + rate_row[:, None, None] * current_key_row[:, :, None] * (value_row - predicted_value)[:, None, :]
        return (recurrent_state, jnp.einsum('sa,sau->su', current_query_row, recurrent_state, precision=highest_precision))

    def split_heads(values):
        return values.reshape(SEQUENCE_TOKENS, HK, DK)
    _, core_rows = lax.scan(advance, jnp.zeros((HK, DK, DK), jnp.float32), (split_heads(kda_query), split_heads(kda_key), split_heads(kda_value), split_heads(decays), beta))
    kda_core = core_rows.reshape(SEQUENCE_TOKENS, HK * DK).astype(jnp.bfloat16)
    kda_proj = jnp.dot(kda_core, kda_out_weight, preferred_element_type=jnp.float32)
    stream_out = (residual.astype(jnp.float32) + kda_proj).astype(jnp.bfloat16)
    normed, latent = prepare(stream_out, norm_gain, latent_weight, latent_gain)
    mla_query = rounded(jnp.dot(normed, query_weight, preferred_element_type=jnp.float32)).astype(jnp.float32).reshape(SEQUENCE_TOKENS, HM, DH)
    paired = rounded(jnp.dot(latent, up_weight.reshape(LAT, 2 * HM * DH), preferred_element_type=jnp.float32)).astype(jnp.float32).reshape(SEQUENCE_TOKENS, 2, HM, DH)
    keys_all = paired[:, 0]
    values_all = paired[:, 1]
    block_rows = math.gcd(SEQUENCE_TOKENS, 256)
    block_count = SEQUENCE_TOKENS // block_rows
    group_count = math.gcd(block_count, 8)
    per_group = block_count // group_count
    query_blocks = mla_query.reshape(block_count, block_rows, HM, DH)
    results = []
    for group_index in range(group_count):
        first_block = group_index * per_group
        key_end = (first_block + per_group) * block_rows
        group_keys = keys_all[:key_end]
        group_values = values_all[:key_end]
        starts = (first_block + jnp.arange(per_group, dtype=jnp.int32)) * block_rows
        group_out = lax.map(lambda item_pair: attend_block(item_pair[1], item_pair[0], group_keys, group_values), (starts, query_blocks[first_block:first_block + per_group]))
        results.append(group_out.reshape(per_group * block_rows, HM * DH))
    attention_out = jnp.concatenate(results, axis=0)
    return (stream_out, attention_out)
```

```python
import math

import jax
import jax.numpy as jnp
from jax import lax
from jax.sharding import PartitionSpec as P

DK = 128
CONV = 4
DH = 128


eps_norm = 1e-06
highest_precision = lax.Precision.HIGHEST


def passed_along(block, axis, distance):
    devices = range(lax.axis_size(axis))
    route = [(i - distance, i) for i in devices if i - distance in devices]
    return lax.ppermute(block, axis, route)


def rounded(values):
    return lax.optimization_barrier(values.astype(jnp.bfloat16))


def unit_heads(activated):
    grouped = activated.reshape(activated.shape[0], -1, DK)
    scaled = grouped * lax.rsqrt(jnp.sum(grouped * grouped, axis=-1, keepdims=True) + eps_norm)
    return scaled.reshape(activated.shape)


def prepare(stream, norm_gain, latent_weight, latent_gain):
    widened = stream.astype(jnp.float32)
    normed = (
        widened
        * lax.rsqrt(jnp.mean(widened * widened, axis=-1, keepdims=True) + eps_norm)
        * norm_gain
    ).astype(jnp.bfloat16)
    latent_pre = jnp.dot(normed, latent_weight, preferred_element_type=jnp.float32)
    latent = (
        latent_pre
        * lax.rsqrt(jnp.mean(latent_pre * latent_pre, axis=-1, keepdims=True) + eps_norm)
        * latent_gain
    ).astype(jnp.bfloat16)
    return (normed, latent)


def span_layout(values, span_rows):
    length, channel_count = values.shape
    return values.reshape(length // span_rows, span_rows, channel_count // DK, DK).transpose(
        0, 2, 1, 3
    )


def matmul_heads(left, right):
    return jnp.einsum("hij,hjk->hik", left, right, precision=highest_precision)


def matmul_batched(left, right):
    return jnp.einsum("...ij,...jk->...ik", left, right, precision=highest_precision)


def unit_lower_inverse(system):
    size = system.shape[-1]
    rows = jnp.arange(size)[:, None]
    cols = jnp.arange(size)[None, :]
    inverse = jnp.broadcast_to(jnp.eye(size, dtype=system.dtype), system.shape)
    width = 1
    while width < size:
        below = (rows // (2 * width) == cols // (2 * width)) & (rows // width != cols // width)
        off_block = jnp.where(below, system, 0.0)
        correction = matmul_batched(matmul_batched(inverse, off_block), inverse)
        inverse = inverse - lax.optimization_barrier(correction)
        width *= 2
    return inverse


def delta_rule(kda_query, kda_key, kda_value, gate_log, beta):
    span_rows = 32
    length, channel_count = gate_log.shape
    heads = channel_count // DK
    queries = span_layout(kda_query.astype(jnp.float32), span_rows)
    keys_unit = span_layout(kda_key.astype(jnp.float32), span_rows)
    values_new = span_layout(kda_value.astype(jnp.float32), span_rows)
    cumulative = jnp.cumsum(span_layout(gate_log, span_rows), axis=2)
    rates = beta.reshape(length // span_rows, span_rows, heads).transpose(0, 2, 1)[..., None]
    growth = jnp.exp(cumulative)
    final_log = cumulative[:, :, -1:, :]
    keys_grown = keys_unit * growth
    keys_shrunk = keys_unit * jnp.exp(-cumulative)
    queries_grown = queries * growth
    keys_final = keys_unit * jnp.exp(final_log - cumulative)
    strict = jnp.tril(jnp.ones((span_rows, span_rows), jnp.float32), -1)
    inclusive = jnp.tril(jnp.ones((span_rows, span_rows), jnp.float32))
    coupling = (
        jnp.einsum("nhtc,nhsc->nhts", keys_grown, keys_shrunk, precision=highest_precision)
        * jnp.swapaxes(rates, -1, -2)
        * strict
    )
    system = coupling + jnp.eye(span_rows, dtype=jnp.float32)
    solved = matmul_batched(
        unit_lower_inverse(system), jnp.concatenate([values_new, keys_grown], axis=-1)
    )
    fresh = solved[..., :DK] * rates
    carried = solved[..., DK:] * rates
    eye_key = jnp.eye(DK, dtype=jnp.float32)
    transition = jnp.exp(final_log[:, :, 0, :])[..., :, None] * eye_key - jnp.einsum(
        "nhsk,nhsv->nhkv", keys_final, carried, precision=highest_precision
    )
    offset = jnp.einsum("nhsk,nhsv->nhkv", keys_final, fresh, precision=highest_precision)
    mixing = (
        jnp.einsum("nhtc,nhsc->nhts", queries_grown, keys_shrunk, precision=highest_precision)
        * inclusive
    )

    def compose(accumulated, span_parts):
        span_move, span_shift = span_parts
        return (
            (
                matmul_heads(span_move, accumulated[0]),
                matmul_heads(span_move, accumulated[1]) + span_shift,
            ),
            None,
        )

    identity_map = jnp.broadcast_to(eye_key, (heads, DK, DK))
    zero_map = jnp.zeros((heads, DK, DK), jnp.float32)
    (device_move, device_shift), _ = lax.scan(
        compose, (identity_map, zero_map), (transition, offset)
    )
    return (device_move, device_shift, (transition, offset, fresh, carried, queries_grown, mixing))


def emit_spans(start_state, span_data):

    def emit(recurrent_state, span_parts):
        span_move, span_shift, fresh_state_term, carried_state_term, query_term, mixing_part = (
            span_parts
        )
        state_update = fresh_state_term - jnp.einsum(
            "orm,omj->orj", carried_state_term, recurrent_state, precision=highest_precision
        )
        produced_output = jnp.einsum(
            "fmb,fbi->fmi", query_term, recurrent_state, precision=highest_precision
        ) + jnp.einsum("hts,hsv->htv", mixing_part, state_update, precision=highest_precision)
        return (matmul_heads(span_move, recurrent_state) + span_shift, produced_output)

    _, outputs = lax.scan(emit, start_state, span_data)
    block_count, heads, span_rows, _ = outputs.shape
    return (
        outputs.transpose(0, 2, 1, 3)
        .reshape(block_count * span_rows, heads * DK)
        .astype(jnp.bfloat16)
    )


def per_device(
    kda_inputs,
    gate_log,
    beta,
    conv_weight,
    kda_out_weight,
    residual,
    norm_gain,
    latent_weight,
    latent_gain,
    query_weight,
    up_weight,
):
    length = residual.shape[0]
    edge_rows = kda_inputs[:, length - (CONV - 1) :, :]
    earlier_rows = passed_along(edge_rows, "ctx", 1)
    extended = jnp.concatenate([earlier_rows, kda_inputs], axis=1).astype(jnp.float32)
    running = jnp.zeros(kda_inputs.shape, jnp.float32)
    for tap_index in range(CONV):
        running = (
            running
            + conv_weight[:, tap_index, None, :] * extended[:, tap_index : tap_index + length, :]
        )
    activated = jax.nn.silu(running)
    kda_query = rounded(unit_heads(activated[0]) * DK ** (-0.5))
    kda_key = rounded(unit_heads(activated[1]))
    kda_value = rounded(activated[2])
    device_move, device_shift, span_data = delta_rule(kda_query, kda_key, kda_value, gate_log, beta)
    heads = device_move.shape[0]

    ctx_size = lax.axis_size("ctx")
    move, shift = device_move, device_shift
    distance = 1
    while distance < ctx_size:
        shift_in = passed_along(shift, "ctx", distance)
        if 2 * distance < ctx_size:
            move_in = passed_along(move, "ctx", distance)
            shift = matmul_heads(move, shift_in) + shift
            move = matmul_heads(move, move_in)
        else:
            shift = matmul_heads(move, shift_in) + shift
        distance *= 2
    start_state = passed_along(shift, "ctx", 1)
    kda_core = emit_spans(start_state, span_data)
    partial_proj = jnp.dot(kda_core, kda_out_weight, preferred_element_type=jnp.float32)
    summed = lax.psum(partial_proj, "head")
    stream_out = (residual.astype(jnp.float32) + summed).astype(jnp.bfloat16)
    normed, latent = prepare(stream_out, norm_gain, latent_weight, latent_gain)
    mla_query = jnp.dot(normed, query_weight, preferred_element_type=jnp.float32).astype(
        jnp.bfloat16
    )
    query_heads = mla_query.reshape(length, -1, DH)
    heads_mla = query_heads.shape[1]
    flat_up = up_weight.reshape(up_weight.shape[0], -1)
    my_first = lax.axis_index("ctx") * length
    query_positions = my_first + jnp.arange(length, dtype=jnp.int32)
    initial = (
        jnp.full((heads_mla, length), -1e30, jnp.float32),
        jnp.zeros((heads_mla, length), jnp.float32),
        jnp.zeros((heads_mla, length, DH), jnp.float32),
    )
    piece = lax.all_gather(latent, "ctx", axis=0, tiled=True)
    piece_rows = piece.shape[0]
    block_rows = math.gcd(piece_rows, 512)
    blocks = piece.reshape(piece_rows // block_rows, block_rows, piece.shape[1])

    def one_block(state_parts, block_parts):
        block_index, latent_block = block_parts
        running_peak, running_total, running_mixed = state_parts
        paired = (
            jnp.dot(latent_block, flat_up, preferred_element_type=jnp.float32)
            .astype(jnp.bfloat16)
            .reshape(block_rows, 2, heads_mla, DH)
        )
        scores = jnp.einsum(
            "qhd,khd->hqk", query_heads, paired[:, 0], preferred_element_type=jnp.float32
        ) * DH ** (-0.5)
        key_positions = block_index * block_rows + jnp.arange(block_rows, dtype=jnp.int32)
        allowed = key_positions[None, :] <= query_positions[:, None]
        new_peak = jnp.maximum(running_peak, jnp.max(jnp.where(allowed, scores, -1e30), axis=-1))
        weights = jnp.where(allowed, jnp.exp(scores - new_peak[..., None]), 0.0)
        factor = jnp.exp(running_peak - new_peak)
        new_total = running_total * factor + jnp.sum(weights, axis=-1)
        new_mixed = running_mixed * factor[..., None] + jnp.einsum(
            "hqk,khd->hqd",
            weights.astype(jnp.bfloat16),
            paired[:, 1],
            preferred_element_type=jnp.float32,
        )
        return ((new_peak, new_total, new_mixed), None)

    def attend(state_parts):
        return lax.scan(
            one_block, state_parts, (jnp.arange(piece_rows // block_rows, dtype=jnp.int32), blocks)
        )[0]

    final_peak, final_total, final_mixed = lax.cond(
        jnp.int32(0) < my_first + length, attend, lambda state_parts: state_parts, initial
    )
    attention_out = (
        (final_mixed / final_total[..., None])
        .transpose(1, 0, 2)
        .reshape(length, heads_mla * DH)
        .astype(jnp.bfloat16)
    )
    return (stream_out, attention_out)


def solution(mesh):
    in_specs = (
        P(None, "ctx", "head"),
        P("ctx", "head"),
        P("ctx", "head"),
        P(None, None, "head"),
        P("head", None),
        P("ctx", None),
        P(),
        P(),
        P(),
        P(None, "head"),
        P(None, None, "head"),
    )
    out_specs = (P("ctx", None), P("ctx", "head"))
    return jax.shard_map(
        per_device, mesh=mesh, in_specs=in_specs, out_specs=out_specs, check_vma=False
    )
```

```python
import math

import jax
import jax.numpy as jnp
from jax import lax
from jax.sharding import PartitionSpec as P
from jax.experimental import pallas as pl
from jax.experimental.pallas import tpu as pltpu

DK = 128
CONV = 4
DH = 128


eps_norm = 1e-06
highest_precision = lax.Precision.HIGHEST


def passed_along(block, axis, distance):
    devices = range(lax.axis_size(axis))
    route = [(i - distance, i) for i in devices if i - distance in devices]
    return lax.ppermute(block, axis, route)


def summed_over_head(partial):
    total = partial
    for partner_bit in (1, 2):
        size = lax.axis_size("head")
        route = [(i, i ^ partner_bit) for i in range(size)]
        total = total + lax.ppermute(total, "head", route)
    return total


def gather_kernel(block_ref, out_ref, send_sems, recv_sems):
    me = lax.axis_index("ctx")
    count = out_ref.shape[0]
    out_ref[me] = block_ref[...]

    def outgoing(peer):
        return pltpu.make_async_remote_copy(
            src_ref=block_ref,
            dst_ref=out_ref.at[me],
            send_sem=send_sems.at[peer],
            recv_sem=recv_sems.at[me],
            device_id={"ctx": peer},
            device_id_type=pl.DeviceIdType.MESH,
        )

    def incoming(peer):
        return pltpu.make_async_remote_copy(
            src_ref=block_ref,
            dst_ref=out_ref.at[peer],
            send_sem=send_sems.at[peer],
            recv_sem=recv_sems.at[peer],
            device_id={"ctx": peer},
            device_id_type=pl.DeviceIdType.MESH,
        )

    @pl.loop(me + 1, count)
    def _(peer):
        outgoing(peer).start()

    @pl.loop(me + 1, count)
    def _(peer):
        out_ref[peer] = jnp.zeros(block_ref.shape, block_ref.dtype)

    @pl.loop(0, me)
    def _(peer):
        incoming(peer).wait_recv()

    @pl.loop(me + 1, count)
    def _(peer):
        outgoing(peer).wait_send()


def gathered_earlier(block):
    count = lax.axis_size("ctx")
    rows, width = block.shape
    stacked = pl.pallas_call(
        gather_kernel,
        out_shape=jax.ShapeDtypeStruct((count, rows, width), block.dtype),
        in_specs=[pl.BlockSpec(memory_space=pltpu.VMEM)],
        out_specs=pl.BlockSpec(memory_space=pltpu.VMEM),
        scratch_shapes=[pltpu.SemaphoreType.DMA((count,)), pltpu.SemaphoreType.DMA((count,))],
        compiler_params=pltpu.CompilerParams(has_side_effects=True),
    )(block)
    return stacked.reshape(count * rows, width)


def rounded(values):
    return lax.optimization_barrier(values.astype(jnp.bfloat16))


def unit_heads(activated):
    grouped = activated.reshape(activated.shape[0], -1, DK)
    scaled = grouped * lax.rsqrt(jnp.sum(grouped * grouped, axis=-1, keepdims=True) + eps_norm)
    return scaled.reshape(activated.shape)


def prepare(stream, norm_gain, latent_weight, latent_gain):
    widened = stream.astype(jnp.float32)
    normed = (
        widened
        * lax.rsqrt(jnp.mean(widened * widened, axis=-1, keepdims=True) + eps_norm)
        * norm_gain
    ).astype(jnp.bfloat16)
    latent_pre = jnp.dot(normed, latent_weight, preferred_element_type=jnp.float32)
    latent = (
        latent_pre
        * lax.rsqrt(jnp.mean(latent_pre * latent_pre, axis=-1, keepdims=True) + eps_norm)
        * latent_gain
    ).astype(jnp.bfloat16)
    return (normed, latent)


def span_layout(values, span_rows):
    length, channel_count = values.shape
    return values.reshape(length // span_rows, span_rows, channel_count // DK, DK).transpose(
        0, 2, 1, 3
    )


def matmul_heads(left, right):
    return jnp.einsum("hij,hjk->hik", left, right, precision=highest_precision)


def matmul_batched(left, right):
    return jnp.einsum("...ij,...jk->...ik", left, right, precision=highest_precision)


def unit_lower_inverse(system):
    size = system.shape[-1]
    rows = jnp.arange(size)[:, None]
    cols = jnp.arange(size)[None, :]
    inverse = jnp.broadcast_to(jnp.eye(size, dtype=system.dtype), system.shape)
    width = 1
    while width < size:
        below = (rows // (2 * width) == cols // (2 * width)) & (rows // width != cols // width)
        off_block = jnp.where(below, system, 0.0)
        correction = matmul_batched(matmul_batched(inverse, off_block), inverse)
        inverse = inverse - lax.optimization_barrier(correction)
        width *= 2
    return inverse


def delta_rule(kda_query, kda_key, kda_value, gate_log, beta):
    span_rows = 32
    length, channel_count = gate_log.shape
    heads = channel_count // DK
    queries = span_layout(kda_query.astype(jnp.float32), span_rows)
    keys_unit = span_layout(kda_key.astype(jnp.float32), span_rows)
    values_new = span_layout(kda_value.astype(jnp.float32), span_rows)
    cumulative = jnp.cumsum(span_layout(gate_log, span_rows), axis=2)
    rates = beta.reshape(length // span_rows, span_rows, heads).transpose(0, 2, 1)[..., None]
    growth = jnp.exp(cumulative)
    final_log = cumulative[:, :, -1:, :]
    keys_grown = keys_unit * growth
    keys_shrunk = keys_unit * jnp.exp(-cumulative)
    queries_grown = queries * growth
    keys_final = keys_unit * jnp.exp(final_log - cumulative)
    strict = jnp.tril(jnp.ones((span_rows, span_rows), jnp.float32), -1)
    inclusive = jnp.tril(jnp.ones((span_rows, span_rows), jnp.float32))
    coupling = (
        jnp.einsum("nhtc,nhsc->nhts", keys_grown, keys_shrunk, precision=highest_precision)
        * jnp.swapaxes(rates, -1, -2)
        * strict
    )
    system = coupling + jnp.eye(span_rows, dtype=jnp.float32)
    solved = matmul_batched(
        unit_lower_inverse(system), jnp.concatenate([values_new, keys_grown], axis=-1)
    )
    fresh = solved[..., :DK] * rates
    carried = solved[..., DK:] * rates
    eye_key = jnp.eye(DK, dtype=jnp.float32)
    transition = jnp.exp(final_log[:, :, 0, :])[..., :, None] * eye_key - jnp.einsum(
        "nhsk,nhsv->nhkv", keys_final, carried, precision=highest_precision
    )
    offset = jnp.einsum("nhsk,nhsv->nhkv", keys_final, fresh, precision=highest_precision)
    mixing = (
        jnp.einsum("nhtc,nhsc->nhts", queries_grown, keys_shrunk, precision=highest_precision)
        * inclusive
    )

    def compose(accumulated, span_parts):
        span_move, span_shift = span_parts
        return (
            (
                matmul_heads(span_move, accumulated[0]),
                matmul_heads(span_move, accumulated[1]) + span_shift,
            ),
            None,
        )

    identity_map = jnp.broadcast_to(eye_key, (heads, DK, DK))
    zero_map = jnp.zeros((heads, DK, DK), jnp.float32)
    (device_move, device_shift), _ = lax.scan(
        compose, (identity_map, zero_map), (transition, offset)
    )
    return (device_move, device_shift, (transition, offset, fresh, carried, queries_grown, mixing))


def emit_spans(start_state, span_data):

    def emit(recurrent_state, span_parts):
        span_move, span_shift, fresh_state_term, carried_state_term, query_term, mixing_part = (
            span_parts
        )
        state_update = fresh_state_term - jnp.einsum(
            "orm,omj->orj", carried_state_term, recurrent_state, precision=highest_precision
        )
        produced_output = jnp.einsum(
            "fmb,fbi->fmi", query_term, recurrent_state, precision=highest_precision
        ) + jnp.einsum("hts,hsv->htv", mixing_part, state_update, precision=highest_precision)
        return (matmul_heads(span_move, recurrent_state) + span_shift, produced_output)

    _, outputs = lax.scan(emit, start_state, span_data)
    block_count, heads, span_rows, _ = outputs.shape
    return (
        outputs.transpose(0, 2, 1, 3)
        .reshape(block_count * span_rows, heads * DK)
        .astype(jnp.bfloat16)
    )


def per_device(
    kda_inputs,
    gate_log,
    beta,
    conv_weight,
    kda_out_weight,
    residual,
    norm_gain,
    latent_weight,
    latent_gain,
    query_weight,
    up_weight,
):
    length = residual.shape[0]
    edge_rows = kda_inputs[:, length - (CONV - 1) :, :]
    earlier_rows = passed_along(edge_rows, "ctx", 1)
    extended = jnp.concatenate([earlier_rows, kda_inputs], axis=1).astype(jnp.float32)
    running = jnp.zeros(kda_inputs.shape, jnp.float32)
    for tap_index in range(CONV):
        running = (
            running
            + conv_weight[:, tap_index, None, :] * extended[:, tap_index : tap_index + length, :]
        )
    activated = jax.nn.silu(running)
    kda_query = rounded(unit_heads(activated[0]) * DK ** (-0.5))
    kda_key = rounded(unit_heads(activated[1]))
    kda_value = rounded(activated[2])
    device_move, device_shift, span_data = delta_rule(kda_query, kda_key, kda_value, gate_log, beta)
    heads = device_move.shape[0]

    ctx_size = lax.axis_size("ctx")
    move, shift = device_move, device_shift
    distance = 1
    while distance < ctx_size:
        shift_in = passed_along(shift, "ctx", distance)
        if 2 * distance < ctx_size:
            move_in = passed_along(move, "ctx", distance)
            shift = matmul_heads(move, shift_in) + shift
            move = matmul_heads(move, move_in)
        else:
            shift = matmul_heads(move, shift_in) + shift
        distance *= 2
    start_state = passed_along(shift, "ctx", 1)
    kda_core = emit_spans(start_state, span_data)
    partial_proj = jnp.dot(kda_core, kda_out_weight, preferred_element_type=jnp.float32)
    summed = summed_over_head(partial_proj)
    stream_out = (residual.astype(jnp.float32) + summed).astype(jnp.bfloat16)
    normed, latent = prepare(stream_out, norm_gain, latent_weight, latent_gain)
    mla_query = jnp.dot(normed, query_weight, preferred_element_type=jnp.float32).astype(
        jnp.bfloat16
    )
    query_heads = mla_query.reshape(length, -1, DH)
    heads_mla = query_heads.shape[1]
    flat_up = up_weight.reshape(up_weight.shape[0], -1)
    my_first = lax.axis_index("ctx") * length
    query_positions = my_first + jnp.arange(length, dtype=jnp.int32)
    initial = (
        jnp.full((heads_mla, length), -1e30, jnp.float32),
        jnp.zeros((heads_mla, length), jnp.float32),
        jnp.zeros((heads_mla, length, DH), jnp.float32),
    )
    piece = gathered_earlier(latent)
    piece_rows = piece.shape[0]
    block_rows = math.gcd(piece_rows, 512)
    blocks = piece.reshape(piece_rows // block_rows, block_rows, piece.shape[1])

    def one_block(state_parts, block_parts):
        block_index, latent_block = block_parts
        running_peak, running_total, running_mixed = state_parts
        paired = (
            jnp.dot(latent_block, flat_up, preferred_element_type=jnp.float32)
            .astype(jnp.bfloat16)
            .reshape(block_rows, 2, heads_mla, DH)
        )
        scores = jnp.einsum(
            "qhd,khd->hqk", query_heads, paired[:, 0], preferred_element_type=jnp.float32
        ) * DH ** (-0.5)
        key_positions = block_index * block_rows + jnp.arange(block_rows, dtype=jnp.int32)
        allowed = key_positions[None, :] <= query_positions[:, None]
        new_peak = jnp.maximum(running_peak, jnp.max(jnp.where(allowed, scores, -1e30), axis=-1))
        weights = jnp.where(allowed, jnp.exp(scores - new_peak[..., None]), 0.0)
        factor = jnp.exp(running_peak - new_peak)
        new_total = running_total * factor + jnp.sum(weights, axis=-1)
        new_mixed = running_mixed * factor[..., None] + jnp.einsum(
            "hqk,khd->hqd",
            weights.astype(jnp.bfloat16),
            paired[:, 1],
            preferred_element_type=jnp.float32,
        )
        return ((new_peak, new_total, new_mixed), None)

    def attend(state_parts):
        return lax.scan(
            one_block, state_parts, (jnp.arange(piece_rows // block_rows, dtype=jnp.int32), blocks)
        )[0]

    final_peak, final_total, final_mixed = lax.cond(
        jnp.int32(0) < my_first + length, attend, lambda state_parts: state_parts, initial
    )
    attention_out = (
        (final_mixed / final_total[..., None])
        .transpose(1, 0, 2)
        .reshape(length, heads_mla * DH)
        .astype(jnp.bfloat16)
    )
    return (stream_out, attention_out)


def solution(mesh):
    in_specs = (
        P(None, "ctx", "head"),
        P("ctx", "head"),
        P("ctx", "head"),
        P(None, None, "head"),
        P("head", None),
        P("ctx", None),
        P(),
        P(),
        P(),
        P(None, "head"),
        P(None, None, "head"),
    )
    out_specs = (P("ctx", None), P("ctx", "head"))
    return jax.shard_map(
        per_device, mesh=mesh, in_specs=in_specs, out_specs=out_specs, check_vma=False
    )
```

```python
import math

import jax
import jax.numpy as jnp
from jax import lax
from jax.sharding import PartitionSpec as P
from jax.experimental import pallas as pl
from jax.experimental.pallas import tpu as pltpu

DK = 128
CONV = 4
DH = 128


eps_norm = 1e-06
highest_precision = lax.Precision.HIGHEST


def passed_along(block, axis, distance):
    devices = range(lax.axis_size(axis))
    route = [(i - distance, i) for i in devices if i - distance in devices]
    return lax.ppermute(block, axis, route)


def summed_over_head(partial):
    total = partial
    for partner_bit in (1, 2):
        size = lax.axis_size("head")
        route = [(i, i ^ partner_bit) for i in range(size)]
        total = total + lax.ppermute(total, "head", route)
    return total


def gather_kernel(block_ref, out_ref, send_sems, recv_sems):
    me = lax.axis_index("ctx")
    count = out_ref.shape[0]
    out_ref[me] = block_ref[...]

    def outgoing(peer):
        return pltpu.make_async_remote_copy(
            src_ref=block_ref,
            dst_ref=out_ref.at[me],
            send_sem=send_sems.at[peer],
            recv_sem=recv_sems.at[me],
            device_id={"ctx": peer},
            device_id_type=pl.DeviceIdType.MESH,
        )

    def incoming(peer):
        return pltpu.make_async_remote_copy(
            src_ref=block_ref,
            dst_ref=out_ref.at[peer],
            send_sem=send_sems.at[peer],
            recv_sem=recv_sems.at[peer],
            device_id={"ctx": peer},
            device_id_type=pl.DeviceIdType.MESH,
        )

    @pl.loop(me + 1, count)
    def _(peer):
        outgoing(peer).start()

    @pl.loop(me + 1, count)
    def _(peer):
        out_ref[peer] = jnp.zeros(block_ref.shape, block_ref.dtype)

    @pl.loop(0, me)
    def _(peer):
        incoming(peer).wait_recv()

    @pl.loop(me + 1, count)
    def _(peer):
        outgoing(peer).wait_send()


def gathered_earlier(block):
    count = lax.axis_size("ctx")
    rows, width = block.shape
    stacked = pl.pallas_call(
        gather_kernel,
        out_shape=jax.ShapeDtypeStruct((count, rows, width), block.dtype),
        in_specs=[pl.BlockSpec(memory_space=pltpu.VMEM)],
        out_specs=pl.BlockSpec(memory_space=pltpu.VMEM),
        scratch_shapes=[pltpu.SemaphoreType.DMA((count,)), pltpu.SemaphoreType.DMA((count,))],
        compiler_params=pltpu.CompilerParams(has_side_effects=True),
    )(block)
    return stacked.reshape(count * rows, width)


def rounded(values):
    return lax.optimization_barrier(values.astype(jnp.bfloat16))


def unit_heads(activated):
    grouped = activated.reshape(activated.shape[0], -1, DK)
    scaled = grouped * lax.rsqrt(jnp.sum(grouped * grouped, axis=-1, keepdims=True) + eps_norm)
    return scaled.reshape(activated.shape)


def prepare(stream, norm_gain, latent_weight, latent_gain):
    widened = stream.astype(jnp.float32)
    normed = (
        widened
        * lax.rsqrt(jnp.mean(widened * widened, axis=-1, keepdims=True) + eps_norm)
        * norm_gain
    ).astype(jnp.bfloat16)
    latent_pre = jnp.dot(normed, latent_weight, preferred_element_type=jnp.float32)
    latent = (
        latent_pre
        * lax.rsqrt(jnp.mean(latent_pre * latent_pre, axis=-1, keepdims=True) + eps_norm)
        * latent_gain
    ).astype(jnp.bfloat16)
    return (normed, latent)


def span_layout(values, span_rows):
    length, channel_count = values.shape
    return values.reshape(length // span_rows, span_rows, channel_count // DK, DK).transpose(
        0, 2, 1, 3
    )


def matmul_heads(left, right):
    return jnp.einsum("hij,hjk->hik", left, right, precision=highest_precision)


def matmul_batched(left, right):
    return jnp.einsum("...ij,...jk->...ik", left, right, precision=highest_precision)


def unit_lower_inverse(system):
    size = system.shape[-1]
    rows = jnp.arange(size)[:, None]
    cols = jnp.arange(size)[None, :]
    inverse = jnp.broadcast_to(jnp.eye(size, dtype=system.dtype), system.shape)
    width = 1
    while width < size:
        below = (rows // (2 * width) == cols // (2 * width)) & (rows // width != cols // width)
        off_block = jnp.where(below, system, 0.0)
        correction = matmul_batched(matmul_batched(inverse, off_block), inverse)
        inverse = inverse - lax.optimization_barrier(correction)
        width *= 2
    return inverse


def delta_rule(kda_query, kda_key, kda_value, gate_log, beta):
    span_rows = 32
    length, channel_count = gate_log.shape
    heads = channel_count // DK
    queries = span_layout(kda_query.astype(jnp.float32), span_rows)
    keys_unit = span_layout(kda_key.astype(jnp.float32), span_rows)
    values_new = span_layout(kda_value.astype(jnp.float32), span_rows)
    cumulative = jnp.cumsum(span_layout(gate_log, span_rows), axis=2)
    rates = beta.reshape(length // span_rows, span_rows, heads).transpose(0, 2, 1)[..., None]
    growth = jnp.exp(cumulative)
    final_log = cumulative[:, :, -1:, :]
    keys_grown = keys_unit * growth
    keys_shrunk = keys_unit * jnp.exp(-cumulative)
    queries_grown = queries * growth
    keys_final = keys_unit * jnp.exp(final_log - cumulative)
    strict = jnp.tril(jnp.ones((span_rows, span_rows), jnp.float32), -1)
    inclusive = jnp.tril(jnp.ones((span_rows, span_rows), jnp.float32))
    coupling = (
        jnp.einsum("nhtc,nhsc->nhts", keys_grown, keys_shrunk, precision=highest_precision)
        * jnp.swapaxes(rates, -1, -2)
        * strict
    )
    system = coupling + jnp.eye(span_rows, dtype=jnp.float32)
    solved = matmul_batched(
        unit_lower_inverse(system), jnp.concatenate([values_new, keys_grown], axis=-1)
    )
    fresh = solved[..., :DK] * rates
    carried = solved[..., DK:] * rates
    eye_key = jnp.eye(DK, dtype=jnp.float32)
    transition = jnp.exp(final_log[:, :, 0, :])[..., :, None] * eye_key - jnp.einsum(
        "nhsk,nhsv->nhkv", keys_final, carried, precision=highest_precision
    )
    offset = jnp.einsum("nhsk,nhsv->nhkv", keys_final, fresh, precision=highest_precision)
    mixing = (
        jnp.einsum("nhtc,nhsc->nhts", queries_grown, keys_shrunk, precision=highest_precision)
        * inclusive
    )

    def compose(accumulated, span_parts):
        span_move, span_shift = span_parts
        return (
            (
                matmul_heads(span_move, accumulated[0]),
                matmul_heads(span_move, accumulated[1]) + span_shift,
            ),
            None,
        )

    identity_map = jnp.broadcast_to(eye_key, (heads, DK, DK))
    zero_map = jnp.zeros((heads, DK, DK), jnp.float32)
    (device_move, device_shift), _ = lax.scan(
        compose, (identity_map, zero_map), (transition, offset)
    )
    return (device_move, device_shift, (transition, offset, fresh, carried, queries_grown, mixing))


def emit_spans(start_state, span_data):

    def emit(recurrent_state, span_parts):
        span_move, span_shift, fresh_state_term, carried_state_term, query_term, mixing_part = (
            span_parts
        )
        state_update = fresh_state_term - jnp.einsum(
            "orm,omj->orj", carried_state_term, recurrent_state, precision=highest_precision
        )
        produced_output = jnp.einsum(
            "fmb,fbi->fmi", query_term, recurrent_state, precision=highest_precision
        ) + jnp.einsum("hts,hsv->htv", mixing_part, state_update, precision=highest_precision)
        return (matmul_heads(span_move, recurrent_state) + span_shift, produced_output)

    _, outputs = lax.scan(emit, start_state, span_data)
    block_count, heads, span_rows, _ = outputs.shape
    return (
        outputs.transpose(0, 2, 1, 3)
        .reshape(block_count * span_rows, heads * DK)
        .astype(jnp.bfloat16)
    )


def per_device(
    kda_inputs,
    gate_log,
    beta,
    conv_weight,
    kda_out_weight,
    residual,
    norm_gain,
    latent_weight,
    latent_gain,
    query_weight,
    up_weight,
):
    length = residual.shape[0]
    edge_rows = kda_inputs[:, length - (CONV - 1) :, :]
    earlier_rows = passed_along(edge_rows, "ctx", 1)
    extended = jnp.concatenate([earlier_rows, kda_inputs], axis=1).astype(jnp.float32)
    running = jnp.zeros(kda_inputs.shape, jnp.float32)
    for tap_index in range(CONV):
        running = (
            running
            + conv_weight[:, tap_index, None, :] * extended[:, tap_index : tap_index + length, :]
        )
    activated = jax.nn.silu(running)
    kda_query = rounded(unit_heads(activated[0]) * DK ** (-0.5))
    kda_key = rounded(unit_heads(activated[1]))
    kda_value = rounded(activated[2])
    device_move, device_shift, span_data = delta_rule(kda_query, kda_key, kda_value, gate_log, beta)
    heads = device_move.shape[0]

    ctx_size = lax.axis_size("ctx")
    move, shift = device_move, device_shift
    distance = 1
    while distance < ctx_size:
        shift_in = passed_along(shift, "ctx", distance)
        if 2 * distance < ctx_size:
            move_in = passed_along(move, "ctx", distance)
            shift = matmul_heads(move, shift_in) + shift
            move = matmul_heads(move, move_in)
        else:
            shift = matmul_heads(move, shift_in) + shift
        distance *= 2
    start_state = passed_along(shift, "ctx", 1)
    kda_core = emit_spans(start_state, span_data)
    partial_proj = jnp.dot(kda_core, kda_out_weight, preferred_element_type=jnp.float32)
    summed = summed_over_head(partial_proj)
    stream_out = (residual.astype(jnp.float32) + summed).astype(jnp.bfloat16)
    normed, latent = prepare(stream_out, norm_gain, latent_weight, latent_gain)
    mla_query = jnp.dot(normed, query_weight, preferred_element_type=jnp.float32).astype(
        jnp.bfloat16
    )
    query_heads = mla_query.reshape(length, -1, DH)
    heads_mla = query_heads.shape[1]
    flat_up = up_weight.reshape(up_weight.shape[0], -1)
    my_first = lax.axis_index("ctx") * length
    query_positions = my_first + jnp.arange(length, dtype=jnp.int32)
    piece = gathered_earlier(latent)
    piece_rows = piece.shape[0]
    paired = (
        jnp.dot(piece, flat_up, preferred_element_type=jnp.float32)
        .astype(jnp.bfloat16)
        .reshape(piece_rows, 2, heads_mla, DH)
    )
    scores = jnp.einsum(
        "qhd,khd->hqk", query_heads, paired[:, 0], preferred_element_type=jnp.float32
    ) * DH ** (-0.5)
    key_positions = jnp.arange(piece_rows, dtype=jnp.int32)
    allowed = key_positions[None, :] <= query_positions[:, None]
    final_peak = jnp.max(jnp.where(allowed, scores, -1e30), axis=-1)
    weights = jnp.where(allowed, jnp.exp(scores - final_peak[..., None]), 0.0)
    final_total = jnp.sum(weights, axis=-1)
    final_mixed = jnp.einsum(
        "hqk,khd->hqd",
        weights.astype(jnp.bfloat16),
        paired[:, 1],
        preferred_element_type=jnp.float32,
    )
    attention_out = (
        (final_mixed / final_total[..., None])
        .transpose(1, 0, 2)
        .reshape(length, heads_mla * DH)
        .astype(jnp.bfloat16)
    )
    return (stream_out, attention_out)


def solution(mesh):
    in_specs = (
        P(None, "ctx", "head"),
        P("ctx", "head"),
        P("ctx", "head"),
        P(None, None, "head"),
        P("head", None),
        P("ctx", None),
        P(),
        P(),
        P(),
        P(None, "head"),
        P(None, None, "head"),
    )
    out_specs = (P("ctx", None), P("ctx", "head"))
    return jax.shard_map(
        per_device, mesh=mesh, in_specs=in_specs, out_specs=out_specs, check_vma=False
    )
```

```python
import math

import jax
import jax.numpy as jnp
from jax import lax
from jax.sharding import PartitionSpec as P
from jax.experimental import pallas as pl
from jax.experimental.pallas import tpu as pltpu

DK = 128
CONV = 4
DH = 128


eps_norm = 1e-06
highest_precision = lax.Precision.HIGHEST


def passed_along(block, axis, distance):
    devices = range(lax.axis_size(axis))
    route = [(i - distance, i) for i in devices if i - distance in devices]
    return lax.ppermute(block, axis, route)


def summed_over_head(partial):
    total = partial
    for partner_bit in (1, 2):
        size = lax.axis_size("head")
        route = [(i, i ^ partner_bit) for i in range(size)]
        total = total + lax.ppermute(total, "head", route)
    return total


def gather_kernel(block_ref, out_ref, send_sems, recv_sems):
    me = lax.axis_index("ctx")
    count = out_ref.shape[0]
    out_ref[me] = block_ref[...]

    def outgoing(peer):
        return pltpu.make_async_remote_copy(
            src_ref=block_ref,
            dst_ref=out_ref.at[me],
            send_sem=send_sems.at[peer],
            recv_sem=recv_sems.at[me],
            device_id={"ctx": peer},
            device_id_type=pl.DeviceIdType.MESH,
        )

    def incoming(peer):
        return pltpu.make_async_remote_copy(
            src_ref=block_ref,
            dst_ref=out_ref.at[peer],
            send_sem=send_sems.at[peer],
            recv_sem=recv_sems.at[peer],
            device_id={"ctx": peer},
            device_id_type=pl.DeviceIdType.MESH,
        )

    @pl.loop(me + 1, count)
    def _(peer):
        outgoing(peer).start()

    @pl.loop(me + 1, count)
    def _(peer):
        out_ref[peer] = jnp.zeros(block_ref.shape, block_ref.dtype)

    @pl.loop(0, me)
    def _(peer):
        incoming(peer).wait_recv()

    @pl.loop(me + 1, count)
    def _(peer):
        outgoing(peer).wait_send()


def gathered_earlier(block):
    count = lax.axis_size("ctx")
    rows, width = block.shape
    stacked = pl.pallas_call(
        gather_kernel,
        out_shape=jax.ShapeDtypeStruct((count, rows, width), block.dtype),
        in_specs=[pl.BlockSpec(memory_space=pltpu.VMEM)],
        out_specs=pl.BlockSpec(memory_space=pltpu.VMEM),
        scratch_shapes=[pltpu.SemaphoreType.DMA((count,)), pltpu.SemaphoreType.DMA((count,))],
        compiler_params=pltpu.CompilerParams(has_side_effects=True),
    )(block)
    return stacked.reshape(count * rows, width)


def rounded(values):
    return lax.optimization_barrier(values.astype(jnp.bfloat16))


def unit_heads(activated):
    grouped = activated.reshape(activated.shape[0], -1, DK)
    scaled = grouped * lax.rsqrt(jnp.sum(grouped * grouped, axis=-1, keepdims=True) + eps_norm)
    return scaled.reshape(activated.shape)


def prepare(stream, norm_gain, latent_weight, latent_gain):
    widened = stream.astype(jnp.float32)
    normed = (
        widened
        * lax.rsqrt(jnp.mean(widened * widened, axis=-1, keepdims=True) + eps_norm)
        * norm_gain
    ).astype(jnp.bfloat16)
    latent_pre = jnp.dot(normed, latent_weight, preferred_element_type=jnp.float32)
    latent = (
        latent_pre
        * lax.rsqrt(jnp.mean(latent_pre * latent_pre, axis=-1, keepdims=True) + eps_norm)
        * latent_gain
    ).astype(jnp.bfloat16)
    return (normed, latent)


def span_layout(values, span_rows):
    length, channel_count = values.shape
    return values.reshape(length // span_rows, span_rows, channel_count // DK, DK).transpose(
        0, 2, 1, 3
    )


def matmul_heads(left, right):
    return jnp.einsum("hij,hjk->hik", left, right, precision=highest_precision)


def matmul_batched(left, right):
    return jnp.einsum("...ij,...jk->...ik", left, right, precision=highest_precision)


def unit_lower_inverse(system):
    size = system.shape[-1]
    rows = jnp.arange(size)[:, None]
    cols = jnp.arange(size)[None, :]
    inverse = jnp.broadcast_to(jnp.eye(size, dtype=system.dtype), system.shape)
    width = 1
    while width < size:
        below = (rows // (2 * width) == cols // (2 * width)) & (rows // width != cols // width)
        off_block = jnp.where(below, system, 0.0)
        correction = matmul_batched(matmul_batched(inverse, off_block), inverse)
        inverse = inverse - lax.optimization_barrier(correction)
        width *= 2
    return inverse


def delta_rule(kda_query, kda_key, kda_value, gate_log, beta):
    span_rows = 32
    length, channel_count = gate_log.shape
    heads = channel_count // DK
    queries = span_layout(kda_query.astype(jnp.float32), span_rows)
    keys_unit = span_layout(kda_key.astype(jnp.float32), span_rows)
    values_new = span_layout(kda_value.astype(jnp.float32), span_rows)
    cumulative = jnp.cumsum(span_layout(gate_log, span_rows), axis=2)
    rates = beta.reshape(length // span_rows, span_rows, heads).transpose(0, 2, 1)[..., None]
    growth = jnp.exp(cumulative)
    final_log = cumulative[:, :, -1:, :]
    keys_grown = keys_unit * growth
    keys_shrunk = keys_unit * jnp.exp(-cumulative)
    queries_grown = queries * growth
    keys_final = keys_unit * jnp.exp(final_log - cumulative)
    strict = jnp.tril(jnp.ones((span_rows, span_rows), jnp.float32), -1)
    inclusive = jnp.tril(jnp.ones((span_rows, span_rows), jnp.float32))
    coupling = (
        jnp.einsum("nhtc,nhsc->nhts", keys_grown, keys_shrunk, precision=highest_precision)
        * jnp.swapaxes(rates, -1, -2)
        * strict
    )
    system = coupling + jnp.eye(span_rows, dtype=jnp.float32)
    solved = matmul_batched(
        unit_lower_inverse(system), jnp.concatenate([values_new, keys_grown], axis=-1)
    )
    fresh = solved[..., :DK] * rates
    carried = solved[..., DK:] * rates
    eye_key = jnp.eye(DK, dtype=jnp.float32)
    transition = jnp.exp(final_log[:, :, 0, :])[..., :, None] * eye_key - jnp.einsum(
        "nhsk,nhsv->nhkv", keys_final, carried, precision=highest_precision
    )
    offset = jnp.einsum("nhsk,nhsv->nhkv", keys_final, fresh, precision=highest_precision)
    mixing = (
        jnp.einsum("nhtc,nhsc->nhts", queries_grown, keys_shrunk, precision=highest_precision)
        * inclusive
    )

    def compose(accumulated, span_parts):
        span_move, span_shift = span_parts
        return (
            (
                matmul_heads(span_move, accumulated[0]),
                matmul_heads(span_move, accumulated[1]) + span_shift,
            ),
            None,
        )

    identity_map = jnp.broadcast_to(eye_key, (heads, DK, DK))
    zero_map = jnp.zeros((heads, DK, DK), jnp.float32)
    (device_move, device_shift), _ = lax.scan(
        compose, (identity_map, zero_map), (transition, offset)
    )
    return (device_move, device_shift, (transition, offset, fresh, carried, queries_grown, mixing))


def emit_spans(span_data):
    span_move = span_data[0]
    heads = span_move.shape[1]
    zero_state = jnp.zeros((heads, DK, DK), jnp.float32)
    identity_map = jnp.broadcast_to(jnp.eye(DK, dtype=jnp.float32), (heads, DK, DK))

    def emit(carried_parts, span_parts):
        recurrent_state, accumulated_move = carried_parts
        span_move, span_shift, fresh_state_term, carried_state_term, query_term, mixing_part = (
            span_parts
        )
        state_update = fresh_state_term - jnp.einsum(
            "orm,omj->orj", carried_state_term, recurrent_state, precision=highest_precision
        )
        produced_output = jnp.einsum(
            "fmb,fbi->fmi", query_term, recurrent_state, precision=highest_precision
        ) + jnp.einsum("hts,hsv->htv", mixing_part, state_update, precision=highest_precision)
        start_weight = query_term - jnp.einsum(
            "hts,hsv->htv", mixing_part, carried_state_term, precision=highest_precision
        )
        start_query = matmul_heads(start_weight, accumulated_move)
        next_parts = (
            matmul_heads(span_move, recurrent_state) + span_shift,
            matmul_heads(span_move, accumulated_move),
        )
        return (next_parts, (produced_output, start_query))

    _, (outputs, start_queries) = lax.scan(emit, (zero_state, identity_map), span_data)
    block_count, heads, span_rows, _ = outputs.shape

    def token_major(values):
        return values.transpose(1, 0, 2, 3).reshape(heads, block_count * span_rows, DK)

    return (token_major(outputs), token_major(start_queries))


def finish_spans(start_state, local_outputs, start_queries):
    outputs = local_outputs + matmul_heads(start_queries, start_state)
    heads, length, _ = outputs.shape
    return outputs.transpose(1, 0, 2).reshape(length, heads * DK).astype(jnp.bfloat16)


def per_device(
    kda_inputs,
    gate_log,
    beta,
    conv_weight,
    kda_out_weight,
    residual,
    norm_gain,
    latent_weight,
    latent_gain,
    query_weight,
    up_weight,
):
    length = residual.shape[0]
    edge_rows = kda_inputs[:, length - (CONV - 1) :, :]
    earlier_rows = passed_along(edge_rows, "ctx", 1)
    extended = jnp.concatenate([earlier_rows, kda_inputs], axis=1).astype(jnp.float32)
    running = jnp.zeros(kda_inputs.shape, jnp.float32)
    for tap_index in range(CONV):
        running = (
            running
            + conv_weight[:, tap_index, None, :] * extended[:, tap_index : tap_index + length, :]
        )
    activated = jax.nn.silu(running)
    kda_query = rounded(unit_heads(activated[0]) * DK ** (-0.5))
    kda_key = rounded(unit_heads(activated[1]))
    kda_value = rounded(activated[2])
    device_move, device_shift, span_data = delta_rule(kda_query, kda_key, kda_value, gate_log, beta)
    heads = device_move.shape[0]
    local_outputs, start_queries = emit_spans(span_data)

    ctx_size = lax.axis_size("ctx")
    move, shift = device_move, device_shift
    distance = 1
    while distance < ctx_size:
        shift_in = passed_along(shift, "ctx", distance)
        if 2 * distance < ctx_size:
            move_in = passed_along(move, "ctx", distance)
            shift = matmul_heads(move, shift_in) + shift
            move = matmul_heads(move, move_in)
        else:
            shift = matmul_heads(move, shift_in) + shift
        distance *= 2
    start_state = passed_along(shift, "ctx", 1)
    kda_core = finish_spans(start_state, local_outputs, start_queries)
    partial_proj = jnp.dot(kda_core, kda_out_weight, preferred_element_type=jnp.float32)
    summed = summed_over_head(partial_proj)
    stream_out = (residual.astype(jnp.float32) + summed).astype(jnp.bfloat16)
    normed, latent = prepare(stream_out, norm_gain, latent_weight, latent_gain)
    mla_query = jnp.dot(normed, query_weight, preferred_element_type=jnp.float32).astype(
        jnp.bfloat16
    )
    query_heads = mla_query.reshape(length, -1, DH)
    heads_mla = query_heads.shape[1]
    flat_up = up_weight.reshape(up_weight.shape[0], -1)
    my_first = lax.axis_index("ctx") * length
    query_positions = my_first + jnp.arange(length, dtype=jnp.int32)
    piece = gathered_earlier(latent)
    piece_rows = piece.shape[0]
    paired = (
        jnp.dot(piece, flat_up, preferred_element_type=jnp.float32)
        .astype(jnp.bfloat16)
        .reshape(piece_rows, 2, heads_mla, DH)
    )
    scores = jnp.einsum(
        "qhd,khd->hqk", query_heads, paired[:, 0], preferred_element_type=jnp.float32
    ) * DH ** (-0.5)
    key_positions = jnp.arange(piece_rows, dtype=jnp.int32)
    allowed = key_positions[None, :] <= query_positions[:, None]
    final_peak = jnp.max(jnp.where(allowed, scores, -1e30), axis=-1)
    weights = jnp.where(allowed, jnp.exp(scores - final_peak[..., None]), 0.0)
    final_total = jnp.sum(weights, axis=-1)
    final_mixed = jnp.einsum(
        "hqk,khd->hqd",
        weights.astype(jnp.bfloat16),
        paired[:, 1],
        preferred_element_type=jnp.float32,
    )
    attention_out = (
        (final_mixed / final_total[..., None])
        .transpose(1, 0, 2)
        .reshape(length, heads_mla * DH)
        .astype(jnp.bfloat16)
    )
    return (stream_out, attention_out)


def solution(mesh):
    in_specs = (
        P(None, "ctx", "head"),
        P("ctx", "head"),
        P("ctx", "head"),
        P(None, None, "head"),
        P("head", None),
        P("ctx", None),
        P(),
        P(),
        P(),
        P(None, "head"),
        P(None, None, "head"),
    )
    out_specs = (P("ctx", None), P("ctx", "head"))
    return jax.shard_map(
        per_device, mesh=mesh, in_specs=in_specs, out_specs=out_specs, check_vma=False
    )
```

```python
import math

import jax
import jax.numpy as jnp
from jax import lax
from jax.sharding import PartitionSpec as P
from jax.experimental import pallas as pl
from jax.experimental.pallas import tpu as pltpu

DK = 128
CONV = 4
DH = 128


eps_norm = 1e-06
highest_precision = lax.Precision.HIGHEST


def passed_along(block, axis, distance):
    devices = range(lax.axis_size(axis))
    route = [(i - distance, i) for i in devices if i - distance in devices]
    return lax.ppermute(block, axis, route)


def summed_over_head(partial):
    total = partial
    for partner_bit in (1, 2):
        size = lax.axis_size("head")
        route = [(i, i ^ partner_bit) for i in range(size)]
        total = total + lax.ppermute(total, "head", route)
    return total


def gather_kernel(block_ref, out_ref, send_sems, recv_sems, forward_sems):
    me = lax.axis_index("ctx")
    head = lax.axis_index("head")
    core = head % 2
    sibling = head + 1 - 2 * core
    count = out_ref.shape[0]
    out_ref[me] = block_ref[...]

    def outgoing(peer):
        return pltpu.make_async_remote_copy(
            src_ref=block_ref,
            dst_ref=out_ref.at[me],
            send_sem=send_sems.at[peer],
            recv_sem=recv_sems.at[me],
            device_id={"ctx": peer, "head": head},
            device_id_type=pl.DeviceIdType.MESH,
        )

    def forwarded(origin):
        return pltpu.make_async_remote_copy(
            src_ref=out_ref.at[origin],
            dst_ref=out_ref.at[origin],
            send_sem=forward_sems.at[origin],
            recv_sem=recv_sems.at[origin],
            device_id={"ctx": me, "head": sibling},
            device_id_type=pl.DeviceIdType.MESH,
        )

    @pl.loop(me + 1, count)
    def _(peer):
        @pl.when((peer + me) % 2 == core)
        def _():
            outgoing(peer).start()

    @pl.loop(me + 1, count)
    def _(peer):
        out_ref[peer] = jnp.zeros(block_ref.shape, block_ref.dtype)

    @pl.loop(0, me)
    def _(origin):
        @pl.when((origin + me) % 2 == core)
        def _():
            forwarded(origin).wait_recv()
            forwarded(origin).start()

    @pl.loop(0, me)
    def _(origin):
        @pl.when((origin + me) % 2 != core)
        def _():
            forwarded(origin).wait_recv()

    @pl.loop(me + 1, count)
    def _(peer):
        @pl.when((peer + me) % 2 == core)
        def _():
            outgoing(peer).wait_send()

    @pl.loop(0, me)
    def _(origin):
        @pl.when((origin + me) % 2 == core)
        def _():
            forwarded(origin).wait_send()


def gathered_earlier(block):
    count = lax.axis_size("ctx")
    rows, width = block.shape
    stacked = pl.pallas_call(
        gather_kernel,
        out_shape=jax.ShapeDtypeStruct((count, rows, width), block.dtype),
        in_specs=[pl.BlockSpec(memory_space=pltpu.VMEM)],
        out_specs=pl.BlockSpec(memory_space=pltpu.VMEM),
        scratch_shapes=[pltpu.SemaphoreType.DMA((count,))] * 3,
        compiler_params=pltpu.CompilerParams(has_side_effects=True),
    )(block)
    return stacked.reshape(count * rows, width)


def rounded(values):
    return lax.optimization_barrier(values.astype(jnp.bfloat16))


def unit_heads(activated):
    grouped = activated.reshape(activated.shape[0], -1, DK)
    scaled = grouped * lax.rsqrt(jnp.sum(grouped * grouped, axis=-1, keepdims=True) + eps_norm)
    return scaled.reshape(activated.shape)


def prepare(stream, norm_gain, latent_weight, latent_gain):
    widened = stream.astype(jnp.float32)
    normed = (
        widened
        * lax.rsqrt(jnp.mean(widened * widened, axis=-1, keepdims=True) + eps_norm)
        * norm_gain
    ).astype(jnp.bfloat16)
    latent_pre = jnp.dot(normed, latent_weight, preferred_element_type=jnp.float32)
    latent = (
        latent_pre
        * lax.rsqrt(jnp.mean(latent_pre * latent_pre, axis=-1, keepdims=True) + eps_norm)
        * latent_gain
    ).astype(jnp.bfloat16)
    return (normed, latent)


def span_layout(values, span_rows):
    length, channel_count = values.shape
    return values.reshape(length // span_rows, span_rows, channel_count // DK, DK).transpose(
        0, 2, 1, 3
    )


def matmul_heads(left, right):
    return jnp.einsum("hij,hjk->hik", left, right, precision=highest_precision)


def matmul_batched(left, right):
    return jnp.einsum("...ij,...jk->...ik", left, right, precision=highest_precision)


def unit_lower_inverse(system):
    size = system.shape[-1]
    rows = jnp.arange(size)[:, None]
    cols = jnp.arange(size)[None, :]
    inverse = jnp.broadcast_to(jnp.eye(size, dtype=system.dtype), system.shape)
    width = 1
    while width < size:
        below = (rows // (2 * width) == cols // (2 * width)) & (rows // width != cols // width)
        off_block = jnp.where(below, system, 0.0)
        correction = matmul_batched(matmul_batched(inverse, off_block), inverse)
        inverse = inverse - lax.optimization_barrier(correction)
        width *= 2
    return inverse


def delta_rule(kda_query, kda_key, kda_value, gate_log, beta):
    span_rows = 32
    length, channel_count = gate_log.shape
    heads = channel_count // DK
    queries = span_layout(kda_query.astype(jnp.float32), span_rows)
    keys_unit = span_layout(kda_key.astype(jnp.float32), span_rows)
    values_new = span_layout(kda_value.astype(jnp.float32), span_rows)
    cumulative = jnp.cumsum(span_layout(gate_log, span_rows), axis=2)
    rates = beta.reshape(length // span_rows, span_rows, heads).transpose(0, 2, 1)[..., None]
    growth = jnp.exp(cumulative)
    final_log = cumulative[:, :, -1:, :]
    keys_grown = keys_unit * growth
    keys_shrunk = keys_unit * jnp.exp(-cumulative)
    queries_grown = queries * growth
    keys_final = keys_unit * jnp.exp(final_log - cumulative)
    strict = jnp.tril(jnp.ones((span_rows, span_rows), jnp.float32), -1)
    inclusive = jnp.tril(jnp.ones((span_rows, span_rows), jnp.float32))
    coupling = (
        jnp.einsum("nhtc,nhsc->nhts", keys_grown, keys_shrunk, precision=highest_precision)
        * jnp.swapaxes(rates, -1, -2)
        * strict
    )
    system = coupling + jnp.eye(span_rows, dtype=jnp.float32)
    solved = matmul_batched(
        unit_lower_inverse(system), jnp.concatenate([values_new, keys_grown], axis=-1)
    )
    fresh = solved[..., :DK] * rates
    carried = solved[..., DK:] * rates
    eye_key = jnp.eye(DK, dtype=jnp.float32)
    transition = jnp.exp(final_log[:, :, 0, :])[..., :, None] * eye_key - jnp.einsum(
        "nhsk,nhsv->nhkv", keys_final, carried, precision=highest_precision
    )
    offset = jnp.einsum("nhsk,nhsv->nhkv", keys_final, fresh, precision=highest_precision)
    mixing = (
        jnp.einsum("nhtc,nhsc->nhts", queries_grown, keys_shrunk, precision=highest_precision)
        * inclusive
    )

    def compose(accumulated, span_parts):
        span_move, span_shift = span_parts
        return (
            (
                matmul_heads(span_move, accumulated[0]),
                matmul_heads(span_move, accumulated[1]) + span_shift,
            ),
            None,
        )

    identity_map = jnp.broadcast_to(eye_key, (heads, DK, DK))
    zero_map = jnp.zeros((heads, DK, DK), jnp.float32)
    (device_move, device_shift), _ = lax.scan(
        compose, (identity_map, zero_map), (transition, offset)
    )
    return (device_move, device_shift, (transition, offset, fresh, carried, queries_grown, mixing))


def emit_spans(span_data):
    span_move = span_data[0]
    heads = span_move.shape[1]
    zero_state = jnp.zeros((heads, DK, DK), jnp.float32)
    identity_map = jnp.broadcast_to(jnp.eye(DK, dtype=jnp.float32), (heads, DK, DK))

    def emit(carried_parts, span_parts):
        recurrent_state, accumulated_move = carried_parts
        span_move, span_shift, fresh_state_term, carried_state_term, query_term, mixing_part = (
            span_parts
        )
        state_update = fresh_state_term - jnp.einsum(
            "orm,omj->orj", carried_state_term, recurrent_state, precision=highest_precision
        )
        produced_output = jnp.einsum(
            "fmb,fbi->fmi", query_term, recurrent_state, precision=highest_precision
        ) + jnp.einsum("hts,hsv->htv", mixing_part, state_update, precision=highest_precision)
        start_weight = query_term - jnp.einsum(
            "hts,hsv->htv", mixing_part, carried_state_term, precision=highest_precision
        )
        start_query = matmul_heads(start_weight, accumulated_move)
        next_parts = (
            matmul_heads(span_move, recurrent_state) + span_shift,
            matmul_heads(span_move, accumulated_move),
        )
        return (next_parts, (produced_output, start_query))

    _, (outputs, start_queries) = lax.scan(emit, (zero_state, identity_map), span_data)
    block_count, heads, span_rows, _ = outputs.shape

    def token_major(values):
        return values.transpose(1, 0, 2, 3).reshape(heads, block_count * span_rows, DK)

    return (token_major(outputs), token_major(start_queries))


def finish_spans(start_state, local_outputs, start_queries):
    outputs = local_outputs + matmul_heads(start_queries, start_state)
    heads, length, _ = outputs.shape
    return outputs.transpose(1, 0, 2).reshape(length, heads * DK).astype(jnp.bfloat16)


def per_device(
    kda_inputs,
    gate_log,
    beta,
    conv_weight,
    kda_out_weight,
    residual,
    norm_gain,
    latent_weight,
    latent_gain,
    query_weight,
    up_weight,
):
    length = residual.shape[0]
    edge_rows = kda_inputs[:, length - (CONV - 1) :, :]
    earlier_rows = passed_along(edge_rows, "ctx", 1)
    extended = jnp.concatenate([earlier_rows, kda_inputs], axis=1).astype(jnp.float32)
    running = jnp.zeros(kda_inputs.shape, jnp.float32)
    for tap_index in range(CONV):
        running = (
            running
            + conv_weight[:, tap_index, None, :] * extended[:, tap_index : tap_index + length, :]
        )
    activated = jax.nn.silu(running)
    kda_query = rounded(unit_heads(activated[0]) * DK ** (-0.5))
    kda_key = rounded(unit_heads(activated[1]))
    kda_value = rounded(activated[2])
    device_move, device_shift, span_data = delta_rule(kda_query, kda_key, kda_value, gate_log, beta)
    heads = device_move.shape[0]
    local_outputs, start_queries = emit_spans(span_data)

    ctx_size = lax.axis_size("ctx")
    move, shift = device_move, device_shift
    distance = 1
    while distance < ctx_size:
        shift_in = passed_along(shift, "ctx", distance)
        if 2 * distance < ctx_size:
            move_in = passed_along(move, "ctx", distance)
            shift = matmul_heads(move, shift_in) + shift
            move = matmul_heads(move, move_in)
        else:
            shift = matmul_heads(move, shift_in) + shift
        distance *= 2
    start_state = passed_along(shift, "ctx", 1)
    kda_core = finish_spans(start_state, local_outputs, start_queries)
    partial_proj = jnp.dot(kda_core, kda_out_weight, preferred_element_type=jnp.float32)
    summed = summed_over_head(partial_proj)
    stream_out = (residual.astype(jnp.float32) + summed).astype(jnp.bfloat16)
    normed, latent = prepare(stream_out, norm_gain, latent_weight, latent_gain)
    mla_query = jnp.dot(normed, query_weight, preferred_element_type=jnp.float32).astype(
        jnp.bfloat16
    )
    query_heads = mla_query.reshape(length, -1, DH)
    heads_mla = query_heads.shape[1]
    flat_up = up_weight.reshape(up_weight.shape[0], -1)
    my_first = lax.axis_index("ctx") * length
    query_positions = my_first + jnp.arange(length, dtype=jnp.int32)
    piece = gathered_earlier(latent)
    piece_rows = piece.shape[0]
    paired = (
        jnp.dot(piece, flat_up, preferred_element_type=jnp.float32)
        .astype(jnp.bfloat16)
        .reshape(piece_rows, 2, heads_mla, DH)
    )
    scores = jnp.einsum(
        "qhd,khd->hqk", query_heads, paired[:, 0], preferred_element_type=jnp.float32
    ) * DH ** (-0.5)
    key_positions = jnp.arange(piece_rows, dtype=jnp.int32)
    allowed = key_positions[None, :] <= query_positions[:, None]
    final_peak = jnp.max(jnp.where(allowed, scores, -1e30), axis=-1)
    weights = jnp.where(allowed, jnp.exp(scores - final_peak[..., None]), 0.0)
    final_total = jnp.sum(weights, axis=-1)
    final_mixed = jnp.einsum(
        "hqk,khd->hqd",
        weights.astype(jnp.bfloat16),
        paired[:, 1],
        preferred_element_type=jnp.float32,
    )
    attention_out = (
        (final_mixed / final_total[..., None])
        .transpose(1, 0, 2)
        .reshape(length, heads_mla * DH)
        .astype(jnp.bfloat16)
    )
    return (stream_out, attention_out)


def solution(mesh):
    in_specs = (
        P(None, "ctx", "head"),
        P("ctx", "head"),
        P("ctx", "head"),
        P(None, None, "head"),
        P("head", None),
        P("ctx", None),
        P(),
        P(),
        P(),
        P(None, "head"),
        P(None, None, "head"),
    )
    out_specs = (P("ctx", None), P("ctx", "head"))
    return jax.shard_map(
        per_device, mesh=mesh, in_specs=in_specs, out_specs=out_specs, check_vma=False
    )
```

```python
import math

import jax
import jax.numpy as jnp
from jax import lax
from jax.sharding import PartitionSpec as P
from jax.experimental import pallas as pl
from jax.experimental.pallas import tpu as pltpu

DK = 128
CONV = 4
DH = 128


eps_norm = 1e-06
highest_precision = lax.Precision.HIGHEST


def passed_along(block, axis, distance):
    devices = range(lax.axis_size(axis))
    route = [(i - distance, i) for i in devices if i - distance in devices]
    return lax.ppermute(block, axis, route)


def summed_over_head(partial):
    total = partial
    for partner_bit in (1, 2):
        size = lax.axis_size("head")
        route = [(i, i ^ partner_bit) for i in range(size)]
        total = total + lax.ppermute(total, "head", route)
    return total


def gather_kernel(block_ref, out_ref, send_sems, recv_sems, forward_sems):
    me = lax.axis_index("ctx")
    head = lax.axis_index("head")
    core = head % 2
    sibling = head + 1 - 2 * core
    count = out_ref.shape[0]
    out_ref[me] = block_ref[...]

    def outgoing(peer):
        return pltpu.make_async_remote_copy(
            src_ref=block_ref,
            dst_ref=out_ref.at[me],
            send_sem=send_sems.at[peer],
            recv_sem=recv_sems.at[me],
            device_id={"ctx": peer, "head": head},
            device_id_type=pl.DeviceIdType.MESH,
        )

    def forwarded(origin):
        return pltpu.make_async_remote_copy(
            src_ref=out_ref.at[origin],
            dst_ref=out_ref.at[origin],
            send_sem=forward_sems.at[origin],
            recv_sem=recv_sems.at[origin],
            device_id={"ctx": me, "head": sibling},
            device_id_type=pl.DeviceIdType.MESH,
        )

    @pl.loop(me + 1, count)
    def _(peer):
        @pl.when((peer + me) % 2 == core)
        def _():
            outgoing(peer).start()

    @pl.loop(me + 1, count)
    def _(peer):
        out_ref[peer] = jnp.zeros(block_ref.shape, block_ref.dtype)

    @pl.loop(0, me)
    def _(origin):
        @pl.when((origin + me) % 2 == core)
        def _():
            forwarded(origin).wait_recv()
            forwarded(origin).start()

    @pl.loop(0, me)
    def _(origin):
        @pl.when((origin + me) % 2 != core)
        def _():
            forwarded(origin).wait_recv()

    @pl.loop(me + 1, count)
    def _(peer):
        @pl.when((peer + me) % 2 == core)
        def _():
            outgoing(peer).wait_send()

    @pl.loop(0, me)
    def _(origin):
        @pl.when((origin + me) % 2 == core)
        def _():
            forwarded(origin).wait_send()


def gathered_earlier(block):
    count = lax.axis_size("ctx")
    rows, width = block.shape
    stacked = pl.pallas_call(
        gather_kernel,
        out_shape=jax.ShapeDtypeStruct((count, rows, width), block.dtype),
        in_specs=[pl.BlockSpec(memory_space=pltpu.VMEM)],
        out_specs=pl.BlockSpec(memory_space=pltpu.VMEM),
        scratch_shapes=[pltpu.SemaphoreType.DMA((count,))] * 3,
        compiler_params=pltpu.CompilerParams(has_side_effects=True),
    )(block)
    return stacked.reshape(count * rows, width)


def rounded(values):
    return lax.optimization_barrier(values.astype(jnp.bfloat16))


def unit_heads(activated):
    grouped = activated.reshape(activated.shape[0], -1, DK)
    scaled = grouped * lax.rsqrt(jnp.sum(grouped * grouped, axis=-1, keepdims=True) + eps_norm)
    return scaled.reshape(activated.shape)


def prepare(stream, norm_gain, latent_weight, latent_gain):
    widened = stream.astype(jnp.float32)
    normed = (
        widened
        * lax.rsqrt(jnp.mean(widened * widened, axis=-1, keepdims=True) + eps_norm)
        * norm_gain
    ).astype(jnp.bfloat16)
    latent_pre = jnp.dot(normed, latent_weight, preferred_element_type=jnp.float32)
    latent = (
        latent_pre
        * lax.rsqrt(jnp.mean(latent_pre * latent_pre, axis=-1, keepdims=True) + eps_norm)
        * latent_gain
    ).astype(jnp.bfloat16)
    return (normed, latent)


def span_layout(values, span_rows):
    length, channel_count = values.shape
    return values.reshape(length // span_rows, span_rows, channel_count // DK, DK).transpose(
        0, 2, 1, 3
    )


def matmul_heads(left, right):
    return jnp.einsum("hij,hjk->hik", left, right, precision=highest_precision)


def matmul_batched(left, right):
    return jnp.einsum("...ij,...jk->...ik", left, right, precision=highest_precision)


def unit_lower_inverse(system):
    size = system.shape[-1]
    rows = jnp.arange(size)[:, None]
    cols = jnp.arange(size)[None, :]
    inverse = jnp.broadcast_to(jnp.eye(size, dtype=system.dtype), system.shape)
    width = 1
    while width < size:
        below = (rows // (2 * width) == cols // (2 * width)) & (rows // width != cols // width)
        off_block = jnp.where(below, system, 0.0)
        correction = matmul_batched(matmul_batched(inverse, off_block), inverse)
        inverse = inverse - lax.optimization_barrier(correction)
        width *= 2
    return inverse


def delta_rule(kda_query, kda_key, kda_value, gate_log, beta):
    span_rows = 32
    length, channel_count = gate_log.shape
    heads = channel_count // DK
    queries = span_layout(kda_query.astype(jnp.float32), span_rows)
    keys_unit = span_layout(kda_key.astype(jnp.float32), span_rows)
    values_new = span_layout(kda_value.astype(jnp.float32), span_rows)
    cumulative = jnp.cumsum(span_layout(gate_log, span_rows), axis=2)
    rates = beta.reshape(length // span_rows, span_rows, heads).transpose(0, 2, 1)[..., None]
    growth = jnp.exp(cumulative)
    final_log = cumulative[:, :, -1:, :]
    keys_grown = keys_unit * growth
    keys_shrunk = keys_unit * jnp.exp(-cumulative)
    queries_grown = queries * growth
    keys_final = keys_unit * jnp.exp(final_log - cumulative)
    strict = jnp.tril(jnp.ones((span_rows, span_rows), jnp.float32), -1)
    inclusive = jnp.tril(jnp.ones((span_rows, span_rows), jnp.float32))
    coupling = (
        jnp.einsum("nhtc,nhsc->nhts", keys_grown, keys_shrunk, precision=highest_precision)
        * jnp.swapaxes(rates, -1, -2)
        * strict
    )
    system = coupling + jnp.eye(span_rows, dtype=jnp.float32)
    solved = matmul_batched(
        unit_lower_inverse(system), jnp.concatenate([values_new, keys_grown], axis=-1)
    )
    fresh = solved[..., :DK] * rates
    carried = solved[..., DK:] * rates
    eye_key = jnp.eye(DK, dtype=jnp.float32)
    transition = jnp.exp(final_log[:, :, 0, :])[..., :, None] * eye_key - jnp.einsum(
        "nhsk,nhsv->nhkv", keys_final, carried, precision=highest_precision
    )
    offset = jnp.einsum("nhsk,nhsv->nhkv", keys_final, fresh, precision=highest_precision)
    mixing = (
        jnp.einsum("nhtc,nhsc->nhts", queries_grown, keys_shrunk, precision=highest_precision)
        * inclusive
    )

    def compose(accumulated, span_parts):
        span_move, span_shift = span_parts
        return (
            (
                matmul_heads(span_move, accumulated[0]),
                matmul_heads(span_move, accumulated[1]) + span_shift,
            ),
            None,
        )

    identity_map = jnp.broadcast_to(eye_key, (heads, DK, DK))
    zero_map = jnp.zeros((heads, DK, DK), jnp.float32)
    (device_move, device_shift), _ = lax.scan(
        compose, (identity_map, zero_map), (transition, offset)
    )
    return (device_move, device_shift, (transition, offset, fresh, carried, queries_grown, mixing))


def emit_step(carried_parts, span_parts):
    recurrent_state, accumulated_move = carried_parts
    span_move, span_shift, fresh_state_term, carried_state_term, query_term, mixing_part = (
        span_parts
    )
    state_update = fresh_state_term - jnp.einsum(
        "orm,omj->orj", carried_state_term, recurrent_state, precision=highest_precision
    )
    produced_output = jnp.einsum(
        "fmb,fbi->fmi", query_term, recurrent_state, precision=highest_precision
    ) + jnp.einsum("hts,hsv->htv", mixing_part, state_update, precision=highest_precision)
    start_weight = query_term - jnp.einsum(
        "hts,hsv->htv", mixing_part, carried_state_term, precision=highest_precision
    )
    start_query = matmul_heads(start_weight, accumulated_move)
    next_parts = (
        matmul_heads(span_move, recurrent_state) + span_shift,
        matmul_heads(span_move, accumulated_move),
    )
    return (next_parts, (produced_output, start_query))


def token_major(span_values):
    stacked = jnp.stack(span_values)
    block_count, heads, span_rows, _ = stacked.shape
    return stacked.transpose(1, 0, 2, 3).reshape(heads, block_count * span_rows, DK)


def finish_spans(start_state, local_outputs, start_queries):
    outputs = local_outputs + matmul_heads(start_queries, start_state)
    heads, length, _ = outputs.shape
    return outputs.transpose(1, 0, 2).reshape(length, heads * DK).astype(jnp.bfloat16)


def per_device(
    kda_inputs,
    gate_log,
    beta,
    conv_weight,
    kda_out_weight,
    residual,
    norm_gain,
    latent_weight,
    latent_gain,
    query_weight,
    up_weight,
):
    length = residual.shape[0]
    edge_rows = kda_inputs[:, length - (CONV - 1) :, :]
    earlier_rows = passed_along(edge_rows, "ctx", 1)
    extended = jnp.concatenate([earlier_rows, kda_inputs], axis=1).astype(jnp.float32)
    running = jnp.zeros(kda_inputs.shape, jnp.float32)
    for tap_index in range(CONV):
        running = (
            running
            + conv_weight[:, tap_index, None, :] * extended[:, tap_index : tap_index + length, :]
        )
    activated = jax.nn.silu(running)
    kda_query = rounded(unit_heads(activated[0]) * DK ** (-0.5))
    kda_key = rounded(unit_heads(activated[1]))
    kda_value = rounded(activated[2])
    device_move, device_shift, span_data = delta_rule(kda_query, kda_key, kda_value, gate_log, beta)
    heads = device_move.shape[0]
    span_count = span_data[0].shape[0]
    emit_carry = (
        jnp.zeros((heads, DK, DK), jnp.float32),
        jnp.broadcast_to(jnp.eye(DK, dtype=jnp.float32), (heads, DK, DK)),
    )
    produced = []

    def run_emit(emit_carry):
        span_index = len(produced)
        emit_carry, emitted = emit_step(emit_carry, tuple(part[span_index] for part in span_data))
        produced.append(emitted)
        return emit_carry

    ctx_size = lax.axis_size("ctx")
    move, shift = device_move, device_shift
    distance = 1
    while distance < ctx_size:
        if 2 * distance < ctx_size:
            both_in = passed_along(jnp.stack([move, shift]), "ctx", distance)
            next_shift = matmul_heads(move, both_in[1]) + shift
            next_move = matmul_heads(move, both_in[0])
        else:
            next_shift = matmul_heads(move, passed_along(shift, "ctx", distance)) + shift
            next_move = move
        if len(produced) < span_count:
            emit_carry = run_emit(emit_carry)
            next_shift, next_move, emit_carry = lax.optimization_barrier(
                (next_shift, next_move, emit_carry)
            )
        move, shift = next_move, next_shift
        distance *= 2
    while len(produced) < span_count:
        emit_carry = run_emit(emit_carry)
    local_outputs = token_major([emitted[0] for emitted in produced])
    start_queries = token_major([emitted[1] for emitted in produced])
    start_state = passed_along(shift, "ctx", 1)
    kda_core = finish_spans(start_state, local_outputs, start_queries)
    partial_proj = jnp.dot(kda_core, kda_out_weight, preferred_element_type=jnp.float32)
    summed = summed_over_head(partial_proj)
    stream_out = (residual.astype(jnp.float32) + summed).astype(jnp.bfloat16)
    normed, latent = prepare(stream_out, norm_gain, latent_weight, latent_gain)
    mla_query = jnp.dot(normed, query_weight, preferred_element_type=jnp.float32).astype(
        jnp.bfloat16
    )
    query_heads = mla_query.reshape(length, -1, DH)
    heads_mla = query_heads.shape[1]
    flat_up = up_weight.reshape(up_weight.shape[0], -1)
    my_first = lax.axis_index("ctx") * length
    query_positions = my_first + jnp.arange(length, dtype=jnp.int32)
    piece = gathered_earlier(latent)
    piece_rows = piece.shape[0]
    paired = (
        jnp.dot(piece, flat_up, preferred_element_type=jnp.float32)
        .astype(jnp.bfloat16)
        .reshape(piece_rows, 2, heads_mla, DH)
    )
    scores = jnp.einsum(
        "qhd,khd->hqk", query_heads, paired[:, 0], preferred_element_type=jnp.float32
    ) * DH ** (-0.5)
    key_positions = jnp.arange(piece_rows, dtype=jnp.int32)
    allowed = key_positions[None, :] <= query_positions[:, None]
    final_peak = jnp.max(jnp.where(allowed, scores, -1e30), axis=-1)
    weights = jnp.where(allowed, jnp.exp(scores - final_peak[..., None]), 0.0)
    final_total = jnp.sum(weights, axis=-1)
    final_mixed = jnp.einsum(
        "hqk,khd->hqd",
        weights.astype(jnp.bfloat16),
        paired[:, 1],
        preferred_element_type=jnp.float32,
    )
    attention_out = (
        (final_mixed / final_total[..., None])
        .transpose(1, 0, 2)
        .reshape(length, heads_mla * DH)
        .astype(jnp.bfloat16)
    )
    return (stream_out, attention_out)


def solution(mesh):
    in_specs = (
        P(None, "ctx", "head"),
        P("ctx", "head"),
        P("ctx", "head"),
        P(None, None, "head"),
        P("head", None),
        P("ctx", None),
        P(),
        P(),
        P(),
        P(None, "head"),
        P(None, None, "head"),
    )
    out_specs = (P("ctx", None), P("ctx", "head"))
    return jax.shard_map(
        per_device, mesh=mesh, in_specs=in_specs, out_specs=out_specs, check_vma=False
    )
```

```python
import math

import jax
import jax.numpy as jnp
from jax import lax
from jax.sharding import PartitionSpec as P
from jax.experimental import pallas as pl
from jax.experimental.pallas import tpu as pltpu

DK = 128
CONV = 4
DH = 128


eps_norm = 1e-06
highest_precision = lax.Precision.HIGHEST


def passed_along(block, axis, distance):
    devices = range(lax.axis_size(axis))
    route = [(i - distance, i) for i in devices if i - distance in devices]
    return lax.ppermute(block, axis, route)


def stream_after_head_sum(partial, residual):
    size = lax.axis_size("head")
    core = lax.axis_index("head") % 2
    half = partial.shape[0] // 2
    pair_route = [(i, i ^ 1) for i in range(size)]
    chip_route = [(i, i ^ 2) for i in range(size)]
    kept = lax.dynamic_slice_in_dim(partial, core * half, half)
    given = lax.dynamic_slice_in_dim(partial, (1 - core) * half, half)
    pair_sum = kept + lax.ppermute(given, "head", pair_route)
    total = pair_sum + lax.ppermute(pair_sum, "head", chip_route)
    my_rows = lax.dynamic_slice_in_dim(residual, core * half, half)
    stream_half = (my_rows.astype(jnp.float32) + total).astype(jnp.bfloat16)
    other_half = lax.ppermute(stream_half, "head", pair_route)
    return jnp.where(
        core == 0,
        jnp.concatenate([stream_half, other_half], axis=0),
        jnp.concatenate([other_half, stream_half], axis=0),
    )


def gather_kernel(block_ref, out_ref, send_sems, recv_sems, forward_sems):
    me = lax.axis_index("ctx")
    head = lax.axis_index("head")
    core = head % 2
    sibling = head + 1 - 2 * core
    count = out_ref.shape[0]
    out_ref[me] = block_ref[...]

    def outgoing(peer):
        return pltpu.make_async_remote_copy(
            src_ref=block_ref,
            dst_ref=out_ref.at[me],
            send_sem=send_sems.at[peer],
            recv_sem=recv_sems.at[me],
            device_id={"ctx": peer, "head": head},
            device_id_type=pl.DeviceIdType.MESH,
        )

    def forwarded(origin):
        return pltpu.make_async_remote_copy(
            src_ref=out_ref.at[origin],
            dst_ref=out_ref.at[origin],
            send_sem=forward_sems.at[origin],
            recv_sem=recv_sems.at[origin],
            device_id={"ctx": me, "head": sibling},
            device_id_type=pl.DeviceIdType.MESH,
        )

    @pl.loop(me + 1, count)
    def _(peer):
        @pl.when((peer + me) % 2 == core)
        def _():
            outgoing(peer).start()

    @pl.loop(me + 1, count)
    def _(peer):
        out_ref[peer] = jnp.zeros(block_ref.shape, block_ref.dtype)

    @pl.loop(0, me)
    def _(origin):
        @pl.when((origin + me) % 2 == core)
        def _():
            forwarded(origin).wait_recv()
            forwarded(origin).start()

    @pl.loop(0, me)
    def _(origin):
        @pl.when((origin + me) % 2 != core)
        def _():
            forwarded(origin).wait_recv()

    @pl.loop(me + 1, count)
    def _(peer):
        @pl.when((peer + me) % 2 == core)
        def _():
            outgoing(peer).wait_send()

    @pl.loop(0, me)
    def _(origin):
        @pl.when((origin + me) % 2 == core)
        def _():
            forwarded(origin).wait_send()


def gathered_earlier(block):
    count = lax.axis_size("ctx")
    rows, width = block.shape
    stacked = pl.pallas_call(
        gather_kernel,
        out_shape=jax.ShapeDtypeStruct((count, rows, width), block.dtype),
        in_specs=[pl.BlockSpec(memory_space=pltpu.VMEM)],
        out_specs=pl.BlockSpec(memory_space=pltpu.VMEM),
        scratch_shapes=[pltpu.SemaphoreType.DMA((count,))] * 3,
        compiler_params=pltpu.CompilerParams(has_side_effects=True),
    )(block)
    return stacked.reshape(count * rows, width)


def rounded(values):
    return lax.optimization_barrier(values.astype(jnp.bfloat16))


def unit_heads(activated):
    grouped = activated.reshape(activated.shape[0], -1, DK)
    scaled = grouped * lax.rsqrt(jnp.sum(grouped * grouped, axis=-1, keepdims=True) + eps_norm)
    return scaled.reshape(activated.shape)


def prepare(stream, norm_gain, latent_weight, latent_gain):
    widened = stream.astype(jnp.float32)
    normed = (
        widened
        * lax.rsqrt(jnp.mean(widened * widened, axis=-1, keepdims=True) + eps_norm)
        * norm_gain
    ).astype(jnp.bfloat16)
    latent_pre = jnp.dot(normed, latent_weight, preferred_element_type=jnp.float32)
    latent = (
        latent_pre
        * lax.rsqrt(jnp.mean(latent_pre * latent_pre, axis=-1, keepdims=True) + eps_norm)
        * latent_gain
    ).astype(jnp.bfloat16)
    return (normed, latent)


def span_layout(values, span_rows):
    length, channel_count = values.shape
    return values.reshape(length // span_rows, span_rows, channel_count // DK, DK).transpose(
        0, 2, 1, 3
    )


def matmul_heads(left, right):
    return jnp.einsum("hij,hjk->hik", left, right, precision=highest_precision)


def matmul_batched(left, right):
    return jnp.einsum("...ij,...jk->...ik", left, right, precision=highest_precision)


def unit_lower_inverse(system):
    size = system.shape[-1]
    rows = jnp.arange(size)[:, None]
    cols = jnp.arange(size)[None, :]
    inverse = jnp.broadcast_to(jnp.eye(size, dtype=system.dtype), system.shape)
    width = 1
    while width < size:
        below = (rows // (2 * width) == cols // (2 * width)) & (rows // width != cols // width)
        off_block = jnp.where(below, system, 0.0)
        correction = matmul_batched(matmul_batched(inverse, off_block), inverse)
        inverse = inverse - lax.optimization_barrier(correction)
        width *= 2
    return inverse


def delta_rule(kda_query, kda_key, kda_value, gate_log, beta):
    span_rows = 32
    length, channel_count = gate_log.shape
    heads = channel_count // DK
    queries = span_layout(kda_query.astype(jnp.float32), span_rows)
    keys_unit = span_layout(kda_key.astype(jnp.float32), span_rows)
    values_new = span_layout(kda_value.astype(jnp.float32), span_rows)
    cumulative = jnp.cumsum(span_layout(gate_log, span_rows), axis=2)
    rates = beta.reshape(length // span_rows, span_rows, heads).transpose(0, 2, 1)[..., None]
    growth = jnp.exp(cumulative)
    final_log = cumulative[:, :, -1:, :]
    keys_grown = keys_unit * growth
    keys_shrunk = keys_unit * jnp.exp(-cumulative)
    queries_grown = queries * growth
    keys_final = keys_unit * jnp.exp(final_log - cumulative)
    strict = jnp.tril(jnp.ones((span_rows, span_rows), jnp.float32), -1)
    inclusive = jnp.tril(jnp.ones((span_rows, span_rows), jnp.float32))
    coupling = (
        jnp.einsum("nhtc,nhsc->nhts", keys_grown, keys_shrunk, precision=highest_precision)
        * jnp.swapaxes(rates, -1, -2)
        * strict
    )
    system = coupling + jnp.eye(span_rows, dtype=jnp.float32)
    solved = matmul_batched(
        unit_lower_inverse(system), jnp.concatenate([values_new, keys_grown], axis=-1)
    )
    fresh = solved[..., :DK] * rates
    carried = solved[..., DK:] * rates
    eye_key = jnp.eye(DK, dtype=jnp.float32)
    transition = jnp.exp(final_log[:, :, 0, :])[..., :, None] * eye_key - jnp.einsum(
        "nhsk,nhsv->nhkv", keys_final, carried, precision=highest_precision
    )
    offset = jnp.einsum("nhsk,nhsv->nhkv", keys_final, fresh, precision=highest_precision)
    mixing = (
        jnp.einsum("nhtc,nhsc->nhts", queries_grown, keys_shrunk, precision=highest_precision)
        * inclusive
    )

    moves, shifts = transition, offset
    while moves.shape[0] > 1:
        later_moves, earlier_moves = moves[1::2], moves[0::2]
        shifts = matmul_batched(later_moves, shifts[0::2]) + shifts[1::2]
        moves = matmul_batched(later_moves, earlier_moves)
    device_move, device_shift = moves[0], shifts[0]
    return (device_move, device_shift, (transition, offset, fresh, carried, queries_grown, mixing))


def emit_step(carried_parts, span_parts):
    recurrent_state, accumulated_move = carried_parts
    span_move, span_shift, fresh_state_term, carried_state_term, query_term, mixing_part = (
        span_parts
    )
    state_update = fresh_state_term - jnp.einsum(
        "orm,omj->orj", carried_state_term, recurrent_state, precision=highest_precision
    )
    produced_output = jnp.einsum(
        "fmb,fbi->fmi", query_term, recurrent_state, precision=highest_precision
    ) + jnp.einsum("hts,hsv->htv", mixing_part, state_update, precision=highest_precision)
    start_weight = query_term - jnp.einsum(
        "hts,hsv->htv", mixing_part, carried_state_term, precision=highest_precision
    )
    start_query = matmul_heads(start_weight, accumulated_move)
    next_parts = (
        matmul_heads(span_move, recurrent_state) + span_shift,
        matmul_heads(span_move, accumulated_move),
    )
    return (next_parts, (produced_output, start_query))


def token_major(span_values):
    stacked = jnp.stack(span_values)
    block_count, heads, span_rows, _ = stacked.shape
    return stacked.transpose(1, 0, 2, 3).reshape(heads, block_count * span_rows, DK)


def finish_spans(start_state, local_outputs, start_queries):
    outputs = local_outputs + matmul_heads(start_queries, start_state)
    heads, length, _ = outputs.shape
    return outputs.transpose(1, 0, 2).reshape(length, heads * DK).astype(jnp.bfloat16)


def per_device(
    kda_inputs,
    gate_log,
    beta,
    conv_weight,
    kda_out_weight,
    residual,
    norm_gain,
    latent_weight,
    latent_gain,
    query_weight,
    up_weight,
):
    length = residual.shape[0]
    edge_rows = kda_inputs[:, length - (CONV - 1) :, :]
    earlier_rows = passed_along(edge_rows, "ctx", 1)
    extended = jnp.concatenate([earlier_rows, kda_inputs], axis=1).astype(jnp.float32)
    running = jnp.zeros(kda_inputs.shape, jnp.float32)
    for tap_index in range(CONV):
        running = (
            running
            + conv_weight[:, tap_index, None, :] * extended[:, tap_index : tap_index + length, :]
        )
    activated = jax.nn.silu(running)
    kda_query = rounded(unit_heads(activated[0]) * DK ** (-0.5))
    kda_key = rounded(unit_heads(activated[1]))
    kda_value = rounded(activated[2])
    device_move, device_shift, span_data = delta_rule(kda_query, kda_key, kda_value, gate_log, beta)
    heads = device_move.shape[0]
    span_count = span_data[0].shape[0]
    emit_carry = (
        jnp.zeros((heads, DK, DK), jnp.float32),
        jnp.broadcast_to(jnp.eye(DK, dtype=jnp.float32), (heads, DK, DK)),
    )
    produced = []

    def run_emit(emit_carry):
        span_index = len(produced)
        emit_carry, emitted = emit_step(emit_carry, tuple(part[span_index] for part in span_data))
        produced.append(emitted)
        return emit_carry

    ctx_size = lax.axis_size("ctx")
    move, shift = device_move, device_shift
    distance = 1
    while distance < ctx_size:
        if 2 * distance < ctx_size:
            both_in = passed_along(jnp.stack([move, shift]), "ctx", distance)
            next_shift = matmul_heads(move, both_in[1]) + shift
            next_move = matmul_heads(move, both_in[0])
        else:
            next_shift = matmul_heads(move, passed_along(shift, "ctx", distance)) + shift
            next_move = move
        if len(produced) < span_count:
            emit_carry = run_emit(emit_carry)
            next_shift, next_move, emit_carry = lax.optimization_barrier(
                (next_shift, next_move, emit_carry)
            )
        move, shift = next_move, next_shift
        distance *= 2
    while len(produced) < span_count:
        emit_carry = run_emit(emit_carry)
    local_outputs = token_major([emitted[0] for emitted in produced])
    start_queries = token_major([emitted[1] for emitted in produced])
    start_state = passed_along(shift, "ctx", 1)
    kda_core = finish_spans(start_state, local_outputs, start_queries)
    partial_proj = jnp.dot(kda_core, kda_out_weight, preferred_element_type=jnp.float32)
    stream_out = stream_after_head_sum(partial_proj, residual)
    normed, latent = prepare(stream_out, norm_gain, latent_weight, latent_gain)
    mla_query = jnp.dot(normed, query_weight, preferred_element_type=jnp.float32).astype(
        jnp.bfloat16
    )
    query_heads = mla_query.reshape(length, -1, DH)
    heads_mla = query_heads.shape[1]
    flat_up = up_weight.reshape(up_weight.shape[0], -1)
    my_first = lax.axis_index("ctx") * length
    query_positions = my_first + jnp.arange(length, dtype=jnp.int32)
    piece = gathered_earlier(latent)
    piece_rows = piece.shape[0]
    paired = (
        jnp.dot(piece, flat_up, preferred_element_type=jnp.float32)
        .astype(jnp.bfloat16)
        .reshape(piece_rows, 2, heads_mla, DH)
    )
    scores = jnp.einsum(
        "qhd,khd->hqk", query_heads, paired[:, 0], preferred_element_type=jnp.float32
    ) * DH ** (-0.5)
    key_positions = jnp.arange(piece_rows, dtype=jnp.int32)
    allowed = key_positions[None, :] <= query_positions[:, None]
    final_peak = jnp.max(jnp.where(allowed, scores, -1e30), axis=-1)
    weights = jnp.where(allowed, jnp.exp(scores - final_peak[..., None]), 0.0)
    final_total = jnp.sum(weights, axis=-1)
    final_mixed = jnp.einsum(
        "hqk,khd->hqd",
        weights.astype(jnp.bfloat16),
        paired[:, 1],
        preferred_element_type=jnp.float32,
    )
    attention_out = (
        (final_mixed / final_total[..., None])
        .transpose(1, 0, 2)
        .reshape(length, heads_mla * DH)
        .astype(jnp.bfloat16)
    )
    return (stream_out, attention_out)


def solution(mesh):
    in_specs = (
        P(None, "ctx", "head"),
        P("ctx", "head"),
        P("ctx", "head"),
        P(None, None, "head"),
        P("head", None),
        P("ctx", None),
        P(),
        P(),
        P(),
        P(None, "head"),
        P(None, None, "head"),
    )
    out_specs = (P("ctx", None), P("ctx", "head"))
    return jax.shard_map(
        per_device, mesh=mesh, in_specs=in_specs, out_specs=out_specs, check_vma=False
    )
```

```python
import math

import jax
import jax.numpy as jnp
from jax import lax
from jax.sharding import PartitionSpec as P
from jax.experimental import pallas as pl
from jax.experimental.pallas import tpu as pltpu

DK = 128
CONV = 4
DH = 128


eps_norm = 1e-06
highest_precision = lax.Precision.HIGHEST


def passed_along(block, axis, distance):
    devices = range(lax.axis_size(axis))
    route = [(i - distance, i) for i in devices if i - distance in devices]
    return lax.ppermute(block, axis, route)


def stream_after_head_sum(partial, residual):
    size = lax.axis_size("head")
    core = lax.axis_index("head") % 2
    half = partial.shape[0] // 2
    pair_route = [(i, i ^ 1) for i in range(size)]
    chip_route = [(i, i ^ 2) for i in range(size)]
    kept = lax.dynamic_slice_in_dim(partial, core * half, half)
    given = lax.dynamic_slice_in_dim(partial, (1 - core) * half, half)
    pair_sum = kept + lax.ppermute(given, "head", pair_route)
    total = pair_sum + lax.ppermute(pair_sum, "head", chip_route)
    my_rows = lax.dynamic_slice_in_dim(residual, core * half, half)
    stream_half = (my_rows.astype(jnp.float32) + total).astype(jnp.bfloat16)
    other_half = lax.ppermute(stream_half, "head", pair_route)
    return jnp.where(
        core == 0,
        jnp.concatenate([stream_half, other_half], axis=0),
        jnp.concatenate([other_half, stream_half], axis=0),
    )


def gather_kernel(block_ref, out_ref, send_sems, recv_sems, forward_sems):
    me = lax.axis_index("ctx")
    head = lax.axis_index("head")
    core = head % 2
    sibling = head + 1 - 2 * core
    count = out_ref.shape[0]
    out_ref[me] = block_ref[...]

    def outgoing(peer):
        return pltpu.make_async_remote_copy(
            src_ref=block_ref,
            dst_ref=out_ref.at[me],
            send_sem=send_sems.at[peer],
            recv_sem=recv_sems.at[me],
            device_id={"ctx": peer, "head": head},
            device_id_type=pl.DeviceIdType.MESH,
        )

    def forwarded(origin):
        return pltpu.make_async_remote_copy(
            src_ref=out_ref.at[origin],
            dst_ref=out_ref.at[origin],
            send_sem=forward_sems.at[origin],
            recv_sem=recv_sems.at[origin],
            device_id={"ctx": me, "head": sibling},
            device_id_type=pl.DeviceIdType.MESH,
        )

    @pl.loop(me + 1, count)
    def _(peer):
        @pl.when((peer + me) % 2 == core)
        def _():
            outgoing(peer).start()

    @pl.loop(me + 1, count)
    def _(peer):
        out_ref[peer] = jnp.zeros(block_ref.shape, block_ref.dtype)

    @pl.loop(0, me)
    def _(origin):
        @pl.when((origin + me) % 2 == core)
        def _():
            forwarded(origin).wait_recv()
            forwarded(origin).start()

    @pl.loop(0, me)
    def _(origin):
        @pl.when((origin + me) % 2 != core)
        def _():
            forwarded(origin).wait_recv()

    @pl.loop(me + 1, count)
    def _(peer):
        @pl.when((peer + me) % 2 == core)
        def _():
            outgoing(peer).wait_send()

    @pl.loop(0, me)
    def _(origin):
        @pl.when((origin + me) % 2 == core)
        def _():
            forwarded(origin).wait_send()


def gathered_earlier(block):
    count = lax.axis_size("ctx")
    rows, width = block.shape
    stacked = pl.pallas_call(
        gather_kernel,
        out_shape=jax.ShapeDtypeStruct((count, rows, width), block.dtype),
        in_specs=[pl.BlockSpec(memory_space=pltpu.VMEM)],
        out_specs=pl.BlockSpec(memory_space=pltpu.VMEM),
        scratch_shapes=[pltpu.SemaphoreType.DMA((count,))] * 3,
        compiler_params=pltpu.CompilerParams(has_side_effects=True),
    )(block)
    return stacked.reshape(count * rows, width)


def rounded(values):
    return lax.optimization_barrier(values.astype(jnp.bfloat16))


def unit_heads(activated):
    grouped = activated.reshape(activated.shape[0], -1, DK)
    scaled = grouped * lax.rsqrt(jnp.sum(grouped * grouped, axis=-1, keepdims=True) + eps_norm)
    return scaled.reshape(activated.shape)


def prepare(stream, norm_gain, latent_weight, latent_gain):
    widened = stream.astype(jnp.float32)
    normed = (
        widened
        * lax.rsqrt(jnp.mean(widened * widened, axis=-1, keepdims=True) + eps_norm)
        * norm_gain
    ).astype(jnp.bfloat16)
    latent_pre = jnp.dot(normed, latent_weight, preferred_element_type=jnp.float32)
    latent = (
        latent_pre
        * lax.rsqrt(jnp.mean(latent_pre * latent_pre, axis=-1, keepdims=True) + eps_norm)
        * latent_gain
    ).astype(jnp.bfloat16)
    return (normed, latent)


def span_layout(values, span_rows):
    length, channel_count = values.shape
    return values.reshape(length // span_rows, span_rows, channel_count // DK, DK).transpose(
        0, 2, 1, 3
    )


def matmul_heads(left, right):
    return jnp.einsum("hij,hjk->hik", left, right, precision=highest_precision)


def matmul_batched(left, right):
    return jnp.einsum("...ij,...jk->...ik", left, right, precision=highest_precision)


def unit_lower_inverse(system):
    size = system.shape[-1]
    rows = jnp.arange(size)[:, None]
    cols = jnp.arange(size)[None, :]
    inverse = jnp.broadcast_to(jnp.eye(size, dtype=system.dtype), system.shape)
    width = 1
    while width < size:
        below = (rows // (2 * width) == cols // (2 * width)) & (rows // width != cols // width)
        off_block = jnp.where(below, system, 0.0)
        correction = matmul_batched(matmul_batched(inverse, off_block), inverse)
        inverse = inverse - lax.optimization_barrier(correction)
        width *= 2
    return inverse


def delta_rule(kda_query, kda_key, kda_value, gate_log, beta):
    span_rows = 32
    length, channel_count = gate_log.shape
    heads = channel_count // DK
    queries = span_layout(kda_query.astype(jnp.float32), span_rows)
    keys_unit = span_layout(kda_key.astype(jnp.float32), span_rows)
    values_new = span_layout(kda_value.astype(jnp.float32), span_rows)
    inclusive_ones = jnp.tril(jnp.ones((span_rows, span_rows), jnp.float32))
    cumulative = jnp.einsum(
        "ts,nhsc->nhtc", inclusive_ones, span_layout(gate_log, span_rows), precision=highest_precision
    )
    rates = beta.reshape(length // span_rows, span_rows, heads).transpose(0, 2, 1)[..., None]
    growth = jnp.exp(cumulative)
    final_log = cumulative[:, :, -1:, :]
    keys_grown = keys_unit * growth
    keys_shrunk = keys_unit * jnp.exp(-cumulative)
    queries_grown = queries * growth
    keys_final = keys_unit * jnp.exp(final_log - cumulative)
    strict = jnp.tril(jnp.ones((span_rows, span_rows), jnp.float32), -1)
    inclusive = jnp.tril(jnp.ones((span_rows, span_rows), jnp.float32))
    coupling = (
        jnp.einsum("nhtc,nhsc->nhts", keys_grown, keys_shrunk, precision=highest_precision)
        * jnp.swapaxes(rates, -1, -2)
        * strict
    )
    system = coupling + jnp.eye(span_rows, dtype=jnp.float32)
    solved = matmul_batched(
        unit_lower_inverse(system), jnp.concatenate([values_new, keys_grown], axis=-1)
    )
    fresh = solved[..., :DK] * rates
    carried = solved[..., DK:] * rates
    eye_key = jnp.eye(DK, dtype=jnp.float32)
    transition = jnp.exp(final_log[:, :, 0, :])[..., :, None] * eye_key - jnp.einsum(
        "nhsk,nhsv->nhkv", keys_final, carried, precision=highest_precision
    )
    offset = jnp.einsum("nhsk,nhsv->nhkv", keys_final, fresh, precision=highest_precision)
    mixing = (
        jnp.einsum("nhtc,nhsc->nhts", queries_grown, keys_shrunk, precision=highest_precision)
        * inclusive
    )

    moves, shifts = transition, offset
    while moves.shape[0] > 1:
        later_moves, earlier_moves = moves[1::2], moves[0::2]
        shifts = matmul_batched(later_moves, shifts[0::2]) + shifts[1::2]
        moves = matmul_batched(later_moves, earlier_moves)
    device_move, device_shift = moves[0], shifts[0]
    return (device_move, device_shift, (transition, offset, fresh, carried, queries_grown, mixing))


def emit_step(carried_parts, span_parts):
    recurrent_state, accumulated_move = carried_parts
    span_move, span_shift, fresh_state_term, carried_state_term, query_term, mixing_part = (
        span_parts
    )
    state_update = fresh_state_term - jnp.einsum(
        "orm,omj->orj", carried_state_term, recurrent_state, precision=highest_precision
    )
    produced_output = jnp.einsum(
        "fmb,fbi->fmi", query_term, recurrent_state, precision=highest_precision
    ) + jnp.einsum("hts,hsv->htv", mixing_part, state_update, precision=highest_precision)
    start_weight = query_term - jnp.einsum(
        "hts,hsv->htv", mixing_part, carried_state_term, precision=highest_precision
    )
    start_query = matmul_heads(start_weight, accumulated_move)
    next_parts = (
        matmul_heads(span_move, recurrent_state) + span_shift,
        matmul_heads(span_move, accumulated_move),
    )
    return (next_parts, (produced_output, start_query))


def token_major(span_values):
    stacked = jnp.stack(span_values)
    block_count, heads, span_rows, _ = stacked.shape
    return stacked.transpose(1, 0, 2, 3).reshape(heads, block_count * span_rows, DK)


def finish_spans(start_state, local_outputs, start_queries):
    outputs = local_outputs + matmul_heads(start_queries, start_state)
    heads, length, _ = outputs.shape
    return outputs.transpose(1, 0, 2).reshape(length, heads * DK).astype(jnp.bfloat16)


def per_device(
    kda_inputs,
    gate_log,
    beta,
    conv_weight,
    kda_out_weight,
    residual,
    norm_gain,
    latent_weight,
    latent_gain,
    query_weight,
    up_weight,
):
    length = residual.shape[0]
    edge_rows = kda_inputs[:, length - (CONV - 1) :, :]
    earlier_rows = passed_along(edge_rows, "ctx", 1)
    extended = jnp.concatenate([earlier_rows, kda_inputs], axis=1).astype(jnp.float32)
    running = jnp.zeros(kda_inputs.shape, jnp.float32)
    for tap_index in range(CONV):
        running = (
            running
            + conv_weight[:, tap_index, None, :] * extended[:, tap_index : tap_index + length, :]
        )
    activated = jax.nn.silu(running)
    kda_query = rounded(unit_heads(activated[0]) * DK ** (-0.5))
    kda_key = rounded(unit_heads(activated[1]))
    kda_value = rounded(activated[2])
    device_move, device_shift, span_data = delta_rule(kda_query, kda_key, kda_value, gate_log, beta)
    heads = device_move.shape[0]
    span_count = span_data[0].shape[0]
    emit_carry = (
        jnp.zeros((heads, DK, DK), jnp.float32),
        jnp.broadcast_to(jnp.eye(DK, dtype=jnp.float32), (heads, DK, DK)),
    )
    produced = []

    def run_emit(emit_carry):
        span_index = len(produced)
        emit_carry, emitted = emit_step(emit_carry, tuple(part[span_index] for part in span_data))
        produced.append(emitted)
        return emit_carry

    ctx_size = lax.axis_size("ctx")
    move, shift = device_move, device_shift
    distance = 1
    while distance < ctx_size:
        if 2 * distance < ctx_size:
            shift_high = shift.astype(jnp.bfloat16)
            shift_low = (shift - shift_high.astype(jnp.float32)).astype(jnp.bfloat16)
            sent = jnp.stack([move.astype(jnp.bfloat16), shift_high, shift_low])
            both_in = passed_along(sent, "ctx", distance).astype(jnp.float32)
            next_shift = matmul_heads(move, both_in[1] + both_in[2]) + shift
            next_move = matmul_heads(move, both_in[0])
        else:
            next_shift = matmul_heads(move, passed_along(shift, "ctx", distance)) + shift
            next_move = move
        if len(produced) < span_count:
            emit_carry = run_emit(emit_carry)
            next_shift, next_move, emit_carry = lax.optimization_barrier(
                (next_shift, next_move, emit_carry)
            )
        move, shift = next_move, next_shift
        distance *= 2
    while len(produced) < span_count:
        emit_carry = run_emit(emit_carry)
    local_outputs = token_major([emitted[0] for emitted in produced])
    start_queries = token_major([emitted[1] for emitted in produced])
    start_state = passed_along(shift, "ctx", 1)
    kda_core = finish_spans(start_state, local_outputs, start_queries)
    partial_proj = jnp.dot(kda_core, kda_out_weight, preferred_element_type=jnp.float32)
    stream_out = stream_after_head_sum(partial_proj, residual)
    normed, latent = prepare(stream_out, norm_gain, latent_weight, latent_gain)
    mla_query = jnp.dot(normed, query_weight, preferred_element_type=jnp.float32).astype(
        jnp.bfloat16
    )
    query_heads = mla_query.reshape(length, -1, DH)
    heads_mla = query_heads.shape[1]
    flat_up = up_weight.reshape(up_weight.shape[0], -1)
    my_first = lax.axis_index("ctx") * length
    query_positions = my_first + jnp.arange(length, dtype=jnp.int32)
    piece = gathered_earlier(latent)
    piece_rows = piece.shape[0]
    paired = (
        jnp.dot(piece, flat_up, preferred_element_type=jnp.float32)
        .astype(jnp.bfloat16)
        .reshape(piece_rows, 2, heads_mla, DH)
    )
    scores = jnp.einsum(
        "qhd,khd->hqk", query_heads, paired[:, 0], preferred_element_type=jnp.float32
    ) * DH ** (-0.5)
    key_positions = jnp.arange(piece_rows, dtype=jnp.int32)
    allowed = key_positions[None, :] <= query_positions[:, None]
    final_peak = jnp.max(jnp.where(allowed, scores, -1e30), axis=-1)
    weights = jnp.where(allowed, jnp.exp(scores - final_peak[..., None]), 0.0)
    final_total = jnp.sum(weights, axis=-1)
    final_mixed = jnp.einsum(
        "hqk,khd->hqd",
        weights.astype(jnp.bfloat16),
        paired[:, 1],
        preferred_element_type=jnp.float32,
    )
    attention_out = (
        (final_mixed / final_total[..., None])
        .transpose(1, 0, 2)
        .reshape(length, heads_mla * DH)
        .astype(jnp.bfloat16)
    )
    return (stream_out, attention_out)


def solution(mesh):
    in_specs = (
        P(None, "ctx", "head"),
        P("ctx", "head"),
        P("ctx", "head"),
        P(None, None, "head"),
        P("head", None),
        P("ctx", None),
        P(),
        P(),
        P(),
        P(None, "head"),
        P(None, None, "head"),
    )
    out_specs = (P("ctx", None), P("ctx", "head"))
    return jax.shard_map(
        per_device, mesh=mesh, in_specs=in_specs, out_specs=out_specs, check_vma=False
    )
```

```python
import math

import jax
import jax.numpy as jnp
from jax import lax
from jax.sharding import PartitionSpec as P
from jax.experimental import pallas as pl
from jax.experimental.pallas import tpu as pltpu

DK = 128
CONV = 4
DH = 128


eps_norm = 1e-06
highest_precision = lax.Precision.HIGHEST


def passed_along(block, axis, distance):
    devices = range(lax.axis_size(axis))
    route = [(i - distance, i) for i in devices if i - distance in devices]
    return lax.ppermute(block, axis, route)


def stream_after_head_sum(partial, residual):
    size = lax.axis_size("head")
    core = lax.axis_index("head") % 2
    half = partial.shape[0] // 2
    pair_route = [(i, i ^ 1) for i in range(size)]
    chip_route = [(i, i ^ 2) for i in range(size)]
    kept = lax.dynamic_slice_in_dim(partial, core * half, half)
    given = lax.dynamic_slice_in_dim(partial, (1 - core) * half, half)
    pair_sum = kept + lax.ppermute(given, "head", pair_route)
    total = pair_sum + lax.ppermute(pair_sum, "head", chip_route)
    my_rows = lax.dynamic_slice_in_dim(residual, core * half, half)
    stream_half = (my_rows.astype(jnp.float32) + total).astype(jnp.bfloat16)
    other_half = lax.ppermute(stream_half, "head", pair_route)
    return jnp.where(
        core == 0,
        jnp.concatenate([stream_half, other_half], axis=0),
        jnp.concatenate([other_half, stream_half], axis=0),
    )


def gather_kernel(block_ref, up_ref, kv_ref, landed, send_sems, recv_sems, forward_sems):
    me = lax.axis_index("ctx")
    head = lax.axis_index("head")
    core = head % 2
    sibling = head + 1 - 2 * core
    count = landed.shape[0]

    def outgoing(peer):
        return pltpu.make_async_remote_copy(
            src_ref=block_ref,
            dst_ref=landed.at[me],
            send_sem=send_sems.at[peer],
            recv_sem=recv_sems.at[me],
            device_id={"ctx": peer, "head": head},
            device_id_type=pl.DeviceIdType.MESH,
        )

    def forwarded(origin):
        return pltpu.make_async_remote_copy(
            src_ref=landed.at[origin],
            dst_ref=landed.at[origin],
            send_sem=forward_sems.at[origin],
            recv_sem=recv_sems.at[origin],
            device_id={"ctx": me, "head": sibling},
            device_id_type=pl.DeviceIdType.MESH,
        )

    def project(latent_rows):
        return jnp.dot(latent_rows, up_ref[...], preferred_element_type=jnp.float32).astype(
            kv_ref.dtype
        )

    @pl.loop(me + 1, count)
    def _(peer):
        @pl.when((peer + me) % 2 == core)
        def _():
            outgoing(peer).start()

    kv_ref[me] = project(block_ref[...])

    @pl.loop(me + 1, count)
    def _(peer):
        kv_ref[peer] = jnp.zeros(kv_ref.shape[1:], kv_ref.dtype)

    @pl.loop(0, me)
    def _(origin):
        @pl.when((origin + me) % 2 == core)
        def _():
            forwarded(origin).wait_recv()
            forwarded(origin).start()

        @pl.when((origin + me) % 2 != core)
        def _():
            forwarded(origin).wait_recv()

        kv_ref[origin] = project(landed[origin])

    @pl.loop(me + 1, count)
    def _(peer):
        @pl.when((peer + me) % 2 == core)
        def _():
            outgoing(peer).wait_send()

    @pl.loop(0, me)
    def _(origin):
        @pl.when((origin + me) % 2 == core)
        def _():
            forwarded(origin).wait_send()


def projected_earlier(block, flat_up):
    count = lax.axis_size("ctx")
    rows, width = block.shape
    projected = pl.pallas_call(
        gather_kernel,
        out_shape=jax.ShapeDtypeStruct((count, rows, flat_up.shape[1]), block.dtype),
        in_specs=[pl.BlockSpec(memory_space=pltpu.VMEM)] * 2,
        out_specs=pl.BlockSpec(memory_space=pltpu.VMEM),
        scratch_shapes=[pltpu.VMEM((count, rows, width), block.dtype)]
        + [pltpu.SemaphoreType.DMA((count,))] * 3,
        compiler_params=pltpu.CompilerParams(has_side_effects=True),
    )(block, flat_up)
    return projected.reshape(count * rows, flat_up.shape[1])


def rounded(values):
    return lax.optimization_barrier(values.astype(jnp.bfloat16))


def unit_heads(activated):
    grouped = activated.reshape(activated.shape[0], -1, DK)
    scaled = grouped * lax.rsqrt(jnp.sum(grouped * grouped, axis=-1, keepdims=True) + eps_norm)
    return scaled.reshape(activated.shape)


def prepare(stream, norm_gain, latent_weight, latent_gain):
    widened = stream.astype(jnp.float32)
    normed = (
        widened
        * lax.rsqrt(jnp.mean(widened * widened, axis=-1, keepdims=True) + eps_norm)
        * norm_gain
    ).astype(jnp.bfloat16)
    latent_pre = jnp.dot(normed, latent_weight, preferred_element_type=jnp.float32)
    latent = (
        latent_pre
        * lax.rsqrt(jnp.mean(latent_pre * latent_pre, axis=-1, keepdims=True) + eps_norm)
        * latent_gain
    ).astype(jnp.bfloat16)
    return (normed, latent)


def span_layout(values, span_rows):
    length, channel_count = values.shape
    return values.reshape(length // span_rows, span_rows, channel_count // DK, DK).transpose(
        0, 2, 1, 3
    )


def matmul_heads(left, right):
    return jnp.einsum("hij,hjk->hik", left, right, precision=highest_precision)


def matmul_batched(left, right):
    return jnp.einsum("...ij,...jk->...ik", left, right, precision=highest_precision)


def unit_lower_inverse(system):
    size = system.shape[-1]
    rows = jnp.arange(size)[:, None]
    cols = jnp.arange(size)[None, :]
    inverse = jnp.broadcast_to(jnp.eye(size, dtype=system.dtype), system.shape)
    width = 1
    while width < size:
        below = (rows // (2 * width) == cols // (2 * width)) & (rows // width != cols // width)
        off_block = jnp.where(below, system, 0.0)
        correction = matmul_batched(matmul_batched(inverse, off_block), inverse)
        inverse = inverse - lax.optimization_barrier(correction)
        width *= 2
    return inverse


def delta_rule(kda_query, kda_key, kda_value, gate_log, beta):
    span_rows = 32
    length, channel_count = gate_log.shape
    heads = channel_count // DK
    queries = span_layout(kda_query.astype(jnp.float32), span_rows)
    keys_unit = span_layout(kda_key.astype(jnp.float32), span_rows)
    values_new = span_layout(kda_value.astype(jnp.float32), span_rows)
    inclusive_ones = jnp.tril(jnp.ones((span_rows, span_rows), jnp.float32))
    cumulative = jnp.einsum(
        "ts,nhsc->nhtc", inclusive_ones, span_layout(gate_log, span_rows), precision=highest_precision
    )
    rates = beta.reshape(length // span_rows, span_rows, heads).transpose(0, 2, 1)[..., None]
    growth = jnp.exp(cumulative)
    final_log = cumulative[:, :, -1:, :]
    keys_grown = keys_unit * growth
    keys_shrunk = keys_unit * jnp.exp(-cumulative)
    queries_grown = queries * growth
    keys_final = keys_unit * jnp.exp(final_log - cumulative)
    strict = jnp.tril(jnp.ones((span_rows, span_rows), jnp.float32), -1)
    inclusive = jnp.tril(jnp.ones((span_rows, span_rows), jnp.float32))
    coupling = (
        jnp.einsum("nhtc,nhsc->nhts", keys_grown, keys_shrunk, precision=highest_precision)
        * jnp.swapaxes(rates, -1, -2)
        * strict
    )
    system = coupling + jnp.eye(span_rows, dtype=jnp.float32)
    solved = matmul_batched(
        unit_lower_inverse(system), jnp.concatenate([values_new, keys_grown], axis=-1)
    )
    fresh = solved[..., :DK] * rates
    carried = solved[..., DK:] * rates
    eye_key = jnp.eye(DK, dtype=jnp.float32)
    transition = jnp.exp(final_log[:, :, 0, :])[..., :, None] * eye_key - jnp.einsum(
        "nhsk,nhsv->nhkv", keys_final, carried, precision=highest_precision
    )
    offset = jnp.einsum("nhsk,nhsv->nhkv", keys_final, fresh, precision=highest_precision)
    mixing = (
        jnp.einsum("nhtc,nhsc->nhts", queries_grown, keys_shrunk, precision=highest_precision)
        * inclusive
    )

    moves, shifts = transition, offset
    while moves.shape[0] > 1:
        later_moves, earlier_moves = moves[1::2], moves[0::2]
        shifts = matmul_batched(later_moves, shifts[0::2]) + shifts[1::2]
        moves = matmul_batched(later_moves, earlier_moves)
    device_move, device_shift = moves[0], shifts[0]
    return (device_move, device_shift, (transition, offset, fresh, carried, queries_grown, mixing))


def emit_step(carried_parts, span_parts):
    recurrent_state, accumulated_move = carried_parts
    span_move, span_shift, fresh_state_term, carried_state_term, query_term, mixing_part = (
        span_parts
    )
    state_update = fresh_state_term - jnp.einsum(
        "orm,omj->orj", carried_state_term, recurrent_state, precision=highest_precision
    )
    produced_output = jnp.einsum(
        "fmb,fbi->fmi", query_term, recurrent_state, precision=highest_precision
    ) + jnp.einsum("hts,hsv->htv", mixing_part, state_update, precision=highest_precision)
    start_weight = query_term - jnp.einsum(
        "hts,hsv->htv", mixing_part, carried_state_term, precision=highest_precision
    )
    start_query = matmul_heads(start_weight, accumulated_move)
    next_parts = (
        matmul_heads(span_move, recurrent_state) + span_shift,
        matmul_heads(span_move, accumulated_move),
    )
    return (next_parts, (produced_output, start_query))


def token_major(span_values):
    stacked = jnp.stack(span_values)
    block_count, heads, span_rows, _ = stacked.shape
    return stacked.transpose(1, 0, 2, 3).reshape(heads, block_count * span_rows, DK)


def finish_spans(start_state, local_outputs, start_queries):
    outputs = local_outputs + matmul_heads(start_queries, start_state)
    heads, length, _ = outputs.shape
    return outputs.transpose(1, 0, 2).reshape(length, heads * DK).astype(jnp.bfloat16)


def per_device(
    kda_inputs,
    gate_log,
    beta,
    conv_weight,
    kda_out_weight,
    residual,
    norm_gain,
    latent_weight,
    latent_gain,
    query_weight,
    up_weight,
):
    length = residual.shape[0]
    edge_rows = kda_inputs[:, length - (CONV - 1) :, :]
    earlier_rows = passed_along(edge_rows, "ctx", 1)
    extended = jnp.concatenate([earlier_rows, kda_inputs], axis=1).astype(jnp.float32)
    running = jnp.zeros(kda_inputs.shape, jnp.float32)
    for tap_index in range(CONV):
        running = (
            running
            + conv_weight[:, tap_index, None, :] * extended[:, tap_index : tap_index + length, :]
        )
    activated = jax.nn.silu(running)
    kda_query = rounded(unit_heads(activated[0]) * DK ** (-0.5))
    kda_key = rounded(unit_heads(activated[1]))
    kda_value = rounded(activated[2])
    device_move, device_shift, span_data = delta_rule(kda_query, kda_key, kda_value, gate_log, beta)
    heads = device_move.shape[0]
    span_count = span_data[0].shape[0]
    emit_carry = (
        jnp.zeros((heads, DK, DK), jnp.float32),
        jnp.broadcast_to(jnp.eye(DK, dtype=jnp.float32), (heads, DK, DK)),
    )
    produced = []

    def run_emit(emit_carry):
        span_index = len(produced)
        emit_carry, emitted = emit_step(emit_carry, tuple(part[span_index] for part in span_data))
        produced.append(emitted)
        return emit_carry

    ctx_size = lax.axis_size("ctx")
    move, shift = device_move, device_shift
    distance = 1
    while distance < ctx_size:
        if 2 * distance < ctx_size:
            shift_high = shift.astype(jnp.bfloat16)
            shift_low = (shift - shift_high.astype(jnp.float32)).astype(jnp.bfloat16)
            sent = jnp.stack([move.astype(jnp.bfloat16), shift_high, shift_low])
            both_in = passed_along(sent, "ctx", distance).astype(jnp.float32)
            next_shift = matmul_heads(move, both_in[1] + both_in[2]) + shift
            next_move = matmul_heads(move, both_in[0])
        else:
            next_shift = matmul_heads(move, passed_along(shift, "ctx", distance)) + shift
            next_move = move
        if len(produced) < span_count:
            emit_carry = run_emit(emit_carry)
            next_shift, next_move, emit_carry = lax.optimization_barrier(
                (next_shift, next_move, emit_carry)
            )
        move, shift = next_move, next_shift
        distance *= 2
    while len(produced) < span_count:
        emit_carry = run_emit(emit_carry)
    local_outputs = token_major([emitted[0] for emitted in produced])
    start_queries = token_major([emitted[1] for emitted in produced])
    start_state = passed_along(shift, "ctx", 1)
    kda_core = finish_spans(start_state, local_outputs, start_queries)
    partial_proj = jnp.dot(kda_core, kda_out_weight, preferred_element_type=jnp.float32)
    stream_out = stream_after_head_sum(partial_proj, residual)
    normed, latent = prepare(stream_out, norm_gain, latent_weight, latent_gain)
    mla_query = jnp.dot(normed, query_weight, preferred_element_type=jnp.float32).astype(
        jnp.bfloat16
    )
    query_heads = mla_query.reshape(length, -1, DH)
    heads_mla = query_heads.shape[1]
    flat_up = up_weight.reshape(up_weight.shape[0], -1)
    my_first = lax.axis_index("ctx") * length
    query_positions = my_first + jnp.arange(length, dtype=jnp.int32)
    projected = projected_earlier(latent, flat_up)
    piece_rows = projected.shape[0]
    paired = projected.reshape(piece_rows, 2, heads_mla, DH)
    scores = jnp.einsum(
        "qhd,khd->hqk", query_heads, paired[:, 0], preferred_element_type=jnp.float32
    ) * DH ** (-0.5)
    key_positions = jnp.arange(piece_rows, dtype=jnp.int32)
    allowed = key_positions[None, :] <= query_positions[:, None]
    final_peak = jnp.max(jnp.where(allowed, scores, -1e30), axis=-1)
    weights = jnp.where(allowed, jnp.exp(scores - final_peak[..., None]), 0.0)
    final_total = jnp.sum(weights, axis=-1)
    final_mixed = jnp.einsum(
        "hqk,khd->hqd",
        weights.astype(jnp.bfloat16),
        paired[:, 1],
        preferred_element_type=jnp.float32,
    )
    attention_out = (
        (final_mixed / final_total[..., None])
        .transpose(1, 0, 2)
        .reshape(length, heads_mla * DH)
        .astype(jnp.bfloat16)
    )
    return (stream_out, attention_out)


def solution(mesh):
    in_specs = (
        P(None, "ctx", "head"),
        P("ctx", "head"),
        P("ctx", "head"),
        P(None, None, "head"),
        P("head", None),
        P("ctx", None),
        P(),
        P(),
        P(),
        P(None, "head"),
        P(None, None, "head"),
    )
    out_specs = (P("ctx", None), P("ctx", "head"))
    return jax.shard_map(
        per_device, mesh=mesh, in_specs=in_specs, out_specs=out_specs, check_vma=False
    )
```

```python
import math

import jax
import jax.numpy as jnp
from jax import lax
from jax.sharding import PartitionSpec as P
from jax.experimental import pallas as pl
from jax.experimental.pallas import tpu as pltpu

DK = 128
CONV = 4
DH = 128


eps_norm = 1e-06
highest_precision = lax.Precision.HIGHEST


def passed_along(block, axis, distance):
    devices = range(lax.axis_size(axis))
    route = [(i - distance, i) for i in devices if i - distance in devices]
    return lax.ppermute(block, axis, route)


def stream_after_head_sum(partial, residual):
    size = lax.axis_size("head")
    core = lax.axis_index("head") % 2
    half = partial.shape[0] // 2
    pair_route = [(i, i ^ 1) for i in range(size)]
    chip_route = [(i, i ^ 2) for i in range(size)]
    kept = lax.dynamic_slice_in_dim(partial, core * half, half)
    given = lax.dynamic_slice_in_dim(partial, (1 - core) * half, half)
    pair_sum = kept + lax.ppermute(given, "head", pair_route)
    total = pair_sum + lax.ppermute(pair_sum, "head", chip_route)
    my_rows = lax.dynamic_slice_in_dim(residual, core * half, half)
    stream_half = (my_rows.astype(jnp.float32) + total).astype(jnp.bfloat16)
    other_half = lax.ppermute(stream_half, "head", pair_route)
    return jnp.where(
        core == 0,
        jnp.concatenate([stream_half, other_half], axis=0),
        jnp.concatenate([other_half, stream_half], axis=0),
    )


def gather_kernel(block_ref, out_ref, send_sems, recv_sems, forward_sems):
    me = lax.axis_index("ctx")
    head = lax.axis_index("head")
    core = head % 2
    sibling = head + 1 - 2 * core
    count = out_ref.shape[0]
    out_ref[me] = block_ref[...]

    def outgoing(peer):
        return pltpu.make_async_remote_copy(
            src_ref=block_ref,
            dst_ref=out_ref.at[me],
            send_sem=send_sems.at[peer],
            recv_sem=recv_sems.at[me],
            device_id={"ctx": peer, "head": head},
            device_id_type=pl.DeviceIdType.MESH,
        )

    def forwarded(origin):
        return pltpu.make_async_remote_copy(
            src_ref=out_ref.at[origin],
            dst_ref=out_ref.at[origin],
            send_sem=forward_sems.at[origin],
            recv_sem=recv_sems.at[origin],
            device_id={"ctx": me, "head": sibling},
            device_id_type=pl.DeviceIdType.MESH,
        )

    @pl.loop(me + 1, count)
    def _(peer):
        @pl.when((peer + me) % 2 == core)
        def _():
            outgoing(peer).start()

    @pl.loop(me + 1, count)
    def _(peer):
        out_ref[peer] = jnp.zeros(block_ref.shape, block_ref.dtype)

    @pl.loop(0, me)
    def _(origin):
        @pl.when((origin + me) % 2 == core)
        def _():
            forwarded(origin).wait_recv()
            forwarded(origin).start()

    @pl.loop(0, me)
    def _(origin):
        @pl.when((origin + me) % 2 != core)
        def _():
            forwarded(origin).wait_recv()

    @pl.loop(me + 1, count)
    def _(peer):
        @pl.when((peer + me) % 2 == core)
        def _():
            outgoing(peer).wait_send()

    @pl.loop(0, me)
    def _(origin):
        @pl.when((origin + me) % 2 == core)
        def _():
            forwarded(origin).wait_send()


def gathered_earlier(block):
    count = lax.axis_size("ctx")
    rows, width = block.shape
    stacked = pl.pallas_call(
        gather_kernel,
        out_shape=jax.ShapeDtypeStruct((count, rows, width), block.dtype),
        in_specs=[pl.BlockSpec(memory_space=pltpu.VMEM)],
        out_specs=pl.BlockSpec(memory_space=pltpu.VMEM),
        scratch_shapes=[pltpu.SemaphoreType.DMA((count,))] * 3,
        compiler_params=pltpu.CompilerParams(has_side_effects=True),
    )(block)
    return stacked.reshape(count * rows, width)


def rounded(values):
    return lax.optimization_barrier(values.astype(jnp.bfloat16))


def unit_heads(activated):
    grouped = activated.reshape(activated.shape[0], -1, DK)
    scaled = grouped * lax.rsqrt(jnp.sum(grouped * grouped, axis=-1, keepdims=True) + eps_norm)
    return scaled.reshape(activated.shape)


def prepare(stream, norm_gain, latent_weight, latent_gain):
    widened = stream.astype(jnp.float32)
    normed = (
        widened
        * lax.rsqrt(jnp.mean(widened * widened, axis=-1, keepdims=True) + eps_norm)
        * norm_gain
    ).astype(jnp.bfloat16)
    latent_pre = jnp.dot(normed, latent_weight, preferred_element_type=jnp.float32)
    latent = (
        latent_pre
        * lax.rsqrt(jnp.mean(latent_pre * latent_pre, axis=-1, keepdims=True) + eps_norm)
        * latent_gain
    ).astype(jnp.bfloat16)
    return (normed, latent)


def span_layout(values, span_rows):
    length, channel_count = values.shape
    return values.reshape(length // span_rows, span_rows, channel_count // DK, DK).transpose(
        0, 2, 1, 3
    )


def matmul_heads(left, right):
    return jnp.einsum("hij,hjk->hik", left, right, precision=highest_precision)


def matmul_batched(left, right):
    return jnp.einsum("...ij,...jk->...ik", left, right, precision=highest_precision)


def unit_lower_inverse(system):
    size = system.shape[-1]
    rows = jnp.arange(size)[:, None]
    cols = jnp.arange(size)[None, :]
    inverse = jnp.broadcast_to(jnp.eye(size, dtype=system.dtype), system.shape)
    width = 1
    while width < size:
        below = (rows // (2 * width) == cols // (2 * width)) & (rows // width != cols // width)
        off_block = jnp.where(below, system, 0.0)
        correction = matmul_batched(matmul_batched(inverse, off_block), inverse)
        inverse = inverse - lax.optimization_barrier(correction)
        width *= 2
    return inverse


def delta_rule(kda_query, kda_key, kda_value, gate_log, beta):
    span_rows = 32
    length, channel_count = gate_log.shape
    heads = channel_count // DK
    queries = span_layout(kda_query.astype(jnp.float32), span_rows)
    keys_unit = span_layout(kda_key.astype(jnp.float32), span_rows)
    values_new = span_layout(kda_value.astype(jnp.float32), span_rows)
    inclusive_ones = jnp.tril(jnp.ones((span_rows, span_rows), jnp.float32))
    cumulative = jnp.einsum(
        "ts,nhsc->nhtc", inclusive_ones, span_layout(gate_log, span_rows), precision=highest_precision
    )
    rates = beta.reshape(length // span_rows, span_rows, heads).transpose(0, 2, 1)[..., None]
    growth = jnp.exp(cumulative)
    final_log = cumulative[:, :, -1:, :]
    keys_grown = keys_unit * growth
    keys_shrunk = keys_unit * jnp.exp(-cumulative)
    queries_grown = queries * growth
    keys_final = keys_unit * jnp.exp(final_log - cumulative)
    strict = jnp.tril(jnp.ones((span_rows, span_rows), jnp.float32), -1)
    inclusive = jnp.tril(jnp.ones((span_rows, span_rows), jnp.float32))
    coupling = (
        jnp.einsum("nhtc,nhsc->nhts", keys_grown, keys_shrunk, precision=highest_precision)
        * jnp.swapaxes(rates, -1, -2)
        * strict
    )
    system = coupling + jnp.eye(span_rows, dtype=jnp.float32)
    solved = matmul_batched(
        unit_lower_inverse(system), jnp.concatenate([values_new, keys_grown], axis=-1)
    )
    fresh = solved[..., :DK] * rates
    carried = solved[..., DK:] * rates
    eye_key = jnp.eye(DK, dtype=jnp.float32)
    transition = jnp.exp(final_log[:, :, 0, :])[..., :, None] * eye_key - jnp.einsum(
        "nhsk,nhsv->nhkv", keys_final, carried, precision=highest_precision
    )
    offset = jnp.einsum("nhsk,nhsv->nhkv", keys_final, fresh, precision=highest_precision)
    mixing = (
        jnp.einsum("nhtc,nhsc->nhts", queries_grown, keys_shrunk, precision=highest_precision)
        * inclusive
    )

    moves, shifts = transition, offset
    while moves.shape[0] > 1:
        later_moves, earlier_moves = moves[1::2], moves[0::2]
        shifts = matmul_batched(later_moves, shifts[0::2]) + shifts[1::2]
        moves = matmul_batched(later_moves, earlier_moves)
    device_move, device_shift = moves[0], shifts[0]
    return (device_move, device_shift, (transition, offset, fresh, carried, queries_grown, mixing))


def emit_step(carried_parts, span_parts):
    recurrent_state, accumulated_move = carried_parts
    span_move, span_shift, fresh_state_term, carried_state_term, query_term, mixing_part = (
        span_parts
    )
    state_update = fresh_state_term - jnp.einsum(
        "orm,omj->orj", carried_state_term, recurrent_state, precision=highest_precision
    )
    produced_output = jnp.einsum(
        "fmb,fbi->fmi", query_term, recurrent_state, precision=highest_precision
    ) + jnp.einsum("hts,hsv->htv", mixing_part, state_update, precision=highest_precision)
    start_weight = query_term - jnp.einsum(
        "hts,hsv->htv", mixing_part, carried_state_term, precision=highest_precision
    )
    start_query = matmul_heads(start_weight, accumulated_move)
    next_parts = (
        matmul_heads(span_move, recurrent_state) + span_shift,
        matmul_heads(span_move, accumulated_move),
    )
    return (next_parts, (produced_output, start_query))


def token_major(span_values):
    stacked = jnp.stack(span_values)
    block_count, heads, span_rows, _ = stacked.shape
    return stacked.transpose(1, 0, 2, 3).reshape(heads, block_count * span_rows, DK)


def finish_spans(start_state, local_outputs, start_queries):
    outputs = local_outputs + matmul_heads(start_queries, start_state)
    heads, length, _ = outputs.shape
    return outputs.transpose(1, 0, 2).reshape(length, heads * DK).astype(jnp.bfloat16)


def per_device(
    kda_inputs,
    gate_log,
    beta,
    conv_weight,
    kda_out_weight,
    residual,
    norm_gain,
    latent_weight,
    latent_gain,
    query_weight,
    up_weight,
):
    length = residual.shape[0]
    edge_rows = kda_inputs[:, length - (CONV - 1) :, :]
    earlier_rows = passed_along(edge_rows, "ctx", 1)
    extended = jnp.concatenate([earlier_rows, kda_inputs], axis=1).astype(jnp.float32)
    running = jnp.zeros(kda_inputs.shape, jnp.float32)
    for tap_index in range(CONV):
        running = (
            running
            + conv_weight[:, tap_index, None, :] * extended[:, tap_index : tap_index + length, :]
        )
    activated = jax.nn.silu(running)
    kda_query = rounded(unit_heads(activated[0]) * DK ** (-0.5))
    kda_key = rounded(unit_heads(activated[1]))
    kda_value = rounded(activated[2])
    device_move, device_shift, span_data = delta_rule(kda_query, kda_key, kda_value, gate_log, beta)
    heads = device_move.shape[0]
    span_count = span_data[0].shape[0]
    emit_carry = (
        jnp.zeros((heads, DK, DK), jnp.float32),
        jnp.broadcast_to(jnp.eye(DK, dtype=jnp.float32), (heads, DK, DK)),
    )
    produced = []

    def run_emit(emit_carry):
        span_index = len(produced)
        emit_carry, emitted = emit_step(emit_carry, tuple(part[span_index] for part in span_data))
        produced.append(emitted)
        return emit_carry

    ctx_size = lax.axis_size("ctx")
    move, shift = device_move, device_shift
    distance = 1
    while distance < ctx_size:
        if 2 * distance < ctx_size:
            shift_high = shift.astype(jnp.bfloat16)
            shift_low = (shift - shift_high.astype(jnp.float32)).astype(jnp.bfloat16)
            sent = jnp.stack([move.astype(jnp.bfloat16), shift_high, shift_low])
            both_in = passed_along(sent, "ctx", distance).astype(jnp.float32)
            next_shift = matmul_heads(move, both_in[1] + both_in[2]) + shift
            next_move = matmul_heads(move, both_in[0])
        else:
            next_shift = matmul_heads(move, passed_along(shift, "ctx", distance)) + shift
            next_move = move
        if len(produced) < span_count:
            emit_carry = run_emit(emit_carry)
            next_shift, next_move, emit_carry = lax.optimization_barrier(
                (next_shift, next_move, emit_carry)
            )
        move, shift = next_move, next_shift
        distance *= 2
    while len(produced) < span_count:
        emit_carry = run_emit(emit_carry)
    local_outputs = token_major([emitted[0] for emitted in produced])
    start_queries = token_major([emitted[1] for emitted in produced])
    start_state = passed_along(shift, "ctx", 1)
    kda_core = finish_spans(start_state, local_outputs, start_queries)
    partial_proj = jnp.dot(kda_core, kda_out_weight, preferred_element_type=jnp.float32)
    stream_out = stream_after_head_sum(partial_proj, residual)
    normed, latent = prepare(stream_out, norm_gain, latent_weight, latent_gain)
    mla_query = jnp.dot(normed, query_weight, preferred_element_type=jnp.float32).astype(
        jnp.bfloat16
    )
    query_heads = mla_query.reshape(length, -1, DH)
    heads_mla = query_heads.shape[1]
    flat_up = up_weight.reshape(up_weight.shape[0], -1)
    my_first = lax.axis_index("ctx") * length
    query_positions = my_first + jnp.arange(length, dtype=jnp.int32)
    up_keys = up_weight[:, 0, :].reshape(up_weight.shape[0], heads_mla, DH)
    up_values = up_weight[:, 1, :].reshape(up_weight.shape[0], heads_mla, DH)
    query_latent = jnp.einsum(
        "qhd,lhd->hql", query_heads, up_keys, preferred_element_type=jnp.float32
    ).astype(jnp.bfloat16)
    piece = gathered_earlier(latent)
    piece_rows = piece.shape[0]
    scores = jnp.einsum(
        "hql,kl->hqk", query_latent, piece, preferred_element_type=jnp.float32
    ) * DH ** (-0.5)
    key_positions = jnp.arange(piece_rows, dtype=jnp.int32)
    allowed = key_positions[None, :] <= query_positions[:, None]
    final_peak = jnp.max(jnp.where(allowed, scores, -1e30), axis=-1)
    weights = jnp.where(allowed, jnp.exp(scores - final_peak[..., None]), 0.0)
    final_total = jnp.sum(weights, axis=-1)
    mixed_latent = jnp.einsum(
        "hqk,kl->hql", weights.astype(jnp.bfloat16), piece, preferred_element_type=jnp.float32
    )
    final_mixed = jnp.einsum(
        "hql,lhd->hqd",
        mixed_latent,
        up_values.astype(jnp.float32),
        precision=highest_precision,
    )
    attention_out = (
        (final_mixed / final_total[..., None])
        .transpose(1, 0, 2)
        .reshape(length, heads_mla * DH)
        .astype(jnp.bfloat16)
    )
    return (stream_out, attention_out)


def solution(mesh):
    in_specs = (
        P(None, "ctx", "head"),
        P("ctx", "head"),
        P("ctx", "head"),
        P(None, None, "head"),
        P("head", None),
        P("ctx", None),
        P(),
        P(),
        P(),
        P(None, "head"),
        P(None, None, "head"),
    )
    out_specs = (P("ctx", None), P("ctx", "head"))
    return jax.shard_map(
        per_device, mesh=mesh, in_specs=in_specs, out_specs=out_specs, check_vma=False
    )
```

```python
import math

import jax
import jax.numpy as jnp
from jax import lax
from jax.sharding import PartitionSpec as P
from jax.experimental import pallas as pl
from jax.experimental.pallas import tpu as pltpu

DK = 128
CONV = 4
DH = 128


eps_norm = 1e-06
highest_precision = lax.Precision.HIGHEST


def passed_along(block, axis, distance):
    devices = range(lax.axis_size(axis))
    route = [(i - distance, i) for i in devices if i - distance in devices]
    return lax.ppermute(block, axis, route)


def stream_after_head_sum(partial, residual):
    size = lax.axis_size("head")
    core = lax.axis_index("head") % 2
    half = partial.shape[0] // 2
    pair_route = [(i, i ^ 1) for i in range(size)]
    chip_route = [(i, i ^ 2) for i in range(size)]
    kept = lax.dynamic_slice_in_dim(partial, core * half, half)
    given = lax.dynamic_slice_in_dim(partial, (1 - core) * half, half)
    pair_sum = kept + lax.ppermute(given, "head", pair_route)
    total = pair_sum + lax.ppermute(pair_sum, "head", chip_route)
    my_rows = lax.dynamic_slice_in_dim(residual, core * half, half)
    stream_half = (my_rows.astype(jnp.float32) + total).astype(jnp.bfloat16)
    other_half = lax.ppermute(stream_half, "head", pair_route)
    return jnp.where(
        core == 0,
        jnp.concatenate([stream_half, other_half], axis=0),
        jnp.concatenate([other_half, stream_half], axis=0),
    )


def gather_kernel(block_ref, out_ref, send_sems, recv_sems, forward_sems):
    me = lax.axis_index("ctx")
    head = lax.axis_index("head")
    core = head % 2
    sibling = head + 1 - 2 * core
    count = out_ref.shape[0]
    out_ref[me] = block_ref[...]

    def outgoing(peer):
        return pltpu.make_async_remote_copy(
            src_ref=block_ref,
            dst_ref=out_ref.at[me],
            send_sem=send_sems.at[peer],
            recv_sem=recv_sems.at[me],
            device_id={"ctx": peer, "head": head},
            device_id_type=pl.DeviceIdType.MESH,
        )

    def forwarded(origin):
        return pltpu.make_async_remote_copy(
            src_ref=out_ref.at[origin],
            dst_ref=out_ref.at[origin],
            send_sem=forward_sems.at[origin],
            recv_sem=recv_sems.at[origin],
            device_id={"ctx": me, "head": sibling},
            device_id_type=pl.DeviceIdType.MESH,
        )

    @pl.loop(me + 1, count)
    def _(peer):
        @pl.when((peer + me) % 2 == core)
        def _():
            outgoing(peer).start()

    @pl.loop(me + 1, count)
    def _(peer):
        out_ref[peer] = jnp.zeros(block_ref.shape, block_ref.dtype)

    @pl.loop(0, me)
    def _(origin):
        @pl.when((origin + me) % 2 == core)
        def _():
            forwarded(origin).wait_recv()
            forwarded(origin).start()

    @pl.loop(0, me)
    def _(origin):
        @pl.when((origin + me) % 2 != core)
        def _():
            forwarded(origin).wait_recv()

    @pl.loop(me + 1, count)
    def _(peer):
        @pl.when((peer + me) % 2 == core)
        def _():
            outgoing(peer).wait_send()

    @pl.loop(0, me)
    def _(origin):
        @pl.when((origin + me) % 2 == core)
        def _():
            forwarded(origin).wait_send()


def gathered_earlier(block):
    count = lax.axis_size("ctx")
    rows, width = block.shape
    stacked = pl.pallas_call(
        gather_kernel,
        out_shape=jax.ShapeDtypeStruct((count, rows, width), block.dtype),
        in_specs=[pl.BlockSpec(memory_space=pltpu.VMEM)],
        out_specs=pl.BlockSpec(memory_space=pltpu.VMEM),
        scratch_shapes=[pltpu.SemaphoreType.DMA((count,))] * 3,
        compiler_params=pltpu.CompilerParams(has_side_effects=True),
    )(block)
    return stacked.reshape(count * rows, width)


def rounded(values):
    return lax.optimization_barrier(values.astype(jnp.bfloat16))


def unit_heads(activated):
    grouped = activated.reshape(activated.shape[0], -1, DK)
    scaled = grouped * lax.rsqrt(jnp.sum(grouped * grouped, axis=-1, keepdims=True) + eps_norm)
    return scaled.reshape(activated.shape)


def prepare(stream, norm_gain, latent_weight, latent_gain):
    widened = stream.astype(jnp.float32)
    normed = (
        widened
        * lax.rsqrt(jnp.mean(widened * widened, axis=-1, keepdims=True) + eps_norm)
        * norm_gain
    ).astype(jnp.bfloat16)
    latent_pre = jnp.dot(normed, latent_weight, preferred_element_type=jnp.float32)
    latent = (
        latent_pre
        * lax.rsqrt(jnp.mean(latent_pre * latent_pre, axis=-1, keepdims=True) + eps_norm)
        * latent_gain
    ).astype(jnp.bfloat16)
    return (normed, latent)


def span_layout(values, span_rows):
    length, channel_count = values.shape
    return values.reshape(length // span_rows, span_rows, channel_count // DK, DK).transpose(
        0, 2, 1, 3
    )


def matmul_heads(left, right):
    return jnp.einsum("hij,hjk->hik", left, right, precision=highest_precision)


def matmul_batched(left, right):
    return jnp.einsum("...ij,...jk->...ik", left, right, precision=highest_precision)


def unit_lower_inverse(system):
    size = system.shape[-1]
    rows = jnp.arange(size)[:, None]
    cols = jnp.arange(size)[None, :]
    inverse = jnp.broadcast_to(jnp.eye(size, dtype=system.dtype), system.shape)
    width = 1
    while width < size:
        below = (rows // (2 * width) == cols // (2 * width)) & (rows // width != cols // width)
        off_block = jnp.where(below, system, 0.0)
        correction = matmul_batched(matmul_batched(inverse, off_block), inverse)
        inverse = inverse - lax.optimization_barrier(correction)
        width *= 2
    return inverse


def delta_rule(kda_query, kda_key, kda_value, gate_log, beta):
    span_rows = 32
    length, channel_count = gate_log.shape
    heads = channel_count // DK
    queries = span_layout(kda_query.astype(jnp.float32), span_rows)
    keys_unit = span_layout(kda_key.astype(jnp.float32), span_rows)
    values_new = span_layout(kda_value.astype(jnp.float32), span_rows)
    inclusive_ones = jnp.tril(jnp.ones((span_rows, span_rows), jnp.float32))
    cumulative = jnp.einsum(
        "ts,nhsc->nhtc", inclusive_ones, span_layout(gate_log, span_rows), precision=highest_precision
    )
    rates = beta.reshape(length // span_rows, span_rows, heads).transpose(0, 2, 1)[..., None]
    growth = jnp.exp(cumulative)
    final_log = cumulative[:, :, -1:, :]
    keys_grown = keys_unit * growth
    keys_shrunk = keys_unit * jnp.exp(-cumulative)
    queries_grown = queries * growth
    keys_final = keys_unit * jnp.exp(final_log - cumulative)
    strict = jnp.tril(jnp.ones((span_rows, span_rows), jnp.float32), -1)
    inclusive = jnp.tril(jnp.ones((span_rows, span_rows), jnp.float32))
    coupling = (
        jnp.einsum("nhtc,nhsc->nhts", keys_grown, keys_shrunk, precision=highest_precision)
        * jnp.swapaxes(rates, -1, -2)
        * strict
    )
    system = coupling + jnp.eye(span_rows, dtype=jnp.float32)
    solved = matmul_batched(
        unit_lower_inverse(system), jnp.concatenate([values_new, keys_grown], axis=-1)
    )
    fresh = solved[..., :DK] * rates
    carried = solved[..., DK:] * rates
    eye_key = jnp.eye(DK, dtype=jnp.float32)
    transition = jnp.exp(final_log[:, :, 0, :])[..., :, None] * eye_key - jnp.einsum(
        "nhsk,nhsv->nhkv", keys_final, carried, precision=highest_precision
    )
    offset = jnp.einsum("nhsk,nhsv->nhkv", keys_final, fresh, precision=highest_precision)
    mixing = (
        jnp.einsum("nhtc,nhsc->nhts", queries_grown, keys_shrunk, precision=highest_precision)
        * inclusive
    )

    moves, shifts = transition, offset
    while moves.shape[0] > 1:
        later_moves, earlier_moves = moves[1::2], moves[0::2]
        shifts = matmul_batched(later_moves, shifts[0::2]) + shifts[1::2]
        moves = matmul_batched(later_moves, earlier_moves)
    device_move, device_shift = moves[0], shifts[0]
    return (device_move, device_shift, (transition, offset, fresh, carried, queries_grown, mixing))


def emit_step(carried_parts, span_parts):
    recurrent_state, accumulated_move = carried_parts
    span_move, span_shift, fresh_state_term, carried_state_term, query_term, mixing_part = (
        span_parts
    )
    state_update = fresh_state_term - jnp.einsum(
        "orm,omj->orj", carried_state_term, recurrent_state, precision=highest_precision
    )
    produced_output = jnp.einsum(
        "fmb,fbi->fmi", query_term, recurrent_state, precision=highest_precision
    ) + jnp.einsum("hts,hsv->htv", mixing_part, state_update, precision=highest_precision)
    start_weight = query_term - jnp.einsum(
        "hts,hsv->htv", mixing_part, carried_state_term, precision=highest_precision
    )
    start_query = matmul_heads(start_weight, accumulated_move)
    next_parts = (
        matmul_heads(span_move, recurrent_state) + span_shift,
        matmul_heads(span_move, accumulated_move),
    )
    return (next_parts, (produced_output, start_query))


def token_major(span_values):
    stacked = jnp.stack(span_values)
    block_count, heads, span_rows, _ = stacked.shape
    return stacked.transpose(1, 0, 2, 3).reshape(heads, block_count * span_rows, DK)


def finish_spans(start_state, local_outputs, start_queries):
    outputs = local_outputs + matmul_heads(start_queries, start_state)
    heads, length, _ = outputs.shape
    return outputs.transpose(1, 0, 2).reshape(length, heads * DK).astype(jnp.bfloat16)


def per_device(
    kda_inputs,
    gate_log,
    beta,
    conv_weight,
    kda_out_weight,
    residual,
    norm_gain,
    latent_weight,
    latent_gain,
    query_weight,
    up_weight,
):
    length = residual.shape[0]
    edge_rows = kda_inputs[:, length - (CONV - 1) :, :]
    earlier_rows = passed_along(edge_rows, "ctx", 1)
    extended = jnp.concatenate([earlier_rows, kda_inputs], axis=1).astype(jnp.float32)
    running = jnp.zeros(kda_inputs.shape, jnp.float32)
    for tap_index in range(CONV):
        running = (
            running
            + conv_weight[:, tap_index, None, :] * extended[:, tap_index : tap_index + length, :]
        )
    activated = jax.nn.silu(running)
    kda_query = rounded(unit_heads(activated[0]) * DK ** (-0.5))
    kda_key = rounded(unit_heads(activated[1]))
    kda_value = rounded(activated[2])
    device_move, device_shift, span_data = delta_rule(kda_query, kda_key, kda_value, gate_log, beta)
    heads = device_move.shape[0]
    span_count = span_data[0].shape[0]
    emit_carry = (
        jnp.zeros((heads, DK, DK), jnp.float32),
        jnp.broadcast_to(jnp.eye(DK, dtype=jnp.float32), (heads, DK, DK)),
    )
    produced = []

    def run_emit(emit_carry):
        span_index = len(produced)
        emit_carry, emitted = emit_step(emit_carry, tuple(part[span_index] for part in span_data))
        produced.append(emitted)
        return emit_carry

    ctx_size = lax.axis_size("ctx")
    move, shift = device_move, device_shift
    distance = 1
    while distance < ctx_size:
        if 2 * distance < ctx_size:
            sent = jnp.stack([move, shift]).astype(jnp.bfloat16)
            both_in = passed_along(sent, "ctx", distance).astype(jnp.float32)
            next_shift = matmul_heads(move, both_in[1]) + shift
            next_move = matmul_heads(move, both_in[0])
        else:
            next_shift = matmul_heads(move, passed_along(shift, "ctx", distance)) + shift
            next_move = move
        if len(produced) < span_count:
            emit_carry = run_emit(emit_carry)
            next_shift, next_move, emit_carry = lax.optimization_barrier(
                (next_shift, next_move, emit_carry)
            )
        move, shift = next_move, next_shift
        distance *= 2
    while len(produced) < span_count:
        emit_carry = run_emit(emit_carry)
    local_outputs = token_major([emitted[0] for emitted in produced])
    start_queries = token_major([emitted[1] for emitted in produced])
    start_state = passed_along(shift, "ctx", 1)
    kda_core = finish_spans(start_state, local_outputs, start_queries)
    partial_proj = jnp.dot(kda_core, kda_out_weight, preferred_element_type=jnp.float32)
    stream_out = stream_after_head_sum(partial_proj, residual)
    normed, latent = prepare(stream_out, norm_gain, latent_weight, latent_gain)
    mla_query = jnp.dot(normed, query_weight, preferred_element_type=jnp.float32).astype(
        jnp.bfloat16
    )
    query_heads = mla_query.reshape(length, -1, DH)
    heads_mla = query_heads.shape[1]
    flat_up = up_weight.reshape(up_weight.shape[0], -1)
    my_first = lax.axis_index("ctx") * length
    query_positions = my_first + jnp.arange(length, dtype=jnp.int32)
    piece = gathered_earlier(latent)
    piece_rows = piece.shape[0]
    paired = (
        jnp.dot(piece, flat_up, preferred_element_type=jnp.float32)
        .astype(jnp.bfloat16)
        .reshape(piece_rows, 2, heads_mla, DH)
    )
    scores = jnp.einsum(
        "qhd,khd->hqk", query_heads, paired[:, 0], preferred_element_type=jnp.float32
    ) * DH ** (-0.5)
    key_positions = jnp.arange(piece_rows, dtype=jnp.int32)
    allowed = key_positions[None, :] <= query_positions[:, None]
    final_peak = jnp.max(jnp.where(allowed, scores, -1e30), axis=-1)
    weights = jnp.where(allowed, jnp.exp(scores - final_peak[..., None]), 0.0)
    final_total = jnp.sum(weights, axis=-1)
    final_mixed = jnp.einsum(
        "hqk,khd->hqd",
        weights.astype(jnp.bfloat16),
        paired[:, 1],
        preferred_element_type=jnp.float32,
    )
    attention_out = (
        (final_mixed / final_total[..., None])
        .transpose(1, 0, 2)
        .reshape(length, heads_mla * DH)
        .astype(jnp.bfloat16)
    )
    return (stream_out, attention_out)


def solution(mesh):
    in_specs = (
        P(None, "ctx", "head"),
        P("ctx", "head"),
        P("ctx", "head"),
        P(None, None, "head"),
        P("head", None),
        P("ctx", None),
        P(),
        P(),
        P(),
        P(None, "head"),
        P(None, None, "head"),
    )
    out_specs = (P("ctx", None), P("ctx", "head"))
    return jax.shard_map(
        per_device, mesh=mesh, in_specs=in_specs, out_specs=out_specs, check_vma=False
    )
```

```python
import math

import jax
import jax.numpy as jnp
from jax import lax
from jax.sharding import PartitionSpec as P
from jax.experimental import pallas as pl
from jax.experimental.pallas import tpu as pltpu

DK = 128
CONV = 4
DH = 128


eps_norm = 1e-06
highest_precision = lax.Precision.HIGHEST


def passed_along(block, axis, distance):
    devices = range(lax.axis_size(axis))
    route = [(i - distance, i) for i in devices if i - distance in devices]
    return lax.ppermute(block, axis, route)


def stream_after_head_sum(partial, residual):
    size = lax.axis_size("head")
    core = lax.axis_index("head") % 2
    half = partial.shape[0] // 2
    pair_route = [(i, i ^ 1) for i in range(size)]
    chip_route = [(i, i ^ 2) for i in range(size)]
    kept = lax.dynamic_slice_in_dim(partial, core * half, half)
    given = lax.dynamic_slice_in_dim(partial, (1 - core) * half, half)
    pair_sum = kept + lax.ppermute(given, "head", pair_route)
    pair_rounded = lax.optimization_barrier(pair_sum.astype(jnp.bfloat16))
    partner_rounded = lax.ppermute(pair_rounded, "head", chip_route)
    total = pair_rounded.astype(jnp.float32) + partner_rounded.astype(jnp.float32)
    my_rows = lax.dynamic_slice_in_dim(residual, core * half, half)
    stream_half = (my_rows.astype(jnp.float32) + total).astype(jnp.bfloat16)
    other_half = lax.ppermute(stream_half, "head", pair_route)
    return jnp.where(
        core == 0,
        jnp.concatenate([stream_half, other_half], axis=0),
        jnp.concatenate([other_half, stream_half], axis=0),
    )


def gather_kernel(block_ref, out_ref, send_sems, recv_sems, forward_sems):
    me = lax.axis_index("ctx")
    head = lax.axis_index("head")
    core = head % 2
    sibling = head + 1 - 2 * core
    count = out_ref.shape[0]
    out_ref[me] = block_ref[...]

    def outgoing(peer):
        return pltpu.make_async_remote_copy(
            src_ref=block_ref,
            dst_ref=out_ref.at[me],
            send_sem=send_sems.at[peer],
            recv_sem=recv_sems.at[me],
            device_id={"ctx": peer, "head": head},
            device_id_type=pl.DeviceIdType.MESH,
        )

    def forwarded(origin):
        return pltpu.make_async_remote_copy(
            src_ref=out_ref.at[origin],
            dst_ref=out_ref.at[origin],
            send_sem=forward_sems.at[origin],
            recv_sem=recv_sems.at[origin],
            device_id={"ctx": me, "head": sibling},
            device_id_type=pl.DeviceIdType.MESH,
        )

    @pl.loop(me + 1, count)
    def _(peer):
        @pl.when((peer + me) % 2 == core)
        def _():
            outgoing(peer).start()

    @pl.loop(me + 1, count)
    def _(peer):
        out_ref[peer] = jnp.zeros(block_ref.shape, block_ref.dtype)

    @pl.loop(0, me)
    def _(origin):
        @pl.when((origin + me) % 2 == core)
        def _():
            forwarded(origin).wait_recv()
            forwarded(origin).start()

    @pl.loop(0, me)
    def _(origin):
        @pl.when((origin + me) % 2 != core)
        def _():
            forwarded(origin).wait_recv()

    @pl.loop(me + 1, count)
    def _(peer):
        @pl.when((peer + me) % 2 == core)
        def _():
            outgoing(peer).wait_send()

    @pl.loop(0, me)
    def _(origin):
        @pl.when((origin + me) % 2 == core)
        def _():
            forwarded(origin).wait_send()


def gathered_earlier(block):
    count = lax.axis_size("ctx")
    rows, width = block.shape
    stacked = pl.pallas_call(
        gather_kernel,
        out_shape=jax.ShapeDtypeStruct((count, rows, width), block.dtype),
        in_specs=[pl.BlockSpec(memory_space=pltpu.VMEM)],
        out_specs=pl.BlockSpec(memory_space=pltpu.VMEM),
        scratch_shapes=[pltpu.SemaphoreType.DMA((count,))] * 3,
        compiler_params=pltpu.CompilerParams(has_side_effects=True),
    )(block)
    return stacked.reshape(count * rows, width)


def rounded(values):
    return lax.optimization_barrier(values.astype(jnp.bfloat16))


def unit_heads(activated):
    grouped = activated.reshape(activated.shape[0], -1, DK)
    scaled = grouped * lax.rsqrt(jnp.sum(grouped * grouped, axis=-1, keepdims=True) + eps_norm)
    return scaled.reshape(activated.shape)


def prepare(stream, norm_gain, latent_weight, latent_gain):
    widened = stream.astype(jnp.float32)
    normed = (
        widened
        * lax.rsqrt(jnp.mean(widened * widened, axis=-1, keepdims=True) + eps_norm)
        * norm_gain
    ).astype(jnp.bfloat16)
    latent_pre = jnp.dot(normed, latent_weight, preferred_element_type=jnp.float32)
    latent = (
        latent_pre
        * lax.rsqrt(jnp.mean(latent_pre * latent_pre, axis=-1, keepdims=True) + eps_norm)
        * latent_gain
    ).astype(jnp.bfloat16)
    return (normed, latent)


def span_layout(values, span_rows):
    length, channel_count = values.shape
    return values.reshape(length // span_rows, span_rows, channel_count // DK, DK).transpose(
        0, 2, 1, 3
    )


def matmul_heads(left, right):
    return jnp.einsum("hij,hjk->hik", left, right, precision=highest_precision)


def matmul_batched(left, right):
    return jnp.einsum("...ij,...jk->...ik", left, right, precision=highest_precision)


def unit_lower_inverse(system):
    size = system.shape[-1]
    rows = jnp.arange(size)[:, None]
    cols = jnp.arange(size)[None, :]
    inverse = jnp.broadcast_to(jnp.eye(size, dtype=system.dtype), system.shape)
    width = 1
    while width < size:
        below = (rows // (2 * width) == cols // (2 * width)) & (rows // width != cols // width)
        off_block = jnp.where(below, system, 0.0)
        correction = matmul_batched(matmul_batched(inverse, off_block), inverse)
        inverse = inverse - lax.optimization_barrier(correction)
        width *= 2
    return inverse


def delta_rule(kda_query, kda_key, kda_value, gate_log, beta):
    span_rows = 32
    length, channel_count = gate_log.shape
    heads = channel_count // DK
    queries = span_layout(kda_query.astype(jnp.float32), span_rows)
    keys_unit = span_layout(kda_key.astype(jnp.float32), span_rows)
    values_new = span_layout(kda_value.astype(jnp.float32), span_rows)
    inclusive_ones = jnp.tril(jnp.ones((span_rows, span_rows), jnp.float32))
    cumulative = jnp.einsum(
        "ts,nhsc->nhtc", inclusive_ones, span_layout(gate_log, span_rows), precision=highest_precision
    )
    rates = beta.reshape(length // span_rows, span_rows, heads).transpose(0, 2, 1)[..., None]
    growth = jnp.exp(cumulative)
    final_log = cumulative[:, :, -1:, :]
    keys_grown = keys_unit * growth
    keys_shrunk = keys_unit * jnp.exp(-cumulative)
    queries_grown = queries * growth
    keys_final = keys_unit * jnp.exp(final_log - cumulative)
    strict = jnp.tril(jnp.ones((span_rows, span_rows), jnp.float32), -1)
    inclusive = jnp.tril(jnp.ones((span_rows, span_rows), jnp.float32))
    coupling = (
        jnp.einsum("nhtc,nhsc->nhts", keys_grown, keys_shrunk, precision=highest_precision)
        * jnp.swapaxes(rates, -1, -2)
        * strict
    )
    system = coupling + jnp.eye(span_rows, dtype=jnp.float32)
    solved = matmul_batched(
        unit_lower_inverse(system), jnp.concatenate([values_new, keys_grown], axis=-1)
    )
    fresh = solved[..., :DK] * rates
    carried = solved[..., DK:] * rates
    eye_key = jnp.eye(DK, dtype=jnp.float32)
    transition = jnp.exp(final_log[:, :, 0, :])[..., :, None] * eye_key - jnp.einsum(
        "nhsk,nhsv->nhkv", keys_final, carried, precision=highest_precision
    )
    offset = jnp.einsum("nhsk,nhsv->nhkv", keys_final, fresh, precision=highest_precision)
    mixing = (
        jnp.einsum("nhtc,nhsc->nhts", queries_grown, keys_shrunk, precision=highest_precision)
        * inclusive
    )

    moves, shifts = transition, offset
    while moves.shape[0] > 1:
        later_moves, earlier_moves = moves[1::2], moves[0::2]
        shifts = matmul_batched(later_moves, shifts[0::2]) + shifts[1::2]
        moves = matmul_batched(later_moves, earlier_moves)
    device_move, device_shift = moves[0], shifts[0]
    return (device_move, device_shift, (transition, offset, fresh, carried, queries_grown, mixing))


def emit_step(carried_parts, span_parts):
    recurrent_state, accumulated_move = carried_parts
    span_move, span_shift, fresh_state_term, carried_state_term, query_term, mixing_part = (
        span_parts
    )
    state_update = fresh_state_term - jnp.einsum(
        "orm,omj->orj", carried_state_term, recurrent_state, precision=highest_precision
    )
    produced_output = jnp.einsum(
        "fmb,fbi->fmi", query_term, recurrent_state, precision=highest_precision
    ) + jnp.einsum("hts,hsv->htv", mixing_part, state_update, precision=highest_precision)
    start_weight = query_term - jnp.einsum(
        "hts,hsv->htv", mixing_part, carried_state_term, precision=highest_precision
    )
    start_query = matmul_heads(start_weight, accumulated_move)
    next_parts = (
        matmul_heads(span_move, recurrent_state) + span_shift,
        matmul_heads(span_move, accumulated_move),
    )
    return (next_parts, (produced_output, start_query))


def token_major(span_values):
    stacked = jnp.stack(span_values)
    block_count, heads, span_rows, _ = stacked.shape
    return stacked.transpose(1, 0, 2, 3).reshape(heads, block_count * span_rows, DK)


def finish_spans(start_state, local_outputs, start_queries):
    outputs = local_outputs + matmul_heads(start_queries, start_state)
    heads, length, _ = outputs.shape
    return outputs.transpose(1, 0, 2).reshape(length, heads * DK).astype(jnp.bfloat16)


def per_device(
    kda_inputs,
    gate_log,
    beta,
    conv_weight,
    kda_out_weight,
    residual,
    norm_gain,
    latent_weight,
    latent_gain,
    query_weight,
    up_weight,
):
    length = residual.shape[0]
    edge_rows = kda_inputs[:, length - (CONV - 1) :, :]
    earlier_rows = passed_along(edge_rows, "ctx", 1)
    extended = jnp.concatenate([earlier_rows, kda_inputs], axis=1).astype(jnp.float32)
    running = jnp.zeros(kda_inputs.shape, jnp.float32)
    for tap_index in range(CONV):
        running = (
            running
            + conv_weight[:, tap_index, None, :] * extended[:, tap_index : tap_index + length, :]
        )
    activated = jax.nn.silu(running)
    kda_query = rounded(unit_heads(activated[0]) * DK ** (-0.5))
    kda_key = rounded(unit_heads(activated[1]))
    kda_value = rounded(activated[2])
    device_move, device_shift, span_data = delta_rule(kda_query, kda_key, kda_value, gate_log, beta)
    heads = device_move.shape[0]
    span_count = span_data[0].shape[0]
    emit_carry = (
        jnp.zeros((heads, DK, DK), jnp.float32),
        jnp.broadcast_to(jnp.eye(DK, dtype=jnp.float32), (heads, DK, DK)),
    )
    produced = []

    def run_emit(emit_carry):
        span_index = len(produced)
        emit_carry, emitted = emit_step(emit_carry, tuple(part[span_index] for part in span_data))
        produced.append(emitted)
        return emit_carry

    ctx_size = lax.axis_size("ctx")
    move, shift = device_move, device_shift
    distance = 1
    while distance < ctx_size:
        if 2 * distance < ctx_size:
            sent = jnp.stack([move, shift]).astype(jnp.bfloat16)
            both_in = passed_along(sent, "ctx", distance).astype(jnp.float32)
            next_shift = matmul_heads(move, both_in[1]) + shift
            next_move = matmul_heads(move, both_in[0])
        else:
            shift_in = passed_along(shift.astype(jnp.bfloat16), "ctx", distance)
            next_shift = matmul_heads(move, shift_in.astype(jnp.float32)) + shift
            next_move = move
        if len(produced) < span_count:
            emit_carry = run_emit(emit_carry)
            next_shift, next_move, emit_carry = lax.optimization_barrier(
                (next_shift, next_move, emit_carry)
            )
        move, shift = next_move, next_shift
        distance *= 2
    while len(produced) < span_count:
        emit_carry = run_emit(emit_carry)
    local_outputs = token_major([emitted[0] for emitted in produced])
    start_queries = token_major([emitted[1] for emitted in produced])
    start_state = passed_along(shift.astype(jnp.bfloat16), "ctx", 1).astype(jnp.float32)
    kda_core = finish_spans(start_state, local_outputs, start_queries)
    partial_proj = jnp.dot(kda_core, kda_out_weight, preferred_element_type=jnp.float32)
    stream_out = stream_after_head_sum(partial_proj, residual)
    normed, latent = prepare(stream_out, norm_gain, latent_weight, latent_gain)
    mla_query = jnp.dot(normed, query_weight, preferred_element_type=jnp.float32).astype(
        jnp.bfloat16
    )
    query_heads = mla_query.reshape(length, -1, DH)
    heads_mla = query_heads.shape[1]
    flat_up = up_weight.reshape(up_weight.shape[0], -1)
    my_first = lax.axis_index("ctx") * length
    query_positions = my_first + jnp.arange(length, dtype=jnp.int32)
    piece = gathered_earlier(latent)
    piece_rows = piece.shape[0]
    paired = (
        jnp.dot(piece, flat_up, preferred_element_type=jnp.float32)
        .astype(jnp.bfloat16)
        .reshape(piece_rows, 2, heads_mla, DH)
    )
    scores = jnp.einsum(
        "qhd,khd->hqk", query_heads, paired[:, 0], preferred_element_type=jnp.float32
    ) * DH ** (-0.5)
    key_positions = jnp.arange(piece_rows, dtype=jnp.int32)
    allowed = key_positions[None, :] <= query_positions[:, None]
    final_peak = jnp.max(jnp.where(allowed, scores, -1e30), axis=-1)
    weights = jnp.where(allowed, jnp.exp(scores - final_peak[..., None]), 0.0)
    final_total = jnp.sum(weights, axis=-1)
    final_mixed = jnp.einsum(
        "hqk,khd->hqd",
        weights.astype(jnp.bfloat16),
        paired[:, 1],
        preferred_element_type=jnp.float32,
    )
    attention_out = (
        (final_mixed / final_total[..., None])
        .transpose(1, 0, 2)
        .reshape(length, heads_mla * DH)
        .astype(jnp.bfloat16)
    )
    return (stream_out, attention_out)


def solution(mesh):
    in_specs = (
        P(None, "ctx", "head"),
        P("ctx", "head"),
        P("ctx", "head"),
        P(None, None, "head"),
        P("head", None),
        P("ctx", None),
        P(),
        P(),
        P(),
        P(None, "head"),
        P(None, None, "head"),
    )
    out_specs = (P("ctx", None), P("ctx", "head"))
    return jax.shard_map(
        per_device, mesh=mesh, in_specs=in_specs, out_specs=out_specs, check_vma=False
    )
```

```python
import math

import jax
import jax.numpy as jnp
from jax import lax
from jax.sharding import PartitionSpec as P
from jax.experimental import pallas as pl
from jax.experimental.pallas import tpu as pltpu

DK = 128
CONV = 4
DH = 128


eps_norm = 1e-06
highest_precision = lax.Precision.HIGHEST


def passed_along(block, axis, distance):
    devices = range(lax.axis_size(axis))
    route = [(i - distance, i) for i in devices if i - distance in devices]
    return lax.ppermute(block, axis, route)


def stream_after_head_sum(partial, residual):
    size = lax.axis_size("head")
    core = lax.axis_index("head") % 2
    half = partial.shape[0] // 2
    pair_route = [(i, i ^ 1) for i in range(size)]
    chip_route = [(i, i ^ 2) for i in range(size)]
    kept = lax.dynamic_slice_in_dim(partial, core * half, half)
    given = lax.dynamic_slice_in_dim(partial, (1 - core) * half, half)
    pair_sum = kept + lax.ppermute(given, "head", pair_route)
    pair_rounded = lax.optimization_barrier(pair_sum.astype(jnp.bfloat16))
    partner_rounded = lax.ppermute(pair_rounded, "head", chip_route)
    total = pair_rounded.astype(jnp.float32) + partner_rounded.astype(jnp.float32)
    my_rows = lax.dynamic_slice_in_dim(residual, core * half, half)
    stream_half = (my_rows.astype(jnp.float32) + total).astype(jnp.bfloat16)
    other_half = lax.ppermute(stream_half, "head", pair_route)
    return jnp.where(
        core == 0,
        jnp.concatenate([stream_half, other_half], axis=0),
        jnp.concatenate([other_half, stream_half], axis=0),
    )


def gather_kernel(block_ref, out_ref, send_sems, recv_sems, forward_sems):
    me = lax.axis_index("ctx")
    head = lax.axis_index("head")
    core = head % 2
    sibling = head + 1 - 2 * core
    count = out_ref.shape[0]
    out_ref[me] = block_ref[...]

    def outgoing(peer):
        crossing = ((peer // 4) % 2 + (me // 4) % 2) % 2
        swap = crossing * (((peer + me) // 2) % 2)
        target_head = ((head // 2 + swap) % 2) * 2 + core
        return pltpu.make_async_remote_copy(
            src_ref=block_ref,
            dst_ref=out_ref.at[me],
            send_sem=send_sems.at[peer],
            recv_sem=recv_sems.at[me],
            device_id={"ctx": peer, "head": target_head},
            device_id_type=pl.DeviceIdType.MESH,
        )

    def forwarded(origin):
        return pltpu.make_async_remote_copy(
            src_ref=out_ref.at[origin],
            dst_ref=out_ref.at[origin],
            send_sem=forward_sems.at[origin],
            recv_sem=recv_sems.at[origin],
            device_id={"ctx": me, "head": sibling},
            device_id_type=pl.DeviceIdType.MESH,
        )

    @pl.loop(me + 1, count)
    def _(peer):
        @pl.when((peer + me) % 2 == core)
        def _():
            outgoing(peer).start()

    @pl.loop(me + 1, count)
    def _(peer):
        out_ref[peer] = jnp.zeros(block_ref.shape, block_ref.dtype)

    @pl.loop(0, me)
    def _(origin):
        @pl.when((origin + me) % 2 == core)
        def _():
            forwarded(origin).wait_recv()
            forwarded(origin).start()

    @pl.loop(0, me)
    def _(origin):
        @pl.when((origin + me) % 2 != core)
        def _():
            forwarded(origin).wait_recv()

    @pl.loop(me + 1, count)
    def _(peer):
        @pl.when((peer + me) % 2 == core)
        def _():
            outgoing(peer).wait_send()

    @pl.loop(0, me)
    def _(origin):
        @pl.when((origin + me) % 2 == core)
        def _():
            forwarded(origin).wait_send()


def gathered_earlier(block):
    count = lax.axis_size("ctx")
    rows, width = block.shape
    stacked = pl.pallas_call(
        gather_kernel,
        out_shape=jax.ShapeDtypeStruct((count, rows, width), block.dtype),
        in_specs=[pl.BlockSpec(memory_space=pltpu.VMEM)],
        out_specs=pl.BlockSpec(memory_space=pltpu.VMEM),
        scratch_shapes=[pltpu.SemaphoreType.DMA((count,))] * 3,
        compiler_params=pltpu.CompilerParams(has_side_effects=True),
    )(block)
    return stacked.reshape(count * rows, width)


def rounded(values):
    return lax.optimization_barrier(values.astype(jnp.bfloat16))


def unit_heads(activated):
    grouped = activated.reshape(activated.shape[0], -1, DK)
    scaled = grouped * lax.rsqrt(jnp.sum(grouped * grouped, axis=-1, keepdims=True) + eps_norm)
    return scaled.reshape(activated.shape)


def prepare(stream, norm_gain, latent_weight, latent_gain):
    widened = stream.astype(jnp.float32)
    normed = (
        widened
        * lax.rsqrt(jnp.mean(widened * widened, axis=-1, keepdims=True) + eps_norm)
        * norm_gain
    ).astype(jnp.bfloat16)
    latent_pre = jnp.dot(normed, latent_weight, preferred_element_type=jnp.float32)
    latent = (
        latent_pre
        * lax.rsqrt(jnp.mean(latent_pre * latent_pre, axis=-1, keepdims=True) + eps_norm)
        * latent_gain
    ).astype(jnp.bfloat16)
    return (normed, latent)


def span_layout(values, span_rows):
    length, channel_count = values.shape
    return values.reshape(length // span_rows, span_rows, channel_count // DK, DK).transpose(
        0, 2, 1, 3
    )


def matmul_heads(left, right):
    return jnp.einsum("hij,hjk->hik", left, right, precision=highest_precision)


def matmul_batched(left, right):
    return jnp.einsum("...ij,...jk->...ik", left, right, precision=highest_precision)


def unit_lower_inverse(system):
    size = system.shape[-1]
    rows = jnp.arange(size)[:, None]
    cols = jnp.arange(size)[None, :]
    inverse = jnp.broadcast_to(jnp.eye(size, dtype=system.dtype), system.shape)
    width = 1
    while width < size:
        below = (rows // (2 * width) == cols // (2 * width)) & (rows // width != cols // width)
        off_block = jnp.where(below, system, 0.0)
        correction = matmul_batched(matmul_batched(inverse, off_block), inverse)
        inverse = inverse - lax.optimization_barrier(correction)
        width *= 2
    return inverse


def delta_rule(kda_query, kda_key, kda_value, gate_log, beta):
    span_rows = 32
    length, channel_count = gate_log.shape
    heads = channel_count // DK
    queries = span_layout(kda_query.astype(jnp.float32), span_rows)
    keys_unit = span_layout(kda_key.astype(jnp.float32), span_rows)
    values_new = span_layout(kda_value.astype(jnp.float32), span_rows)
    inclusive_ones = jnp.tril(jnp.ones((span_rows, span_rows), jnp.float32))
    cumulative = jnp.einsum(
        "ts,nhsc->nhtc", inclusive_ones, span_layout(gate_log, span_rows), precision=highest_precision
    )
    rates = beta.reshape(length // span_rows, span_rows, heads).transpose(0, 2, 1)[..., None]
    growth = jnp.exp(cumulative)
    final_log = cumulative[:, :, -1:, :]
    keys_grown = keys_unit * growth
    keys_shrunk = keys_unit * jnp.exp(-cumulative)
    queries_grown = queries * growth
    keys_final = keys_unit * jnp.exp(final_log - cumulative)
    strict = jnp.tril(jnp.ones((span_rows, span_rows), jnp.float32), -1)
    inclusive = jnp.tril(jnp.ones((span_rows, span_rows), jnp.float32))
    coupling = (
        jnp.einsum("nhtc,nhsc->nhts", keys_grown, keys_shrunk, precision=highest_precision)
        * jnp.swapaxes(rates, -1, -2)
        * strict
    )
    system = coupling + jnp.eye(span_rows, dtype=jnp.float32)
    solved = matmul_batched(
        unit_lower_inverse(system), jnp.concatenate([values_new, keys_grown], axis=-1)
    )
    fresh = solved[..., :DK] * rates
    carried = solved[..., DK:] * rates
    eye_key = jnp.eye(DK, dtype=jnp.float32)
    transition = jnp.exp(final_log[:, :, 0, :])[..., :, None] * eye_key - jnp.einsum(
        "nhsk,nhsv->nhkv", keys_final, carried, precision=highest_precision
    )
    offset = jnp.einsum("nhsk,nhsv->nhkv", keys_final, fresh, precision=highest_precision)
    mixing = (
        jnp.einsum("nhtc,nhsc->nhts", queries_grown, keys_shrunk, precision=highest_precision)
        * inclusive
    )

    moves, shifts = transition, offset
    while moves.shape[0] > 1:
        later_moves, earlier_moves = moves[1::2], moves[0::2]
        shifts = matmul_batched(later_moves, shifts[0::2]) + shifts[1::2]
        moves = matmul_batched(later_moves, earlier_moves)
    device_move, device_shift = moves[0], shifts[0]
    return (device_move, device_shift, (transition, offset, fresh, carried, queries_grown, mixing))


def emit_step(carried_parts, span_parts):
    recurrent_state, accumulated_move = carried_parts
    span_move, span_shift, fresh_state_term, carried_state_term, query_term, mixing_part = (
        span_parts
    )
    state_update = fresh_state_term - jnp.einsum(
        "orm,omj->orj", carried_state_term, recurrent_state, precision=highest_precision
    )
    produced_output = jnp.einsum(
        "fmb,fbi->fmi", query_term, recurrent_state, precision=highest_precision
    ) + jnp.einsum("hts,hsv->htv", mixing_part, state_update, precision=highest_precision)
    start_weight = query_term - jnp.einsum(
        "hts,hsv->htv", mixing_part, carried_state_term, precision=highest_precision
    )
    start_query = matmul_heads(start_weight, accumulated_move)
    next_parts = (
        matmul_heads(span_move, recurrent_state) + span_shift,
        matmul_heads(span_move, accumulated_move),
    )
    return (next_parts, (produced_output, start_query))


def token_major(span_values):
    stacked = jnp.stack(span_values)
    block_count, heads, span_rows, _ = stacked.shape
    return stacked.transpose(1, 0, 2, 3).reshape(heads, block_count * span_rows, DK)


def finish_spans(start_state, local_outputs, start_queries):
    outputs = local_outputs + matmul_heads(start_queries, start_state)
    heads, length, _ = outputs.shape
    return outputs.transpose(1, 0, 2).reshape(length, heads * DK).astype(jnp.bfloat16)


def per_device(
    kda_inputs,
    gate_log,
    beta,
    conv_weight,
    kda_out_weight,
    residual,
    norm_gain,
    latent_weight,
    latent_gain,
    query_weight,
    up_weight,
):
    length = residual.shape[0]
    edge_rows = kda_inputs[:, length - (CONV - 1) :, :]
    earlier_rows = passed_along(edge_rows, "ctx", 1)
    extended = jnp.concatenate([earlier_rows, kda_inputs], axis=1).astype(jnp.float32)
    running = jnp.zeros(kda_inputs.shape, jnp.float32)
    for tap_index in range(CONV):
        running = (
            running
            + conv_weight[:, tap_index, None, :] * extended[:, tap_index : tap_index + length, :]
        )
    activated = jax.nn.silu(running)
    kda_query = rounded(unit_heads(activated[0]) * DK ** (-0.5))
    kda_key = rounded(unit_heads(activated[1]))
    kda_value = rounded(activated[2])
    device_move, device_shift, span_data = delta_rule(kda_query, kda_key, kda_value, gate_log, beta)
    heads = device_move.shape[0]
    span_count = span_data[0].shape[0]
    emit_carry = (
        jnp.zeros((heads, DK, DK), jnp.float32),
        jnp.broadcast_to(jnp.eye(DK, dtype=jnp.float32), (heads, DK, DK)),
    )
    produced = []

    def run_emit(emit_carry):
        span_index = len(produced)
        emit_carry, emitted = emit_step(emit_carry, tuple(part[span_index] for part in span_data))
        produced.append(emitted)
        return emit_carry

    ctx_size = lax.axis_size("ctx")
    move, shift = device_move, device_shift
    distance = 1
    while distance < ctx_size:
        if 2 * distance < ctx_size:
            sent = jnp.stack([move, shift]).astype(jnp.bfloat16)
            both_in = passed_along(sent, "ctx", distance).astype(jnp.float32)
            next_shift = matmul_heads(move, both_in[1]) + shift
            next_move = matmul_heads(move, both_in[0])
        else:
            shift_in = passed_along(shift.astype(jnp.bfloat16), "ctx", distance)
            next_shift = matmul_heads(move, shift_in.astype(jnp.float32)) + shift
            next_move = move
        if len(produced) < span_count:
            emit_carry = run_emit(emit_carry)
            next_shift, next_move, emit_carry = lax.optimization_barrier(
                (next_shift, next_move, emit_carry)
            )
        move, shift = next_move, next_shift
        distance *= 2
    while len(produced) < span_count:
        emit_carry = run_emit(emit_carry)
    local_outputs = token_major([emitted[0] for emitted in produced])
    start_queries = token_major([emitted[1] for emitted in produced])
    start_state = passed_along(shift.astype(jnp.bfloat16), "ctx", 1).astype(jnp.float32)
    kda_core = finish_spans(start_state, local_outputs, start_queries)
    partial_proj = jnp.dot(kda_core, kda_out_weight, preferred_element_type=jnp.float32)
    stream_out = stream_after_head_sum(partial_proj, residual)
    normed, latent = prepare(stream_out, norm_gain, latent_weight, latent_gain)
    mla_query = jnp.dot(normed, query_weight, preferred_element_type=jnp.float32).astype(
        jnp.bfloat16
    )
    query_heads = mla_query.reshape(length, -1, DH)
    heads_mla = query_heads.shape[1]
    flat_up = up_weight.reshape(up_weight.shape[0], -1)
    my_first = lax.axis_index("ctx") * length
    query_positions = my_first + jnp.arange(length, dtype=jnp.int32)
    piece = gathered_earlier(latent)
    piece_rows = piece.shape[0]
    paired = (
        jnp.dot(piece, flat_up, preferred_element_type=jnp.float32)
        .astype(jnp.bfloat16)
        .reshape(piece_rows, 2, heads_mla, DH)
    )
    scores = jnp.einsum(
        "qhd,khd->hqk", query_heads, paired[:, 0], preferred_element_type=jnp.float32
    ) * DH ** (-0.5)
    key_positions = jnp.arange(piece_rows, dtype=jnp.int32)
    allowed = key_positions[None, :] <= query_positions[:, None]
    final_peak = jnp.max(jnp.where(allowed, scores, -1e30), axis=-1)
    weights = jnp.where(allowed, jnp.exp(scores - final_peak[..., None]), 0.0)
    final_total = jnp.sum(weights, axis=-1)
    final_mixed = jnp.einsum(
        "hqk,khd->hqd",
        weights.astype(jnp.bfloat16),
        paired[:, 1],
        preferred_element_type=jnp.float32,
    )
    attention_out = (
        (final_mixed / final_total[..., None])
        .transpose(1, 0, 2)
        .reshape(length, heads_mla * DH)
        .astype(jnp.bfloat16)
    )
    return (stream_out, attention_out)


def solution(mesh):
    in_specs = (
        P(None, "ctx", "head"),
        P("ctx", "head"),
        P("ctx", "head"),
        P(None, None, "head"),
        P("head", None),
        P("ctx", None),
        P(),
        P(),
        P(),
        P(None, "head"),
        P(None, None, "head"),
    )
    out_specs = (P("ctx", None), P("ctx", "head"))
    return jax.shard_map(
        per_device, mesh=mesh, in_specs=in_specs, out_specs=out_specs, check_vma=False
    )
```

```python
import math

import jax
import jax.numpy as jnp
from jax import lax
from jax.sharding import PartitionSpec as P
from jax.experimental import pallas as pl
from jax.experimental.pallas import tpu as pltpu

DK = 128
CONV = 4
DH = 128


eps_norm = 1e-06
highest_precision = lax.Precision.HIGHEST


def passed_along(block, axis, distance):
    devices = range(lax.axis_size(axis))
    route = [(i - distance, i) for i in devices if i - distance in devices]
    return lax.ppermute(block, axis, route)


def stream_after_head_sum(partial, residual):
    size = lax.axis_size("head")
    core = lax.axis_index("head") % 2
    half = partial.shape[0] // 2
    pair_route = [(i, i ^ 1) for i in range(size)]
    chip_route = [(i, i ^ 2) for i in range(size)]
    kept = lax.dynamic_slice_in_dim(partial, core * half, half)
    given = lax.dynamic_slice_in_dim(partial, (1 - core) * half, half)
    pair_sum = kept + lax.ppermute(given, "head", pair_route)
    pair_rounded = lax.optimization_barrier(pair_sum.astype(jnp.bfloat16))
    partner_rounded = lax.ppermute(pair_rounded, "head", chip_route)
    total = pair_rounded.astype(jnp.float32) + partner_rounded.astype(jnp.float32)
    my_rows = lax.dynamic_slice_in_dim(residual, core * half, half)
    stream_half = (my_rows.astype(jnp.float32) + total).astype(jnp.bfloat16)
    other_half = lax.ppermute(stream_half, "head", pair_route)
    return jnp.where(
        core == 0,
        jnp.concatenate([stream_half, other_half], axis=0),
        jnp.concatenate([other_half, stream_half], axis=0),
    )


def gather_kernel(
    block_ref, up_ref, keys_ref, values_ref, landed, send_sems, recv_sems, forward_sems
):
    me = lax.axis_index("ctx")
    head = lax.axis_index("head")
    core = head % 2
    sibling = head + 1 - 2 * core
    count, rows, _ = landed.shape
    heads = keys_ref.shape[0]

    def outgoing(peer):
        return pltpu.make_async_remote_copy(
            src_ref=block_ref,
            dst_ref=landed.at[me],
            send_sem=send_sems.at[peer],
            recv_sem=recv_sems.at[me],
            device_id={"ctx": peer, "head": head},
            device_id_type=pl.DeviceIdType.MESH,
        )

    def forwarded(origin):
        return pltpu.make_async_remote_copy(
            src_ref=landed.at[origin],
            dst_ref=landed.at[origin],
            send_sem=forward_sems.at[origin],
            recv_sem=recv_sems.at[origin],
            device_id={"ctx": me, "head": sibling},
            device_id_type=pl.DeviceIdType.MESH,
        )

    def project(origin, latent_rows):
        paired = jnp.dot(latent_rows, up_ref[...], preferred_element_type=jnp.float32).astype(
            keys_ref.dtype
        )
        place = pl.ds(pl.multiple_of(origin * rows, rows), rows)
        for index in range(heads):
            keys_ref[index, place, :] = paired[:, index * DH : (index + 1) * DH]
            values_ref[index, place, :] = paired[:, (heads + index) * DH : (heads + index + 1) * DH]

    @pl.loop(me + 1, count)
    def _(peer):
        @pl.when((peer + me) % 2 == core)
        def _():
            outgoing(peer).start()

    project(me, block_ref[...])

    @pl.loop(me + 1, count)
    def _(peer):
        place = pl.ds(pl.multiple_of(peer * rows, rows), rows)
        for index in range(heads):
            keys_ref[index, place, :] = jnp.zeros((rows, DH), keys_ref.dtype)
            values_ref[index, place, :] = jnp.zeros((rows, DH), values_ref.dtype)

    @pl.loop(0, me)
    def _(origin):
        @pl.when((origin + me) % 2 == core)
        def _():
            forwarded(origin).wait_recv()
            forwarded(origin).start()

        @pl.when((origin + me) % 2 != core)
        def _():
            forwarded(origin).wait_recv()

        project(origin, landed[origin])

    @pl.loop(me + 1, count)
    def _(peer):
        @pl.when((peer + me) % 2 == core)
        def _():
            outgoing(peer).wait_send()

    @pl.loop(0, me)
    def _(origin):
        @pl.when((origin + me) % 2 == core)
        def _():
            forwarded(origin).wait_send()


def projected_earlier(block, flat_up):
    count = lax.axis_size("ctx")
    rows, width = block.shape
    heads = flat_up.shape[1] // (2 * DH)
    side = jax.ShapeDtypeStruct((heads, count * rows, DH), block.dtype)
    return pl.pallas_call(
        gather_kernel,
        out_shape=(side, side),
        in_specs=[pl.BlockSpec(memory_space=pltpu.VMEM)] * 2,
        out_specs=(pl.BlockSpec(memory_space=pltpu.VMEM),) * 2,
        scratch_shapes=[pltpu.VMEM((count, rows, width), block.dtype)]
        + [pltpu.SemaphoreType.DMA((count,))] * 3,
        compiler_params=pltpu.CompilerParams(has_side_effects=True),
    )(block, flat_up)


def rounded(values):
    return lax.optimization_barrier(values.astype(jnp.bfloat16))


def unit_heads(activated):
    grouped = activated.reshape(activated.shape[0], -1, DK)
    scaled = grouped * lax.rsqrt(jnp.sum(grouped * grouped, axis=-1, keepdims=True) + eps_norm)
    return scaled.reshape(activated.shape)


def prepare(stream, norm_gain, latent_weight, latent_gain):
    widened = stream.astype(jnp.float32)
    normed = (
        widened
        * lax.rsqrt(jnp.mean(widened * widened, axis=-1, keepdims=True) + eps_norm)
        * norm_gain
    ).astype(jnp.bfloat16)
    latent_pre = jnp.dot(normed, latent_weight, preferred_element_type=jnp.float32)
    latent = (
        latent_pre
        * lax.rsqrt(jnp.mean(latent_pre * latent_pre, axis=-1, keepdims=True) + eps_norm)
        * latent_gain
    ).astype(jnp.bfloat16)
    return (normed, latent)


def span_layout(values, span_rows):
    length, channel_count = values.shape
    return values.reshape(length // span_rows, span_rows, channel_count // DK, DK).transpose(
        0, 2, 1, 3
    )


def matmul_heads(left, right):
    return jnp.einsum("hij,hjk->hik", left, right, precision=highest_precision)


def matmul_batched(left, right):
    return jnp.einsum("...ij,...jk->...ik", left, right, precision=highest_precision)


def unit_lower_inverse(system):
    size = system.shape[-1]
    rows = jnp.arange(size)[:, None]
    cols = jnp.arange(size)[None, :]
    inverse = jnp.broadcast_to(jnp.eye(size, dtype=system.dtype), system.shape)
    width = 1
    while width < size:
        below = (rows // (2 * width) == cols // (2 * width)) & (rows // width != cols // width)
        off_block = jnp.where(below, system, 0.0)
        correction = matmul_batched(matmul_batched(inverse, off_block), inverse)
        inverse = inverse - lax.optimization_barrier(correction)
        width *= 2
    return inverse


def delta_rule(kda_query, kda_key, kda_value, gate_log, beta):
    span_rows = 32
    length, channel_count = gate_log.shape
    heads = channel_count // DK
    queries = span_layout(kda_query.astype(jnp.float32), span_rows)
    keys_unit = span_layout(kda_key.astype(jnp.float32), span_rows)
    values_new = span_layout(kda_value.astype(jnp.float32), span_rows)
    inclusive_ones = jnp.tril(jnp.ones((span_rows, span_rows), jnp.float32))
    cumulative = jnp.einsum(
        "ts,nhsc->nhtc", inclusive_ones, span_layout(gate_log, span_rows), precision=highest_precision
    )
    rates = beta.reshape(length // span_rows, span_rows, heads).transpose(0, 2, 1)[..., None]
    growth = jnp.exp(cumulative)
    final_log = cumulative[:, :, -1:, :]
    keys_grown = keys_unit * growth
    keys_shrunk = keys_unit * jnp.exp(-cumulative)
    queries_grown = queries * growth
    keys_final = keys_unit * jnp.exp(final_log - cumulative)
    strict = jnp.tril(jnp.ones((span_rows, span_rows), jnp.float32), -1)
    inclusive = jnp.tril(jnp.ones((span_rows, span_rows), jnp.float32))
    coupling = (
        jnp.einsum("nhtc,nhsc->nhts", keys_grown, keys_shrunk, precision=highest_precision)
        * jnp.swapaxes(rates, -1, -2)
        * strict
    )
    system = coupling + jnp.eye(span_rows, dtype=jnp.float32)
    solved = matmul_batched(
        unit_lower_inverse(system), jnp.concatenate([values_new, keys_grown], axis=-1)
    )
    fresh = solved[..., :DK] * rates
    carried = solved[..., DK:] * rates
    eye_key = jnp.eye(DK, dtype=jnp.float32)
    transition = jnp.exp(final_log[:, :, 0, :])[..., :, None] * eye_key - jnp.einsum(
        "nhsk,nhsv->nhkv", keys_final, carried, precision=highest_precision
    )
    offset = jnp.einsum("nhsk,nhsv->nhkv", keys_final, fresh, precision=highest_precision)
    mixing = (
        jnp.einsum("nhtc,nhsc->nhts", queries_grown, keys_shrunk, precision=highest_precision)
        * inclusive
    )

    moves, shifts = transition, offset
    while moves.shape[0] > 1:
        later_moves, earlier_moves = moves[1::2], moves[0::2]
        shifts = matmul_batched(later_moves, shifts[0::2]) + shifts[1::2]
        moves = matmul_batched(later_moves, earlier_moves)
    device_move, device_shift = moves[0], shifts[0]
    return (device_move, device_shift, (transition, offset, fresh, carried, queries_grown, mixing))


def emit_step(carried_parts, span_parts):
    recurrent_state, accumulated_move = carried_parts
    span_move, span_shift, fresh_state_term, carried_state_term, query_term, mixing_part = (
        span_parts
    )
    state_update = fresh_state_term - jnp.einsum(
        "orm,omj->orj", carried_state_term, recurrent_state, precision=highest_precision
    )
    produced_output = jnp.einsum(
        "fmb,fbi->fmi", query_term, recurrent_state, precision=highest_precision
    ) + jnp.einsum("hts,hsv->htv", mixing_part, state_update, precision=highest_precision)
    start_weight = query_term - jnp.einsum(
        "hts,hsv->htv", mixing_part, carried_state_term, precision=highest_precision
    )
    start_query = matmul_heads(start_weight, accumulated_move)
    next_parts = (
        matmul_heads(span_move, recurrent_state) + span_shift,
        matmul_heads(span_move, accumulated_move),
    )
    return (next_parts, (produced_output, start_query))


def token_major(span_values):
    stacked = jnp.stack(span_values)
    block_count, heads, span_rows, _ = stacked.shape
    return stacked.transpose(1, 0, 2, 3).reshape(heads, block_count * span_rows, DK)


def finish_spans(start_state, local_outputs, start_queries):
    outputs = local_outputs + matmul_heads(start_queries, start_state)
    heads, length, _ = outputs.shape
    return outputs.transpose(1, 0, 2).reshape(length, heads * DK).astype(jnp.bfloat16)


def per_device(
    kda_inputs,
    gate_log,
    beta,
    conv_weight,
    kda_out_weight,
    residual,
    norm_gain,
    latent_weight,
    latent_gain,
    query_weight,
    up_weight,
):
    length = residual.shape[0]
    edge_rows = kda_inputs[:, length - (CONV - 1) :, :]
    earlier_rows = passed_along(edge_rows, "ctx", 1)
    extended = jnp.concatenate([earlier_rows, kda_inputs], axis=1).astype(jnp.float32)
    running = jnp.zeros(kda_inputs.shape, jnp.float32)
    for tap_index in range(CONV):
        running = (
            running
            + conv_weight[:, tap_index, None, :] * extended[:, tap_index : tap_index + length, :]
        )
    activated = jax.nn.silu(running)
    kda_query = rounded(unit_heads(activated[0]) * DK ** (-0.5))
    kda_key = rounded(unit_heads(activated[1]))
    kda_value = rounded(activated[2])
    device_move, device_shift, span_data = delta_rule(kda_query, kda_key, kda_value, gate_log, beta)
    heads = device_move.shape[0]
    span_count = span_data[0].shape[0]
    emit_carry = (
        jnp.zeros((heads, DK, DK), jnp.float32),
        jnp.broadcast_to(jnp.eye(DK, dtype=jnp.float32), (heads, DK, DK)),
    )
    produced = []

    def run_emit(emit_carry):
        span_index = len(produced)
        emit_carry, emitted = emit_step(emit_carry, tuple(part[span_index] for part in span_data))
        produced.append(emitted)
        return emit_carry

    ctx_size = lax.axis_size("ctx")
    move, shift = device_move, device_shift
    distance = 1
    while distance < ctx_size:
        if 2 * distance < ctx_size:
            sent = jnp.stack([move, shift]).astype(jnp.bfloat16)
            both_in = passed_along(sent, "ctx", distance).astype(jnp.float32)
            next_shift = matmul_heads(move, both_in[1]) + shift
            next_move = matmul_heads(move, both_in[0])
        else:
            shift_in = passed_along(shift.astype(jnp.bfloat16), "ctx", distance)
            next_shift = matmul_heads(move, shift_in.astype(jnp.float32)) + shift
            next_move = move
        if len(produced) < span_count:
            emit_carry = run_emit(emit_carry)
            next_shift, next_move, emit_carry = lax.optimization_barrier(
                (next_shift, next_move, emit_carry)
            )
        move, shift = next_move, next_shift
        distance *= 2
    while len(produced) < span_count:
        emit_carry = run_emit(emit_carry)
    local_outputs = token_major([emitted[0] for emitted in produced])
    start_queries = token_major([emitted[1] for emitted in produced])
    start_state = passed_along(shift.astype(jnp.bfloat16), "ctx", 1).astype(jnp.float32)
    kda_core = finish_spans(start_state, local_outputs, start_queries)
    partial_proj = jnp.dot(kda_core, kda_out_weight, preferred_element_type=jnp.float32)
    stream_out = stream_after_head_sum(partial_proj, residual)
    normed, latent = prepare(stream_out, norm_gain, latent_weight, latent_gain)
    mla_query = jnp.dot(normed, query_weight, preferred_element_type=jnp.float32).astype(
        jnp.bfloat16
    )
    query_heads = mla_query.reshape(length, -1, DH)
    heads_mla = query_heads.shape[1]
    flat_up = up_weight.reshape(up_weight.shape[0], -1)
    my_first = lax.axis_index("ctx") * length
    query_positions = my_first + jnp.arange(length, dtype=jnp.int32)
    key_rows, value_rows = projected_earlier(latent, flat_up)
    piece_rows = key_rows.shape[1]
    scores = jnp.einsum(
        "qhd,hkd->hqk", query_heads, key_rows, preferred_element_type=jnp.float32
    ) * DH ** (-0.5)
    key_positions = jnp.arange(piece_rows, dtype=jnp.int32)
    allowed = key_positions[None, :] <= query_positions[:, None]
    final_peak = jnp.max(jnp.where(allowed, scores, -1e30), axis=-1)
    weights = jnp.where(allowed, jnp.exp(scores - final_peak[..., None]), 0.0)
    final_total = jnp.sum(weights, axis=-1)
    final_mixed = jnp.einsum(
        "hqk,hkd->hqd",
        weights.astype(jnp.bfloat16),
        value_rows,
        preferred_element_type=jnp.float32,
    )
    attention_out = (
        (final_mixed / final_total[..., None])
        .transpose(1, 0, 2)
        .reshape(length, heads_mla * DH)
        .astype(jnp.bfloat16)
    )
    return (stream_out, attention_out)


def solution(mesh):
    in_specs = (
        P(None, "ctx", "head"),
        P("ctx", "head"),
        P("ctx", "head"),
        P(None, None, "head"),
        P("head", None),
        P("ctx", None),
        P(),
        P(),
        P(),
        P(None, "head"),
        P(None, None, "head"),
    )
    out_specs = (P("ctx", None), P("ctx", "head"))
    return jax.shard_map(
        per_device, mesh=mesh, in_specs=in_specs, out_specs=out_specs, check_vma=False
    )
```

```python
import math

import jax
import jax.numpy as jnp
from jax import lax
from jax.sharding import PartitionSpec as P
from jax.experimental import pallas as pl
from jax.experimental.pallas import tpu as pltpu

DK = 128
CONV = 4
DH = 128


eps_norm = 1e-06
highest_precision = lax.Precision.HIGHEST


def passed_along(block, axis, distance):
    devices = range(lax.axis_size(axis))
    route = [(i - distance, i) for i in devices if i - distance in devices]
    return lax.ppermute(block, axis, route)


def stream_after_head_sum(partial, residual):
    size = lax.axis_size("head")
    core = lax.axis_index("head") % 2
    half = partial.shape[0] // 2
    pair_route = [(i, i ^ 1) for i in range(size)]
    chip_route = [(i, i ^ 2) for i in range(size)]
    kept = lax.dynamic_slice_in_dim(partial, core * half, half)
    given = lax.dynamic_slice_in_dim(partial, (1 - core) * half, half)
    pair_sum = kept + lax.ppermute(given, "head", pair_route)
    pair_rounded = lax.optimization_barrier(pair_sum.astype(jnp.bfloat16))
    partner_rounded = lax.ppermute(pair_rounded, "head", chip_route)
    total = pair_rounded.astype(jnp.float32) + partner_rounded.astype(jnp.float32)
    my_rows = lax.dynamic_slice_in_dim(residual, core * half, half)
    stream_half = (my_rows.astype(jnp.float32) + total).astype(jnp.bfloat16)
    other_half = lax.ppermute(stream_half, "head", pair_route)
    return jnp.where(
        core == 0,
        jnp.concatenate([stream_half, other_half], axis=0),
        jnp.concatenate([other_half, stream_half], axis=0),
    )


def gather_kernel(block_ref, out_ref, send_sems, recv_sems, forward_sems):
    me = lax.axis_index("ctx")
    head = lax.axis_index("head")
    core = head % 2
    sibling = head + 1 - 2 * core
    count = out_ref.shape[0]
    out_ref[me] = block_ref[...]

    def outgoing(peer):
        return pltpu.make_async_remote_copy(
            src_ref=block_ref,
            dst_ref=out_ref.at[me],
            send_sem=send_sems.at[peer],
            recv_sem=recv_sems.at[me],
            device_id={"ctx": peer, "head": head},
            device_id_type=pl.DeviceIdType.MESH,
        )

    def forwarded(origin):
        return pltpu.make_async_remote_copy(
            src_ref=out_ref.at[origin],
            dst_ref=out_ref.at[origin],
            send_sem=forward_sems.at[origin],
            recv_sem=recv_sems.at[origin],
            device_id={"ctx": me, "head": sibling},
            device_id_type=pl.DeviceIdType.MESH,
        )

    @pl.loop(me + 1, count)
    def _(peer):
        @pl.when((peer + me) % 2 == core)
        def _():
            outgoing(peer).start()

    @pl.loop(me + 1, count)
    def _(peer):
        out_ref[peer] = jnp.zeros(block_ref.shape, block_ref.dtype)

    @pl.loop(0, me)
    def _(step):
        origin = me - 1 - step

        @pl.when((origin + me) % 2 == core)
        def _():
            forwarded(origin).wait_recv()
            forwarded(origin).start()

    @pl.loop(0, me)
    def _(step):
        origin = me - 1 - step

        @pl.when((origin + me) % 2 != core)
        def _():
            forwarded(origin).wait_recv()

    @pl.loop(me + 1, count)
    def _(peer):
        @pl.when((peer + me) % 2 == core)
        def _():
            outgoing(peer).wait_send()

    @pl.loop(0, me)
    def _(origin):
        @pl.when((origin + me) % 2 == core)
        def _():
            forwarded(origin).wait_send()


def gathered_earlier(block):
    count = lax.axis_size("ctx")
    rows, width = block.shape
    stacked = pl.pallas_call(
        gather_kernel,
        out_shape=jax.ShapeDtypeStruct((count, rows, width), block.dtype),
        in_specs=[pl.BlockSpec(memory_space=pltpu.VMEM)],
        out_specs=pl.BlockSpec(memory_space=pltpu.VMEM),
        scratch_shapes=[pltpu.SemaphoreType.DMA((count,))] * 3,
        compiler_params=pltpu.CompilerParams(has_side_effects=True),
    )(block)
    return stacked.reshape(count * rows, width)


def rounded(values):
    return lax.optimization_barrier(values.astype(jnp.bfloat16))


def unit_heads(activated):
    grouped = activated.reshape(activated.shape[0], -1, DK)
    scaled = grouped * lax.rsqrt(jnp.sum(grouped * grouped, axis=-1, keepdims=True) + eps_norm)
    return scaled.reshape(activated.shape)


def prepare(stream, norm_gain, latent_weight, latent_gain):
    widened = stream.astype(jnp.float32)
    normed = (
        widened
        * lax.rsqrt(jnp.mean(widened * widened, axis=-1, keepdims=True) + eps_norm)
        * norm_gain
    ).astype(jnp.bfloat16)
    latent_pre = jnp.dot(normed, latent_weight, preferred_element_type=jnp.float32)
    latent = (
        latent_pre
        * lax.rsqrt(jnp.mean(latent_pre * latent_pre, axis=-1, keepdims=True) + eps_norm)
        * latent_gain
    ).astype(jnp.bfloat16)
    return (normed, latent)


def span_layout(values, span_rows):
    length, channel_count = values.shape
    return values.reshape(length // span_rows, span_rows, channel_count // DK, DK).transpose(
        0, 2, 1, 3
    )


def matmul_heads(left, right):
    return jnp.einsum("hij,hjk->hik", left, right, precision=highest_precision)


def matmul_batched(left, right):
    return jnp.einsum("...ij,...jk->...ik", left, right, precision=highest_precision)


def unit_lower_inverse(system):
    size = system.shape[-1]
    rows = jnp.arange(size)[:, None]
    cols = jnp.arange(size)[None, :]
    inverse = jnp.broadcast_to(jnp.eye(size, dtype=system.dtype), system.shape)
    width = 1
    while width < size:
        below = (rows // (2 * width) == cols // (2 * width)) & (rows // width != cols // width)
        off_block = jnp.where(below, system, 0.0)
        correction = matmul_batched(matmul_batched(inverse, off_block), inverse)
        inverse = inverse - lax.optimization_barrier(correction)
        width *= 2
    return inverse


def delta_rule(kda_query, kda_key, kda_value, gate_log, beta):
    span_rows = 32
    length, channel_count = gate_log.shape
    heads = channel_count // DK
    queries = span_layout(kda_query.astype(jnp.float32), span_rows)
    keys_unit = span_layout(kda_key.astype(jnp.float32), span_rows)
    values_new = span_layout(kda_value.astype(jnp.float32), span_rows)
    inclusive_ones = jnp.tril(jnp.ones((span_rows, span_rows), jnp.float32))
    cumulative = jnp.einsum(
        "ts,nhsc->nhtc", inclusive_ones, span_layout(gate_log, span_rows), precision=highest_precision
    )
    rates = beta.reshape(length // span_rows, span_rows, heads).transpose(0, 2, 1)[..., None]
    growth = jnp.exp(cumulative)
    final_log = cumulative[:, :, -1:, :]
    keys_grown = keys_unit * growth
    keys_shrunk = keys_unit * jnp.exp(-cumulative)
    queries_grown = queries * growth
    keys_final = keys_unit * jnp.exp(final_log - cumulative)
    strict = jnp.tril(jnp.ones((span_rows, span_rows), jnp.float32), -1)
    inclusive = jnp.tril(jnp.ones((span_rows, span_rows), jnp.float32))
    coupling = (
        jnp.einsum("nhtc,nhsc->nhts", keys_grown, keys_shrunk, precision=highest_precision)
        * jnp.swapaxes(rates, -1, -2)
        * strict
    )
    system = coupling + jnp.eye(span_rows, dtype=jnp.float32)
    solved = matmul_batched(
        unit_lower_inverse(system), jnp.concatenate([values_new, keys_grown], axis=-1)
    )
    fresh = solved[..., :DK] * rates
    carried = solved[..., DK:] * rates
    eye_key = jnp.eye(DK, dtype=jnp.float32)
    transition = jnp.exp(final_log[:, :, 0, :])[..., :, None] * eye_key - jnp.einsum(
        "nhsk,nhsv->nhkv", keys_final, carried, precision=highest_precision
    )
    offset = jnp.einsum("nhsk,nhsv->nhkv", keys_final, fresh, precision=highest_precision)
    mixing = (
        jnp.einsum("nhtc,nhsc->nhts", queries_grown, keys_shrunk, precision=highest_precision)
        * inclusive
    )

    moves, shifts = transition, offset
    while moves.shape[0] > 1:
        later_moves, earlier_moves = moves[1::2], moves[0::2]
        shifts = matmul_batched(later_moves, shifts[0::2]) + shifts[1::2]
        moves = matmul_batched(later_moves, earlier_moves)
    device_move, device_shift = moves[0], shifts[0]
    return (device_move, device_shift, (transition, offset, fresh, carried, queries_grown, mixing))


def emit_step(carried_parts, span_parts):
    recurrent_state, accumulated_move = carried_parts
    span_move, span_shift, fresh_state_term, carried_state_term, query_term, mixing_part = (
        span_parts
    )
    state_update = fresh_state_term - jnp.einsum(
        "orm,omj->orj", carried_state_term, recurrent_state, precision=highest_precision
    )
    produced_output = jnp.einsum(
        "fmb,fbi->fmi", query_term, recurrent_state, precision=highest_precision
    ) + jnp.einsum("hts,hsv->htv", mixing_part, state_update, precision=highest_precision)
    start_weight = query_term - jnp.einsum(
        "hts,hsv->htv", mixing_part, carried_state_term, precision=highest_precision
    )
    start_query = matmul_heads(start_weight, accumulated_move)
    next_parts = (
        matmul_heads(span_move, recurrent_state) + span_shift,
        matmul_heads(span_move, accumulated_move),
    )
    return (next_parts, (produced_output, start_query))


def token_major(span_values):
    stacked = jnp.stack(span_values)
    block_count, heads, span_rows, _ = stacked.shape
    return stacked.transpose(1, 0, 2, 3).reshape(heads, block_count * span_rows, DK)


def finish_spans(start_state, local_outputs, start_queries):
    outputs = local_outputs + matmul_heads(start_queries, start_state)
    heads, length, _ = outputs.shape
    return outputs.transpose(1, 0, 2).reshape(length, heads * DK).astype(jnp.bfloat16)


def per_device(
    kda_inputs,
    gate_log,
    beta,
    conv_weight,
    kda_out_weight,
    residual,
    norm_gain,
    latent_weight,
    latent_gain,
    query_weight,
    up_weight,
):
    length = residual.shape[0]
    edge_rows = kda_inputs[:, length - (CONV - 1) :, :]
    earlier_rows = passed_along(edge_rows, "ctx", 1)
    extended = jnp.concatenate([earlier_rows, kda_inputs], axis=1).astype(jnp.float32)
    running = jnp.zeros(kda_inputs.shape, jnp.float32)
    for tap_index in range(CONV):
        running = (
            running
            + conv_weight[:, tap_index, None, :] * extended[:, tap_index : tap_index + length, :]
        )
    activated = jax.nn.silu(running)
    kda_query = rounded(unit_heads(activated[0]) * DK ** (-0.5))
    kda_key = rounded(unit_heads(activated[1]))
    kda_value = rounded(activated[2])
    device_move, device_shift, span_data = delta_rule(kda_query, kda_key, kda_value, gate_log, beta)
    heads = device_move.shape[0]
    span_count = span_data[0].shape[0]
    emit_carry = (
        jnp.zeros((heads, DK, DK), jnp.float32),
        jnp.broadcast_to(jnp.eye(DK, dtype=jnp.float32), (heads, DK, DK)),
    )
    produced = []

    def run_emit(emit_carry):
        span_index = len(produced)
        emit_carry, emitted = emit_step(emit_carry, tuple(part[span_index] for part in span_data))
        produced.append(emitted)
        return emit_carry

    ctx_size = lax.axis_size("ctx")
    move, shift = device_move, device_shift
    distance = 1
    while distance < ctx_size:
        if 2 * distance < ctx_size:
            sent = jnp.stack([move, shift]).astype(jnp.bfloat16)
            both_in = passed_along(sent, "ctx", distance).astype(jnp.float32)
            next_shift = matmul_heads(move, both_in[1]) + shift
            next_move = matmul_heads(move, both_in[0])
        else:
            shift_in = passed_along(shift.astype(jnp.bfloat16), "ctx", distance)
            next_shift = matmul_heads(move, shift_in.astype(jnp.float32)) + shift
            next_move = move
        if len(produced) < span_count:
            emit_carry = run_emit(emit_carry)
            next_shift, next_move, emit_carry = lax.optimization_barrier(
                (next_shift, next_move, emit_carry)
            )
        move, shift = next_move, next_shift
        distance *= 2
    while len(produced) < span_count:
        emit_carry = run_emit(emit_carry)
    local_outputs = token_major([emitted[0] for emitted in produced])
    start_queries = token_major([emitted[1] for emitted in produced])
    start_state = passed_along(shift.astype(jnp.bfloat16), "ctx", 1).astype(jnp.float32)
    kda_core = finish_spans(start_state, local_outputs, start_queries)
    partial_proj = jnp.dot(kda_core, kda_out_weight, preferred_element_type=jnp.float32)
    stream_out = stream_after_head_sum(partial_proj, residual)
    normed, latent = prepare(stream_out, norm_gain, latent_weight, latent_gain)
    mla_query = jnp.dot(normed, query_weight, preferred_element_type=jnp.float32).astype(
        jnp.bfloat16
    )
    query_heads = mla_query.reshape(length, -1, DH)
    heads_mla = query_heads.shape[1]
    flat_up = up_weight.reshape(up_weight.shape[0], -1)
    my_first = lax.axis_index("ctx") * length
    query_positions = my_first + jnp.arange(length, dtype=jnp.int32)
    piece = gathered_earlier(latent)
    piece_rows = piece.shape[0]
    paired = (
        jnp.dot(piece, flat_up, preferred_element_type=jnp.float32)
        .astype(jnp.bfloat16)
        .reshape(piece_rows, 2, heads_mla, DH)
    )
    scores = jnp.einsum(
        "qhd,khd->hqk", query_heads, paired[:, 0], preferred_element_type=jnp.float32
    ) * DH ** (-0.5)
    key_positions = jnp.arange(piece_rows, dtype=jnp.int32)
    allowed = key_positions[None, :] <= query_positions[:, None]
    final_peak = jnp.max(jnp.where(allowed, scores, -1e30), axis=-1)
    weights = jnp.where(allowed, jnp.exp(scores - final_peak[..., None]), 0.0)
    final_total = jnp.sum(weights, axis=-1)
    final_mixed = jnp.einsum(
        "hqk,khd->hqd",
        weights.astype(jnp.bfloat16),
        paired[:, 1],
        preferred_element_type=jnp.float32,
    )
    attention_out = (
        (final_mixed / final_total[..., None])
        .transpose(1, 0, 2)
        .reshape(length, heads_mla * DH)
        .astype(jnp.bfloat16)
    )
    return (stream_out, attention_out)


def solution(mesh):
    in_specs = (
        P(None, "ctx", "head"),
        P("ctx", "head"),
        P("ctx", "head"),
        P(None, None, "head"),
        P("head", None),
        P("ctx", None),
        P(),
        P(),
        P(),
        P(None, "head"),
        P(None, None, "head"),
    )
    out_specs = (P("ctx", None), P("ctx", "head"))
    return jax.shard_map(
        per_device, mesh=mesh, in_specs=in_specs, out_specs=out_specs, check_vma=False
    )
```

```python
import math

import jax
import jax.numpy as jnp
from jax import lax
from jax.sharding import PartitionSpec as P
from jax.experimental import pallas as pl
from jax.experimental.pallas import tpu as pltpu

DK = 128
CONV = 4
DH = 128


eps_norm = 1e-06
highest_precision = lax.Precision.HIGHEST


def passed_along(block, axis, distance):
    devices = range(lax.axis_size(axis))
    route = [(i - distance, i) for i in devices if i - distance in devices]
    return lax.ppermute(block, axis, route)


def stream_after_head_sum(partial, residual):
    size = lax.axis_size("head")
    core = lax.axis_index("head") % 2
    half = partial.shape[0] // 2
    pair_route = [(i, i ^ 1) for i in range(size)]
    chip_route = [(i, i ^ 2) for i in range(size)]
    kept = lax.dynamic_slice_in_dim(partial, core * half, half)
    given = lax.dynamic_slice_in_dim(partial, (1 - core) * half, half)
    pair_sum = kept + lax.ppermute(given, "head", pair_route)
    pair_rounded = lax.optimization_barrier(pair_sum.astype(jnp.bfloat16))
    partner_rounded = lax.ppermute(pair_rounded, "head", chip_route)
    total = pair_rounded.astype(jnp.float32) + partner_rounded.astype(jnp.float32)
    my_rows = lax.dynamic_slice_in_dim(residual, core * half, half)
    stream_half = (my_rows.astype(jnp.float32) + total).astype(jnp.bfloat16)
    other_half = lax.ppermute(stream_half, "head", pair_route)
    return jnp.where(
        core == 0,
        jnp.concatenate([stream_half, other_half], axis=0),
        jnp.concatenate([other_half, stream_half], axis=0),
    )


def gather_kernel(block_ref, out_ref, send_sems, recv_sems, forward_sems):
    me = lax.axis_index("ctx")
    head = lax.axis_index("head")
    core = head % 2
    sibling = head + 1 - 2 * core
    count = out_ref.shape[0]
    out_ref[me] = block_ref[...]

    def outgoing(peer):
        return pltpu.make_async_remote_copy(
            src_ref=block_ref,
            dst_ref=out_ref.at[me],
            send_sem=send_sems.at[peer],
            recv_sem=recv_sems.at[me],
            device_id={"ctx": peer, "head": head},
            device_id_type=pl.DeviceIdType.MESH,
        )

    def forwarded(origin):
        return pltpu.make_async_remote_copy(
            src_ref=out_ref.at[origin],
            dst_ref=out_ref.at[origin],
            send_sem=forward_sems.at[origin],
            recv_sem=recv_sems.at[origin],
            device_id={"ctx": me, "head": sibling},
            device_id_type=pl.DeviceIdType.MESH,
        )

    @pl.loop(me + 1, count)
    def _(peer):
        @pl.when((peer + me) % 2 == core)
        def _():
            outgoing(peer).start()

    @pl.loop(me + 1, count)
    def _(peer):
        out_ref[peer] = jnp.zeros(block_ref.shape, block_ref.dtype)

    @pl.loop(0, me)
    def _(step):
        origin = me - 1 - step

        @pl.when((origin + me) % 2 == core)
        def _():
            forwarded(origin).wait_recv()
            forwarded(origin).start()

    @pl.loop(0, me)
    def _(step):
        origin = me - 1 - step

        @pl.when((origin + me) % 2 != core)
        def _():
            forwarded(origin).wait_recv()

    @pl.loop(me + 1, count)
    def _(peer):
        @pl.when((peer + me) % 2 == core)
        def _():
            outgoing(peer).wait_send()

    @pl.loop(0, me)
    def _(origin):
        @pl.when((origin + me) % 2 == core)
        def _():
            forwarded(origin).wait_send()


def gathered_earlier(block):
    count = lax.axis_size("ctx")
    rows, width = block.shape
    stacked = pl.pallas_call(
        gather_kernel,
        out_shape=jax.ShapeDtypeStruct((count, rows, width), block.dtype),
        in_specs=[pl.BlockSpec(memory_space=pltpu.VMEM)],
        out_specs=pl.BlockSpec(memory_space=pltpu.VMEM),
        scratch_shapes=[pltpu.SemaphoreType.DMA((count,))] * 3,
        compiler_params=pltpu.CompilerParams(has_side_effects=True),
    )(block)
    return stacked.reshape(count * rows, width)


def rounded(values):
    return lax.optimization_barrier(values.astype(jnp.bfloat16))


def unit_heads(activated):
    grouped = activated.reshape(activated.shape[0], -1, DK)
    scaled = grouped * lax.rsqrt(jnp.sum(grouped * grouped, axis=-1, keepdims=True) + eps_norm)
    return scaled.reshape(activated.shape)


def prepare(stream, norm_gain, latent_weight, latent_gain):
    widened = stream.astype(jnp.float32)
    normed = (
        widened
        * lax.rsqrt(jnp.mean(widened * widened, axis=-1, keepdims=True) + eps_norm)
        * norm_gain
    ).astype(jnp.bfloat16)
    latent_pre = jnp.dot(normed, latent_weight, preferred_element_type=jnp.float32)
    latent = (
        latent_pre
        * lax.rsqrt(jnp.mean(latent_pre * latent_pre, axis=-1, keepdims=True) + eps_norm)
        * latent_gain
    ).astype(jnp.bfloat16)
    return (normed, latent)


def span_layout(values, span_rows):
    length, channel_count = values.shape
    return values.reshape(length // span_rows, span_rows, channel_count // DK, DK).transpose(
        0, 2, 1, 3
    )


def matmul_heads(left, right):
    return jnp.einsum("hij,hjk->hik", left, right, precision=highest_precision)


def matmul_batched(left, right):
    return jnp.einsum("...ij,...jk->...ik", left, right, precision=highest_precision)


def unit_lower_inverse(system):
    size = system.shape[-1]
    rows = jnp.arange(size)[:, None]
    cols = jnp.arange(size)[None, :]
    inverse = jnp.broadcast_to(jnp.eye(size, dtype=system.dtype), system.shape)
    width = 1
    while width < size:
        below = (rows // (2 * width) == cols // (2 * width)) & (rows // width != cols // width)
        off_block = jnp.where(below, system, 0.0)
        correction = matmul_batched(matmul_batched(inverse, off_block), inverse)
        inverse = inverse - lax.optimization_barrier(correction)
        width *= 2
    return inverse


def delta_rule(kda_query, kda_key, kda_value, gate_log, beta):
    span_rows = 32
    length, channel_count = gate_log.shape
    heads = channel_count // DK
    queries = span_layout(kda_query.astype(jnp.float32), span_rows)
    keys_unit = span_layout(kda_key.astype(jnp.float32), span_rows)
    values_new = span_layout(kda_value.astype(jnp.float32), span_rows)
    inclusive_ones = jnp.tril(jnp.ones((span_rows, span_rows), jnp.float32))
    cumulative = jnp.einsum(
        "ts,nhsc->nhtc", inclusive_ones, span_layout(gate_log, span_rows), precision=highest_precision
    )
    rates = beta.reshape(length // span_rows, span_rows, heads).transpose(0, 2, 1)[..., None]
    growth = jnp.exp(cumulative)
    final_log = cumulative[:, :, -1:, :]
    keys_grown = keys_unit * growth
    keys_shrunk = keys_unit * jnp.exp(-cumulative)
    queries_grown = queries * growth
    keys_final = keys_unit * jnp.exp(final_log - cumulative)
    strict = jnp.tril(jnp.ones((span_rows, span_rows), jnp.float32), -1)
    inclusive = jnp.tril(jnp.ones((span_rows, span_rows), jnp.float32))
    coupling = (
        jnp.einsum("nhtc,nhsc->nhts", keys_grown, keys_shrunk, precision=highest_precision)
        * jnp.swapaxes(rates, -1, -2)
        * strict
    )
    system = coupling + jnp.eye(span_rows, dtype=jnp.float32)
    solved = matmul_batched(
        unit_lower_inverse(system), jnp.concatenate([values_new, keys_grown], axis=-1)
    )
    fresh = solved[..., :DK] * rates
    carried = solved[..., DK:] * rates
    eye_key = jnp.eye(DK, dtype=jnp.float32)
    transition = jnp.exp(final_log[:, :, 0, :])[..., :, None] * eye_key - jnp.einsum(
        "nhsk,nhsv->nhkv", keys_final, carried, precision=highest_precision
    )
    offset = jnp.einsum("nhsk,nhsv->nhkv", keys_final, fresh, precision=highest_precision)
    mixing = (
        jnp.einsum("nhtc,nhsc->nhts", queries_grown, keys_shrunk, precision=highest_precision)
        * inclusive
    )

    moves, shifts = transition, offset
    while moves.shape[0] > 1:
        later_moves, earlier_moves = moves[1::2], moves[0::2]
        shifts = matmul_batched(later_moves, shifts[0::2]) + shifts[1::2]
        moves = matmul_batched(later_moves, earlier_moves)
    device_move, device_shift = moves[0], shifts[0]
    return (device_move, device_shift, (transition, offset, fresh, carried, queries_grown, mixing))


def emit_step(carried_parts, span_parts):
    recurrent_state, accumulated_move = carried_parts
    span_move, span_shift, fresh_state_term, carried_state_term, query_term, mixing_part = (
        span_parts
    )
    state_update = fresh_state_term - jnp.einsum(
        "orm,omj->orj", carried_state_term, recurrent_state, precision=highest_precision
    )
    produced_output = jnp.einsum(
        "fmb,fbi->fmi", query_term, recurrent_state, precision=highest_precision
    ) + jnp.einsum("hts,hsv->htv", mixing_part, state_update, precision=highest_precision)
    start_weight = query_term - jnp.einsum(
        "hts,hsv->htv", mixing_part, carried_state_term, precision=highest_precision
    )
    start_query = matmul_heads(start_weight, accumulated_move)
    next_parts = (
        matmul_heads(span_move, recurrent_state) + span_shift,
        matmul_heads(span_move, accumulated_move),
    )
    return (next_parts, (produced_output, start_query))


def token_major(span_values):
    stacked = jnp.stack(span_values)
    block_count, heads, span_rows, _ = stacked.shape
    return stacked.transpose(1, 0, 2, 3).reshape(heads, block_count * span_rows, DK)


def finish_spans(start_state, local_outputs, start_queries):
    outputs = local_outputs + matmul_heads(start_queries, start_state)
    heads, length, _ = outputs.shape
    return outputs.transpose(1, 0, 2).reshape(length, heads * DK).astype(jnp.bfloat16)


def per_device(
    kda_inputs,
    gate_log,
    beta,
    conv_weight,
    kda_out_weight,
    residual,
    norm_gain,
    latent_weight,
    latent_gain,
    query_weight,
    up_weight,
):
    length = residual.shape[0]
    edge_rows = kda_inputs[:, length - (CONV - 1) :, :]
    earlier_rows = passed_along(edge_rows, "ctx", 1)
    extended = jnp.concatenate([earlier_rows, kda_inputs], axis=1).astype(jnp.float32)
    running = jnp.zeros(kda_inputs.shape, jnp.float32)
    for tap_index in range(CONV):
        running = (
            running
            + conv_weight[:, tap_index, None, :] * extended[:, tap_index : tap_index + length, :]
        )
    activated = jax.nn.silu(running)
    kda_query = rounded(unit_heads(activated[0]) * DK ** (-0.5))
    kda_key = rounded(unit_heads(activated[1]))
    kda_value = rounded(activated[2])
    device_move, device_shift, span_data = delta_rule(kda_query, kda_key, kda_value, gate_log, beta)
    heads = device_move.shape[0]
    span_count = span_data[0].shape[0]
    emit_carry = (
        jnp.zeros((heads, DK, DK), jnp.float32),
        jnp.broadcast_to(jnp.eye(DK, dtype=jnp.float32), (heads, DK, DK)),
    )
    produced = []

    def run_emit(emit_carry):
        span_index = len(produced)
        emit_carry, emitted = emit_step(emit_carry, tuple(part[span_index] for part in span_data))
        produced.append(emitted)
        return emit_carry

    ctx_size = lax.axis_size("ctx")
    move, shift = device_move, device_shift
    distance = 1
    while distance < ctx_size:
        if 2 * distance < ctx_size:
            sent = jnp.stack([move, shift]).astype(jnp.bfloat16)
            both_in = passed_along(sent, "ctx", distance).astype(jnp.float32)
            next_shift = matmul_heads(move, both_in[1]) + shift
            next_move = matmul_heads(move, both_in[0])
        else:
            shift_in = passed_along(shift.astype(jnp.bfloat16), "ctx", distance)
            next_shift = matmul_heads(move, shift_in.astype(jnp.float32)) + shift
            next_move = move
        if len(produced) < span_count:
            emit_carry = run_emit(emit_carry)
            next_shift, next_move, emit_carry = lax.optimization_barrier(
                (next_shift, next_move, emit_carry)
            )
        move, shift = next_move, next_shift
        distance *= 2
    while len(produced) < span_count:
        emit_carry = run_emit(emit_carry)
    local_outputs = token_major([emitted[0] for emitted in produced])
    start_queries = token_major([emitted[1] for emitted in produced])
    start_state = passed_along(shift.astype(jnp.bfloat16), "ctx", 1).astype(jnp.float32)
    kda_core = finish_spans(start_state, local_outputs, start_queries)
    partial_proj = jnp.dot(kda_core, kda_out_weight, preferred_element_type=jnp.float32)
    stream_out = stream_after_head_sum(partial_proj, residual)
    normed, latent = prepare(stream_out, norm_gain, latent_weight, latent_gain)
    mla_query = jnp.dot(normed, query_weight, preferred_element_type=jnp.float32).astype(
        jnp.bfloat16
    )
    query_heads = mla_query.reshape(length, -1, DH)
    heads_mla = query_heads.shape[1]
    my_first = lax.axis_index("ctx") * length
    query_positions = my_first + jnp.arange(length, dtype=jnp.int32)
    piece = gathered_earlier(latent)
    piece_rows = piece.shape[0]
    up_heads = up_weight.reshape(up_weight.shape[0], 2, heads_mla, DH)
    key_rows = jnp.einsum(
        "kl,lhd->hkd", piece, up_heads[:, 0], preferred_element_type=jnp.float32
    ).astype(jnp.bfloat16)
    value_rows = jnp.einsum(
        "kl,lhd->hkd", piece, up_heads[:, 1], preferred_element_type=jnp.float32
    ).astype(jnp.bfloat16)
    scores = jnp.einsum(
        "qhd,hkd->hqk", query_heads, key_rows, preferred_element_type=jnp.float32
    ) * DH ** (-0.5)
    key_positions = jnp.arange(piece_rows, dtype=jnp.int32)
    allowed = key_positions[None, :] <= query_positions[:, None]
    final_peak = jnp.max(jnp.where(allowed, scores, -1e30), axis=-1)
    weights = jnp.where(allowed, jnp.exp(scores - final_peak[..., None]), 0.0)
    final_total = jnp.sum(weights, axis=-1)
    final_mixed = jnp.einsum(
        "hqk,hkd->hqd",
        weights.astype(jnp.bfloat16),
        value_rows,
        preferred_element_type=jnp.float32,
    )
    attention_out = (
        (final_mixed / final_total[..., None])
        .transpose(1, 0, 2)
        .reshape(length, heads_mla * DH)
        .astype(jnp.bfloat16)
    )
    return (stream_out, attention_out)


def solution(mesh):
    in_specs = (
        P(None, "ctx", "head"),
        P("ctx", "head"),
        P("ctx", "head"),
        P(None, None, "head"),
        P("head", None),
        P("ctx", None),
        P(),
        P(),
        P(),
        P(None, "head"),
        P(None, None, "head"),
    )
    out_specs = (P("ctx", None), P("ctx", "head"))
    return jax.shard_map(
        per_device, mesh=mesh, in_specs=in_specs, out_specs=out_specs, check_vma=False
    )
```

```python
import math

import jax
import jax.numpy as jnp
from jax import lax
from jax.sharding import PartitionSpec as P
from jax.experimental import pallas as pl
from jax.experimental.pallas import tpu as pltpu

DK = 128
CONV = 4
DH = 128


eps_norm = 1e-06
highest_precision = lax.Precision.HIGHEST


def passed_along(block, axis, distance):
    devices = range(lax.axis_size(axis))
    route = [(i - distance, i) for i in devices if i - distance in devices]
    return lax.ppermute(block, axis, route)


def stream_after_head_sum(partial, residual):
    size = lax.axis_size("head")
    core = lax.axis_index("head") % 2
    half = partial.shape[0] // 2
    pair_route = [(i, i ^ 1) for i in range(size)]
    chip_route = [(i, i ^ 2) for i in range(size)]
    kept = lax.dynamic_slice_in_dim(partial, core * half, half)
    given = lax.dynamic_slice_in_dim(partial, (1 - core) * half, half)
    pair_sum = kept + lax.ppermute(given, "head", pair_route)
    pair_rounded = lax.optimization_barrier(pair_sum.astype(jnp.bfloat16))
    partner_rounded = lax.ppermute(pair_rounded, "head", chip_route)
    total = pair_rounded.astype(jnp.float32) + partner_rounded.astype(jnp.float32)
    my_rows = lax.dynamic_slice_in_dim(residual, core * half, half)
    stream_half = (my_rows.astype(jnp.float32) + total).astype(jnp.bfloat16)
    other_half = lax.ppermute(stream_half, "head", pair_route)
    return jnp.where(
        core == 0,
        jnp.concatenate([stream_half, other_half], axis=0),
        jnp.concatenate([other_half, stream_half], axis=0),
    )


def gather_kernel(block_ref, out_ref, send_sems, recv_sems, forward_sems):
    me = lax.axis_index("ctx")
    head = lax.axis_index("head")
    core = head % 2
    sibling = head + 1 - 2 * core
    count = out_ref.shape[0]
    out_ref[me] = block_ref[...]

    def outgoing(peer):
        return pltpu.make_async_remote_copy(
            src_ref=block_ref,
            dst_ref=out_ref.at[me],
            send_sem=send_sems.at[peer],
            recv_sem=recv_sems.at[me],
            device_id={"ctx": peer, "head": head},
            device_id_type=pl.DeviceIdType.MESH,
        )

    def forwarded(origin):
        return pltpu.make_async_remote_copy(
            src_ref=out_ref.at[origin],
            dst_ref=out_ref.at[origin],
            send_sem=forward_sems.at[origin],
            recv_sem=recv_sems.at[origin],
            device_id={"ctx": me, "head": sibling},
            device_id_type=pl.DeviceIdType.MESH,
        )

    @pl.loop(me + 1, count)
    def _(peer):
        @pl.when((peer + me) % 2 == core)
        def _():
            outgoing(peer).start()

    @pl.loop(me + 1, count)
    def _(peer):
        out_ref[peer] = jnp.zeros(block_ref.shape, block_ref.dtype)

    @pl.loop(0, me)
    def _(step):
        origin = me - 1 - step

        @pl.when((origin + me) % 2 == core)
        def _():
            forwarded(origin).wait_recv()
            forwarded(origin).start()

    @pl.loop(0, me)
    def _(step):
        origin = me - 1 - step

        @pl.when((origin + me) % 2 != core)
        def _():
            forwarded(origin).wait_recv()

    @pl.loop(me + 1, count)
    def _(peer):
        @pl.when((peer + me) % 2 == core)
        def _():
            outgoing(peer).wait_send()

    @pl.loop(0, me)
    def _(origin):
        @pl.when((origin + me) % 2 == core)
        def _():
            forwarded(origin).wait_send()


def gathered_earlier(block):
    count = lax.axis_size("ctx")
    rows, width = block.shape
    stacked = pl.pallas_call(
        gather_kernel,
        out_shape=jax.ShapeDtypeStruct((count, rows, width), block.dtype),
        in_specs=[pl.BlockSpec(memory_space=pltpu.VMEM)],
        out_specs=pl.BlockSpec(memory_space=pltpu.VMEM),
        scratch_shapes=[pltpu.SemaphoreType.DMA((count,))] * 3,
        compiler_params=pltpu.CompilerParams(has_side_effects=True),
    )(block)
    return stacked.reshape(count * rows, width)


def rounded(values):
    return lax.optimization_barrier(values.astype(jnp.bfloat16))


def unit_heads(activated):
    grouped = activated.reshape(activated.shape[0], -1, DK)
    scaled = grouped * lax.rsqrt(jnp.sum(grouped * grouped, axis=-1, keepdims=True) + eps_norm)
    return scaled.reshape(activated.shape)


def prepare(stream, norm_gain, latent_weight, latent_gain):
    widened = stream.astype(jnp.float32)
    normed = (
        widened
        * lax.rsqrt(jnp.mean(widened * widened, axis=-1, keepdims=True) + eps_norm)
        * norm_gain
    ).astype(jnp.bfloat16)
    latent_pre = jnp.dot(normed, latent_weight, preferred_element_type=jnp.float32)
    latent = (
        latent_pre
        * lax.rsqrt(jnp.mean(latent_pre * latent_pre, axis=-1, keepdims=True) + eps_norm)
        * latent_gain
    ).astype(jnp.bfloat16)
    return (normed, latent)


def span_layout(values, span_rows):
    length, channel_count = values.shape
    return values.reshape(length // span_rows, span_rows, channel_count // DK, DK).transpose(
        0, 2, 1, 3
    )


def matmul_heads(left, right):
    return jnp.einsum("hij,hjk->hik", left, right, precision=highest_precision)


def matmul_batched(left, right):
    return jnp.einsum("...ij,...jk->...ik", left, right, precision=highest_precision)


def unit_lower_inverse(system):
    size = system.shape[-1]
    rows = jnp.arange(size)[:, None]
    cols = jnp.arange(size)[None, :]
    first_below = (rows // 2 == cols // 2) & (rows != cols)
    inverse = jnp.eye(size, dtype=system.dtype) - jnp.where(first_below, system, 0.0)
    width = 2
    while width < size:
        below = (rows // (2 * width) == cols // (2 * width)) & (rows // width != cols // width)
        off_block = jnp.where(below, system, 0.0)
        correction = matmul_batched(matmul_batched(inverse, off_block), inverse)
        inverse = inverse - lax.optimization_barrier(correction)
        width *= 2
    return inverse


def delta_rule(kda_query, kda_key, kda_value, gate_log, beta):
    span_rows = 32
    length, channel_count = gate_log.shape
    heads = channel_count // DK
    queries = span_layout(kda_query.astype(jnp.float32), span_rows)
    keys_unit = span_layout(kda_key.astype(jnp.float32), span_rows)
    values_new = span_layout(kda_value.astype(jnp.float32), span_rows)
    inclusive_ones = jnp.tril(jnp.ones((span_rows, span_rows), jnp.float32))
    cumulative = jnp.einsum(
        "ts,nhsc->nhtc", inclusive_ones, span_layout(gate_log, span_rows), precision=highest_precision
    )
    rates = beta.reshape(length // span_rows, span_rows, heads).transpose(0, 2, 1)[..., None]
    growth = jnp.exp(cumulative)
    final_log = cumulative[:, :, -1:, :]
    keys_grown = keys_unit * growth
    keys_shrunk = keys_unit * jnp.exp(-cumulative)
    queries_grown = queries * growth
    keys_final = keys_unit * jnp.exp(final_log - cumulative)
    strict = jnp.tril(jnp.ones((span_rows, span_rows), jnp.float32), -1)
    inclusive = jnp.tril(jnp.ones((span_rows, span_rows), jnp.float32))
    coupling = (
        jnp.einsum("nhtc,nhsc->nhts", keys_grown, keys_shrunk, precision=highest_precision)
        * jnp.swapaxes(rates, -1, -2)
        * strict
    )
    system = coupling + jnp.eye(span_rows, dtype=jnp.float32)
    solved = matmul_batched(
        unit_lower_inverse(system), jnp.concatenate([values_new, keys_grown], axis=-1)
    )
    fresh = solved[..., :DK] * rates
    carried = solved[..., DK:] * rates
    eye_key = jnp.eye(DK, dtype=jnp.float32)
    transition = jnp.exp(final_log[:, :, 0, :])[..., :, None] * eye_key - jnp.einsum(
        "nhsk,nhsv->nhkv", keys_final, carried, precision=highest_precision
    )
    offset = jnp.einsum("nhsk,nhsv->nhkv", keys_final, fresh, precision=highest_precision)
    mixing = (
        jnp.einsum("nhtc,nhsc->nhts", queries_grown, keys_shrunk, precision=highest_precision)
        * inclusive
    )

    moves, shifts = transition, offset
    while moves.shape[0] > 1:
        later_moves, earlier_moves = moves[1::2], moves[0::2]
        shifts = matmul_batched(later_moves, shifts[0::2]) + shifts[1::2]
        moves = matmul_batched(later_moves, earlier_moves)
    device_move, device_shift = moves[0], shifts[0]
    return (device_move, device_shift, (transition, offset, fresh, carried, queries_grown, mixing))


def emit_step(carried_parts, span_parts):
    recurrent_state, accumulated_move = carried_parts
    span_move, span_shift, fresh_state_term, carried_state_term, query_term, mixing_part = (
        span_parts
    )
    state_update = fresh_state_term - jnp.einsum(
        "orm,omj->orj", carried_state_term, recurrent_state, precision=highest_precision
    )
    produced_output = jnp.einsum(
        "fmb,fbi->fmi", query_term, recurrent_state, precision=highest_precision
    ) + jnp.einsum("hts,hsv->htv", mixing_part, state_update, precision=highest_precision)
    start_weight = query_term - jnp.einsum(
        "hts,hsv->htv", mixing_part, carried_state_term, precision=highest_precision
    )
    start_query = matmul_heads(start_weight, accumulated_move)
    next_parts = (
        matmul_heads(span_move, recurrent_state) + span_shift,
        matmul_heads(span_move, accumulated_move),
    )
    return (next_parts, (produced_output, start_query))


def token_major(span_values):
    stacked = jnp.stack(span_values)
    block_count, heads, span_rows, _ = stacked.shape
    return stacked.transpose(1, 0, 2, 3).reshape(heads, block_count * span_rows, DK)


def finish_spans(start_state, local_outputs, start_queries):
    outputs = local_outputs + matmul_heads(start_queries, start_state)
    heads, length, _ = outputs.shape
    return outputs.transpose(1, 0, 2).reshape(length, heads * DK).astype(jnp.bfloat16)


def per_device(
    kda_inputs,
    gate_log,
    beta,
    conv_weight,
    kda_out_weight,
    residual,
    norm_gain,
    latent_weight,
    latent_gain,
    query_weight,
    up_weight,
):
    length = residual.shape[0]
    edge_rows = kda_inputs[:, length - (CONV - 1) :, :]
    earlier_rows = passed_along(edge_rows, "ctx", 1)
    extended = jnp.concatenate([earlier_rows, kda_inputs], axis=1).astype(jnp.float32)
    running = jnp.zeros(kda_inputs.shape, jnp.float32)
    for tap_index in range(CONV):
        running = (
            running
            + conv_weight[:, tap_index, None, :] * extended[:, tap_index : tap_index + length, :]
        )
    activated = jax.nn.silu(running)
    kda_query = rounded(unit_heads(activated[0]) * DK ** (-0.5))
    kda_key = rounded(unit_heads(activated[1]))
    kda_value = rounded(activated[2])
    device_move, device_shift, span_data = delta_rule(kda_query, kda_key, kda_value, gate_log, beta)
    heads = device_move.shape[0]
    span_count = span_data[0].shape[0]
    emit_carry = (
        jnp.zeros((heads, DK, DK), jnp.float32),
        jnp.broadcast_to(jnp.eye(DK, dtype=jnp.float32), (heads, DK, DK)),
    )
    produced = []

    def run_emit(emit_carry):
        span_index = len(produced)
        emit_carry, emitted = emit_step(emit_carry, tuple(part[span_index] for part in span_data))
        produced.append(emitted)
        return emit_carry

    ctx_size = lax.axis_size("ctx")
    move, shift = device_move, device_shift
    distance = 1
    while distance < ctx_size:
        if 2 * distance < ctx_size:
            sent = jnp.stack([move, shift]).astype(jnp.bfloat16)
            both_in = passed_along(sent, "ctx", distance).astype(jnp.float32)
            next_shift = matmul_heads(move, both_in[1]) + shift
            next_move = matmul_heads(move, both_in[0])
        else:
            shift_in = passed_along(shift.astype(jnp.bfloat16), "ctx", distance)
            next_shift = matmul_heads(move, shift_in.astype(jnp.float32)) + shift
            next_move = move
        if len(produced) < span_count:
            emit_carry = run_emit(emit_carry)
            next_shift, next_move, emit_carry = lax.optimization_barrier(
                (next_shift, next_move, emit_carry)
            )
        move, shift = next_move, next_shift
        distance *= 2
    while len(produced) < span_count:
        emit_carry = run_emit(emit_carry)
    local_outputs = token_major([emitted[0] for emitted in produced])
    start_queries = token_major([emitted[1] for emitted in produced])
    start_state = passed_along(shift.astype(jnp.bfloat16), "ctx", 1).astype(jnp.float32)
    kda_core = finish_spans(start_state, local_outputs, start_queries)
    partial_proj = jnp.dot(kda_core, kda_out_weight, preferred_element_type=jnp.float32)
    stream_out = stream_after_head_sum(partial_proj, residual)
    normed, latent = prepare(stream_out, norm_gain, latent_weight, latent_gain)
    mla_query = jnp.dot(normed, query_weight, preferred_element_type=jnp.float32).astype(
        jnp.bfloat16
    )
    query_heads = mla_query.reshape(length, -1, DH)
    heads_mla = query_heads.shape[1]
    flat_up = up_weight.reshape(up_weight.shape[0], -1)
    my_first = lax.axis_index("ctx") * length
    query_positions = my_first + jnp.arange(length, dtype=jnp.int32)
    piece = gathered_earlier(latent)
    piece_rows = piece.shape[0]
    paired = (
        jnp.dot(piece, flat_up, preferred_element_type=jnp.float32)
        .astype(jnp.bfloat16)
        .reshape(piece_rows, 2, heads_mla, DH)
    )
    scores = jnp.einsum(
        "qhd,khd->hqk", query_heads, paired[:, 0], preferred_element_type=jnp.float32
    ) * DH ** (-0.5)
    key_positions = jnp.arange(piece_rows, dtype=jnp.int32)
    allowed = key_positions[None, :] <= query_positions[:, None]
    final_peak = jnp.max(jnp.where(allowed, scores, -1e30), axis=-1)
    weights = jnp.where(allowed, jnp.exp(scores - final_peak[..., None]), 0.0)
    final_total = jnp.sum(weights, axis=-1)
    final_mixed = jnp.einsum(
        "hqk,khd->hqd",
        weights.astype(jnp.bfloat16),
        paired[:, 1],
        preferred_element_type=jnp.float32,
    )
    attention_out = (
        (final_mixed / final_total[..., None])
        .transpose(1, 0, 2)
        .reshape(length, heads_mla * DH)
        .astype(jnp.bfloat16)
    )
    return (stream_out, attention_out)


def solution(mesh):
    in_specs = (
        P(None, "ctx", "head"),
        P("ctx", "head"),
        P("ctx", "head"),
        P(None, None, "head"),
        P("head", None),
        P("ctx", None),
        P(),
        P(),
        P(),
        P(None, "head"),
        P(None, None, "head"),
    )
    out_specs = (P("ctx", None), P("ctx", "head"))
    return jax.shard_map(
        per_device, mesh=mesh, in_specs=in_specs, out_specs=out_specs, check_vma=False
    )
```

```python
import math

import jax
import jax.numpy as jnp
from jax import lax
from jax.sharding import PartitionSpec as P
from jax.experimental import pallas as pl
from jax.experimental.pallas import tpu as pltpu

DK = 128
CONV = 4
DH = 128


eps_norm = 1e-06
highest_precision = lax.Precision.HIGHEST


def passed_along(block, axis, distance):
    devices = range(lax.axis_size(axis))
    route = [(i - distance, i) for i in devices if i - distance in devices]
    return lax.ppermute(block, axis, route)


def stream_after_head_sum(partial, residual):
    size = lax.axis_size("head")
    core = lax.axis_index("head") % 2
    half = partial.shape[0] // 2
    pair_route = [(i, i ^ 1) for i in range(size)]
    chip_route = [(i, i ^ 2) for i in range(size)]
    kept = lax.dynamic_slice_in_dim(partial, core * half, half)
    given = lax.dynamic_slice_in_dim(partial, (1 - core) * half, half)
    pair_sum = kept + lax.ppermute(given, "head", pair_route)
    pair_rounded = lax.optimization_barrier(pair_sum.astype(jnp.bfloat16))
    partner_rounded = lax.ppermute(pair_rounded, "head", chip_route)
    total = pair_rounded.astype(jnp.float32) + partner_rounded.astype(jnp.float32)
    my_rows = lax.dynamic_slice_in_dim(residual, core * half, half)
    stream_half = (my_rows.astype(jnp.float32) + total).astype(jnp.bfloat16)
    other_half = lax.ppermute(stream_half, "head", pair_route)
    return jnp.where(
        core == 0,
        jnp.concatenate([stream_half, other_half], axis=0),
        jnp.concatenate([other_half, stream_half], axis=0),
    )


def gather_kernel(block_ref, out_ref, send_sems, recv_sems, forward_sems):
    me = lax.axis_index("ctx")
    head = lax.axis_index("head")
    core = head % 2
    sibling = head + 1 - 2 * core
    count = out_ref.shape[0]
    out_ref[me] = block_ref[...]

    def outgoing(peer):
        return pltpu.make_async_remote_copy(
            src_ref=block_ref,
            dst_ref=out_ref.at[me],
            send_sem=send_sems.at[peer],
            recv_sem=recv_sems.at[me],
            device_id={"ctx": peer, "head": head},
            device_id_type=pl.DeviceIdType.MESH,
        )

    def forwarded(origin):
        return pltpu.make_async_remote_copy(
            src_ref=out_ref.at[origin],
            dst_ref=out_ref.at[origin],
            send_sem=forward_sems.at[origin],
            recv_sem=recv_sems.at[origin],
            device_id={"ctx": me, "head": sibling},
            device_id_type=pl.DeviceIdType.MESH,
        )

    @pl.loop(me + 1, count)
    def _(peer):
        @pl.when((peer + me) % 2 == core)
        def _():
            outgoing(peer).start()

    @pl.loop(me + 1, count)
    def _(peer):
        out_ref[peer] = jnp.zeros(block_ref.shape, block_ref.dtype)

    @pl.loop(0, me)
    def _(step):
        origin = me - 1 - step

        @pl.when((origin + me) % 2 == core)
        def _():
            forwarded(origin).wait_recv()
            forwarded(origin).start()

    @pl.loop(0, me)
    def _(step):
        origin = me - 1 - step

        @pl.when((origin + me) % 2 != core)
        def _():
            forwarded(origin).wait_recv()

    @pl.loop(me + 1, count)
    def _(peer):
        @pl.when((peer + me) % 2 == core)
        def _():
            outgoing(peer).wait_send()

    @pl.loop(0, me)
    def _(origin):
        @pl.when((origin + me) % 2 == core)
        def _():
            forwarded(origin).wait_send()


def gathered_earlier(block):
    count = lax.axis_size("ctx")
    rows, width = block.shape
    stacked = pl.pallas_call(
        gather_kernel,
        out_shape=jax.ShapeDtypeStruct((count, rows, width), block.dtype),
        in_specs=[pl.BlockSpec(memory_space=pltpu.VMEM)],
        out_specs=pl.BlockSpec(memory_space=pltpu.VMEM),
        scratch_shapes=[pltpu.SemaphoreType.DMA((count,))] * 3,
        compiler_params=pltpu.CompilerParams(has_side_effects=True),
    )(block)
    return stacked.reshape(count * rows, width)


def rounded(values):
    return lax.optimization_barrier(values.astype(jnp.bfloat16))


def unit_heads(activated):
    grouped = activated.reshape(activated.shape[0], -1, DK)
    scaled = grouped * lax.rsqrt(jnp.sum(grouped * grouped, axis=-1, keepdims=True) + eps_norm)
    return scaled.reshape(activated.shape)


def prepare(stream, norm_gain, latent_weight, latent_gain):
    widened = stream.astype(jnp.float32)
    normed = (
        widened
        * lax.rsqrt(jnp.mean(widened * widened, axis=-1, keepdims=True) + eps_norm)
        * norm_gain
    ).astype(jnp.bfloat16)
    latent_pre = jnp.dot(normed, latent_weight, preferred_element_type=jnp.float32)
    latent = (
        latent_pre
        * lax.rsqrt(jnp.mean(latent_pre * latent_pre, axis=-1, keepdims=True) + eps_norm)
        * latent_gain
    ).astype(jnp.bfloat16)
    return (normed, latent)


def span_layout(values, span_rows):
    length, channel_count = values.shape
    return values.reshape(length // span_rows, span_rows, channel_count // DK, DK).transpose(
        0, 2, 1, 3
    )


def matmul_heads(left, right):
    return jnp.einsum("hij,hjk->hik", left, right, precision=highest_precision)


def matmul_batched(left, right):
    return jnp.einsum("...ij,...jk->...ik", left, right, precision=highest_precision)


def unit_lower_inverse(system):
    size = system.shape[-1]
    rows = jnp.arange(size)[:, None]
    cols = jnp.arange(size)[None, :]
    first_below = (rows // 2 == cols // 2) & (rows != cols)
    inverse = jnp.eye(size, dtype=system.dtype) - jnp.where(first_below, system, 0.0)
    width = 2
    while width < size:
        below = (rows // (2 * width) == cols // (2 * width)) & (rows // width != cols // width)
        off_block = jnp.where(below, system, 0.0)
        correction = matmul_batched(matmul_batched(inverse, off_block), inverse)
        inverse = inverse - lax.optimization_barrier(correction)
        width *= 2
    return inverse


def delta_rule(kda_query, kda_key, kda_value, gate_log, beta):
    span_rows = 32
    length, channel_count = gate_log.shape
    heads = channel_count // DK
    queries = span_layout(kda_query.astype(jnp.float32), span_rows)
    keys_unit = span_layout(kda_key.astype(jnp.float32), span_rows)
    values_new = span_layout(kda_value.astype(jnp.float32), span_rows)
    inclusive_ones = jnp.tril(jnp.ones((span_rows, span_rows), jnp.float32))
    cumulative = jnp.einsum(
        "ts,nhsc->nhtc", inclusive_ones, span_layout(gate_log, span_rows), precision=highest_precision
    )
    rates = beta.reshape(length // span_rows, span_rows, heads).transpose(0, 2, 1)[..., None]
    growth = jnp.exp(cumulative)
    final_log = cumulative[:, :, -1:, :]
    keys_grown = keys_unit * growth
    keys_shrunk = keys_unit * jnp.exp(-cumulative)
    queries_grown = queries * growth
    keys_final = keys_unit * jnp.exp(final_log - cumulative)
    strict = jnp.tril(jnp.ones((span_rows, span_rows), jnp.float32), -1)
    inclusive = jnp.tril(jnp.ones((span_rows, span_rows), jnp.float32))
    coupling = (
        jnp.einsum("nhtc,nhsc->nhts", keys_grown, keys_shrunk, precision=highest_precision)
        * jnp.swapaxes(rates, -1, -2)
        * strict
    )
    system = coupling + jnp.eye(span_rows, dtype=jnp.float32)
    solved = matmul_batched(
        unit_lower_inverse(system), jnp.concatenate([values_new, keys_grown], axis=-1)
    )
    fresh = solved[..., :DK] * rates
    carried = solved[..., DK:] * rates
    eye_key = jnp.eye(DK, dtype=jnp.float32)
    transition = jnp.exp(final_log[:, :, 0, :])[..., :, None] * eye_key - jnp.einsum(
        "nhsk,nhsv->nhkv", keys_final, carried, precision=highest_precision
    )
    offset = jnp.einsum("nhsk,nhsv->nhkv", keys_final, fresh, precision=highest_precision)
    mixing = (
        jnp.einsum("nhtc,nhsc->nhts", queries_grown, keys_shrunk, precision=highest_precision)
        * inclusive
    )

    moves, shifts = transition, offset
    while moves.shape[0] > 1:
        later_moves, earlier_moves = moves[1::2], moves[0::2]
        shifts = matmul_batched(later_moves, shifts[0::2]) + shifts[1::2]
        moves = matmul_batched(later_moves, earlier_moves)
    device_move, device_shift = moves[0], shifts[0]
    return (device_move, device_shift, (transition, offset, fresh, carried, queries_grown, mixing))


def emit_step(carried_parts, span_parts):
    recurrent_state, accumulated_move = carried_parts
    span_move, span_shift, fresh_state_term, carried_state_term, query_term, mixing_part = (
        span_parts
    )
    state_update = fresh_state_term - jnp.einsum(
        "orm,omj->orj", carried_state_term, recurrent_state, precision=highest_precision
    )
    produced_output = jnp.einsum(
        "fmb,fbi->fmi", query_term, recurrent_state, precision=highest_precision
    ) + jnp.einsum("hts,hsv->htv", mixing_part, state_update, precision=highest_precision)
    start_weight = query_term - jnp.einsum(
        "hts,hsv->htv", mixing_part, carried_state_term, precision=highest_precision
    )
    start_query = matmul_heads(start_weight, accumulated_move)
    next_parts = (
        matmul_heads(span_move, recurrent_state) + span_shift,
        matmul_heads(span_move, accumulated_move),
    )
    return (next_parts, (produced_output, start_query))


def token_major(span_values):
    stacked = jnp.stack(span_values)
    block_count, heads, span_rows, _ = stacked.shape
    return stacked.transpose(1, 0, 2, 3).reshape(heads, block_count * span_rows, DK)


def finish_spans(start_state, local_outputs, start_queries):
    outputs = local_outputs + matmul_heads(start_queries, start_state)
    heads, length, _ = outputs.shape
    return outputs.transpose(1, 0, 2).reshape(length, heads * DK).astype(jnp.bfloat16)


def per_device(
    kda_inputs,
    gate_log,
    beta,
    conv_weight,
    kda_out_weight,
    residual,
    norm_gain,
    latent_weight,
    latent_gain,
    query_weight,
    up_weight,
):
    length = residual.shape[0]
    edge_rows = kda_inputs[:, length - (CONV - 1) :, :]
    earlier_rows = passed_along(edge_rows, "ctx", 1)
    extended = jnp.concatenate([earlier_rows, kda_inputs], axis=1).astype(jnp.float32)
    running = jnp.zeros(kda_inputs.shape, jnp.float32)
    for tap_index in range(CONV):
        running = (
            running
            + conv_weight[:, tap_index, None, :] * extended[:, tap_index : tap_index + length, :]
        )
    activated = jax.nn.silu(running)
    kda_query = rounded(unit_heads(activated[0]) * DK ** (-0.5))
    kda_key = rounded(unit_heads(activated[1]))
    kda_value = rounded(activated[2])
    device_move, device_shift, span_data = delta_rule(kda_query, kda_key, kda_value, gate_log, beta)
    heads = device_move.shape[0]
    span_count = span_data[0].shape[0]
    emit_carry = (
        jnp.zeros((heads, DK, DK), jnp.float32),
        jnp.broadcast_to(jnp.eye(DK, dtype=jnp.float32), (heads, DK, DK)),
    )
    produced = []

    def run_emit(emit_carry):
        span_index = len(produced)
        emit_carry, emitted = emit_step(emit_carry, tuple(part[span_index] for part in span_data))
        produced.append(emitted)
        return emit_carry

    ctx_size = lax.axis_size("ctx")
    move, shift = device_move, device_shift
    distance = 1
    while 2 * distance < ctx_size:
        sent = jnp.stack([move, shift]).astype(jnp.bfloat16)
        both_in = passed_along(sent, "ctx", distance).astype(jnp.float32)
        next_shift = matmul_heads(move, both_in[1]) + shift
        next_move = matmul_heads(move, both_in[0])
        if len(produced) < span_count:
            emit_carry = run_emit(emit_carry)
            next_shift, next_move, emit_carry = lax.optimization_barrier(
                (next_shift, next_move, emit_carry)
            )
        move, shift = next_move, next_shift
        distance *= 2
    while len(produced) < span_count:
        emit_carry = run_emit(emit_carry)
    local_outputs = token_major([emitted[0] for emitted in produced])
    start_queries = token_major([emitted[1] for emitted in produced])
    previous = passed_along(jnp.stack([move, shift]).astype(jnp.bfloat16), "ctx", 1)
    farther = passed_along(shift.astype(jnp.bfloat16), "ctx", distance + 1)
    start_state = matmul_heads(
        previous[0].astype(jnp.float32), farther.astype(jnp.float32)
    ) + previous[1].astype(jnp.float32)
    kda_core = finish_spans(start_state, local_outputs, start_queries)
    partial_proj = jnp.dot(kda_core, kda_out_weight, preferred_element_type=jnp.float32)
    stream_out = stream_after_head_sum(partial_proj, residual)
    normed, latent = prepare(stream_out, norm_gain, latent_weight, latent_gain)
    mla_query = jnp.dot(normed, query_weight, preferred_element_type=jnp.float32).astype(
        jnp.bfloat16
    )
    query_heads = mla_query.reshape(length, -1, DH)
    heads_mla = query_heads.shape[1]
    flat_up = up_weight.reshape(up_weight.shape[0], -1)
    my_first = lax.axis_index("ctx") * length
    query_positions = my_first + jnp.arange(length, dtype=jnp.int32)
    piece = gathered_earlier(latent)
    piece_rows = piece.shape[0]
    paired = (
        jnp.dot(piece, flat_up, preferred_element_type=jnp.float32)
        .astype(jnp.bfloat16)
        .reshape(piece_rows, 2, heads_mla, DH)
    )
    scores = jnp.einsum(
        "qhd,khd->hqk", query_heads, paired[:, 0], preferred_element_type=jnp.float32
    ) * DH ** (-0.5)
    key_positions = jnp.arange(piece_rows, dtype=jnp.int32)
    allowed = key_positions[None, :] <= query_positions[:, None]
    final_peak = jnp.max(jnp.where(allowed, scores, -1e30), axis=-1)
    weights = jnp.where(allowed, jnp.exp(scores - final_peak[..., None]), 0.0)
    final_total = jnp.sum(weights, axis=-1)
    final_mixed = jnp.einsum(
        "hqk,khd->hqd",
        weights.astype(jnp.bfloat16),
        paired[:, 1],
        preferred_element_type=jnp.float32,
    )
    attention_out = (
        (final_mixed / final_total[..., None])
        .transpose(1, 0, 2)
        .reshape(length, heads_mla * DH)
        .astype(jnp.bfloat16)
    )
    return (stream_out, attention_out)


def solution(mesh):
    in_specs = (
        P(None, "ctx", "head"),
        P("ctx", "head"),
        P("ctx", "head"),
        P(None, None, "head"),
        P("head", None),
        P("ctx", None),
        P(),
        P(),
        P(),
        P(None, "head"),
        P(None, None, "head"),
    )
    out_specs = (P("ctx", None), P("ctx", "head"))
    return jax.shard_map(
        per_device, mesh=mesh, in_specs=in_specs, out_specs=out_specs, check_vma=False
    )
```

```python
import math

import jax
import jax.numpy as jnp
from jax import lax
from jax.sharding import PartitionSpec as P
from jax.experimental import pallas as pl
from jax.experimental.pallas import tpu as pltpu

DK = 128
CONV = 4
DH = 128


eps_norm = 1e-06
highest_precision = lax.Precision.HIGHEST


def passed_along(block, axis, distance):
    devices = range(lax.axis_size(axis))
    route = [(i - distance, i) for i in devices if i - distance in devices]
    return lax.ppermute(block, axis, route)


def stream_after_head_sum(partial, residual):
    size = lax.axis_size("head")
    core = lax.axis_index("head") % 2
    half = partial.shape[0] // 2
    pair_route = [(i, i ^ 1) for i in range(size)]
    chip_route = [(i, i ^ 2) for i in range(size)]
    kept = lax.dynamic_slice_in_dim(partial, core * half, half)
    given = lax.dynamic_slice_in_dim(partial, (1 - core) * half, half)
    pair_sum = kept + lax.ppermute(given, "head", pair_route)
    pair_rounded = lax.optimization_barrier(pair_sum.astype(jnp.bfloat16))
    partner_rounded = lax.ppermute(pair_rounded, "head", chip_route)
    total = pair_rounded.astype(jnp.float32) + partner_rounded.astype(jnp.float32)
    my_rows = lax.dynamic_slice_in_dim(residual, core * half, half)
    stream_half = (my_rows.astype(jnp.float32) + total).astype(jnp.bfloat16)
    other_half = lax.ppermute(stream_half, "head", pair_route)
    return jnp.where(
        core == 0,
        jnp.concatenate([stream_half, other_half], axis=0),
        jnp.concatenate([other_half, stream_half], axis=0),
    )


def gather_kernel(block_ref, out_ref, send_sems, recv_sems, forward_sems):
    me = lax.axis_index("ctx")
    head = lax.axis_index("head")
    core = head % 2
    sibling = head + 1 - 2 * core
    count = out_ref.shape[0]
    out_ref[me] = block_ref[...]

    def outgoing(peer):
        return pltpu.make_async_remote_copy(
            src_ref=block_ref,
            dst_ref=out_ref.at[me],
            send_sem=send_sems.at[peer],
            recv_sem=recv_sems.at[me],
            device_id={"ctx": peer, "head": head},
            device_id_type=pl.DeviceIdType.MESH,
        )

    def forwarded(origin):
        return pltpu.make_async_remote_copy(
            src_ref=out_ref.at[origin],
            dst_ref=out_ref.at[origin],
            send_sem=forward_sems.at[origin],
            recv_sem=recv_sems.at[origin],
            device_id={"ctx": me, "head": sibling},
            device_id_type=pl.DeviceIdType.MESH,
        )

    @pl.loop(me + 1, count)
    def _(peer):
        @pl.when((peer + me) % 2 == core)
        def _():
            outgoing(peer).start()

    @pl.loop(me + 1, count)
    def _(peer):
        out_ref[peer] = jnp.zeros(block_ref.shape, block_ref.dtype)

    @pl.loop(0, me)
    def _(step):
        origin = me - 1 - step

        @pl.when((origin + me) % 2 == core)
        def _():
            forwarded(origin).wait_recv()
            forwarded(origin).start()

    @pl.loop(0, me)
    def _(step):
        origin = me - 1 - step

        @pl.when((origin + me) % 2 != core)
        def _():
            forwarded(origin).wait_recv()

    @pl.loop(me + 1, count)
    def _(peer):
        @pl.when((peer + me) % 2 == core)
        def _():
            outgoing(peer).wait_send()

    @pl.loop(0, me)
    def _(origin):
        @pl.when((origin + me) % 2 == core)
        def _():
            forwarded(origin).wait_send()


def gathered_earlier(block):
    count = lax.axis_size("ctx")
    rows, width = block.shape
    stacked = pl.pallas_call(
        gather_kernel,
        out_shape=jax.ShapeDtypeStruct((count, rows, width), block.dtype),
        in_specs=[pl.BlockSpec(memory_space=pltpu.VMEM)],
        out_specs=pl.BlockSpec(memory_space=pltpu.VMEM),
        scratch_shapes=[pltpu.SemaphoreType.DMA((count,))] * 3,
        compiler_params=pltpu.CompilerParams(has_side_effects=True),
    )(block)
    return stacked.reshape(count * rows, width)


def rounded(values):
    return lax.optimization_barrier(values.astype(jnp.bfloat16))


def unit_heads(activated):
    grouped = activated.reshape(activated.shape[0], -1, DK)
    scaled = grouped * lax.rsqrt(jnp.sum(grouped * grouped, axis=-1, keepdims=True) + eps_norm)
    return scaled.reshape(activated.shape)


def prepare(stream, norm_gain, latent_weight, latent_gain):
    widened = stream.astype(jnp.float32)
    normed = (
        widened
        * lax.rsqrt(jnp.mean(widened * widened, axis=-1, keepdims=True) + eps_norm)
        * norm_gain
    ).astype(jnp.bfloat16)
    latent_pre = jnp.dot(normed, latent_weight, preferred_element_type=jnp.float32)
    latent = (
        latent_pre
        * lax.rsqrt(jnp.mean(latent_pre * latent_pre, axis=-1, keepdims=True) + eps_norm)
        * latent_gain
    ).astype(jnp.bfloat16)
    return (normed, latent)


def span_layout(values, span_rows):
    length, channel_count = values.shape
    return values.reshape(length // span_rows, span_rows, channel_count // DK, DK).transpose(
        0, 2, 1, 3
    )


def matmul_heads(left, right):
    return jnp.einsum("hij,hjk->hik", left, right, precision=highest_precision)


def matmul_batched(left, right):
    return jnp.einsum("...ij,...jk->...ik", left, right, precision=highest_precision)


def unit_lower_inverse(system):
    size = system.shape[-1]
    rows = jnp.arange(size)[:, None]
    cols = jnp.arange(size)[None, :]
    first_below = (rows // 2 == cols // 2) & (rows != cols)
    inverse = jnp.eye(size, dtype=system.dtype) - jnp.where(first_below, system, 0.0)
    width = 2
    while width < size:
        below = (rows // (2 * width) == cols // (2 * width)) & (rows // width != cols // width)
        off_block = jnp.where(below, system, 0.0)
        correction = matmul_batched(matmul_batched(inverse, off_block), inverse)
        inverse = inverse - lax.optimization_barrier(correction)
        width *= 2
    return inverse


def delta_rule(kda_query, kda_key, kda_value, gate_log, beta):
    span_rows = 32
    length, channel_count = gate_log.shape
    heads = channel_count // DK
    queries = span_layout(kda_query.astype(jnp.float32), span_rows)
    keys_unit = span_layout(kda_key.astype(jnp.float32), span_rows)
    values_new = span_layout(kda_value.astype(jnp.float32), span_rows)
    inclusive_ones = jnp.tril(jnp.ones((span_rows, span_rows), jnp.float32))
    cumulative = jnp.einsum(
        "ts,nhsc->nhtc", inclusive_ones, span_layout(gate_log, span_rows), precision=highest_precision
    )
    rates = beta.reshape(length // span_rows, span_rows, heads).transpose(0, 2, 1)[..., None]
    growth = jnp.exp(cumulative)
    final_log = cumulative[:, :, -1:, :]
    keys_grown = keys_unit * growth
    keys_shrunk = keys_unit * jnp.exp(-cumulative)
    queries_grown = queries * growth
    keys_final = keys_unit * jnp.exp(final_log - cumulative)
    strict = jnp.tril(jnp.ones((span_rows, span_rows), jnp.float32), -1)
    inclusive = jnp.tril(jnp.ones((span_rows, span_rows), jnp.float32))
    coupling = (
        jnp.einsum("nhtc,nhsc->nhts", keys_grown, keys_shrunk, precision=highest_precision)
        * jnp.swapaxes(rates, -1, -2)
        * strict
    )
    system = coupling + jnp.eye(span_rows, dtype=jnp.float32)
    solved = matmul_batched(
        unit_lower_inverse(system), jnp.concatenate([values_new, keys_grown], axis=-1)
    )
    fresh = solved[..., :DK] * rates
    carried = solved[..., DK:] * rates
    eye_key = jnp.eye(DK, dtype=jnp.float32)
    transition = jnp.exp(final_log[:, :, 0, :])[..., :, None] * eye_key - jnp.einsum(
        "nhsk,nhsv->nhkv", keys_final, carried, precision=highest_precision
    )
    offset = jnp.einsum("nhsk,nhsv->nhkv", keys_final, fresh, precision=highest_precision)
    mixing = (
        jnp.einsum("nhtc,nhsc->nhts", queries_grown, keys_shrunk, precision=highest_precision)
        * inclusive
    )

    moves, shifts = transition, offset
    while moves.shape[0] > 1:
        later_moves, earlier_moves = moves[1::2], moves[0::2]
        shifts = matmul_batched(later_moves, shifts[0::2]) + shifts[1::2]
        moves = matmul_batched(later_moves, earlier_moves)
    device_move, device_shift = moves[0], shifts[0]
    return (device_move, device_shift, (transition, offset, fresh, carried, queries_grown, mixing))


def emit_step(carried_parts, span_parts):
    recurrent_state, accumulated_move = carried_parts
    span_move, span_shift, fresh_state_term, carried_state_term, query_term, mixing_part = (
        span_parts
    )
    state_update = fresh_state_term - jnp.einsum(
        "orm,omj->orj", carried_state_term, recurrent_state, precision=highest_precision
    )
    produced_output = jnp.einsum(
        "fmb,fbi->fmi", query_term, recurrent_state, precision=highest_precision
    ) + jnp.einsum("hts,hsv->htv", mixing_part, state_update, precision=highest_precision)
    start_weight = query_term - jnp.einsum(
        "hts,hsv->htv", mixing_part, carried_state_term, precision=highest_precision
    )
    start_query = matmul_heads(start_weight, accumulated_move)
    next_parts = (
        matmul_heads(span_move, recurrent_state) + span_shift,
        matmul_heads(span_move, accumulated_move),
    )
    return (next_parts, (produced_output, start_query))


def token_major(span_values):
    stacked = jnp.stack(span_values)
    block_count, heads, span_rows, _ = stacked.shape
    return stacked.transpose(1, 0, 2, 3).reshape(heads, block_count * span_rows, DK)


def finish_spans(start_state, local_outputs, start_queries):
    outputs = local_outputs + matmul_heads(start_queries, start_state)
    heads, length, _ = outputs.shape
    return outputs.transpose(1, 0, 2).reshape(length, heads * DK).astype(jnp.bfloat16)


def per_device(
    kda_inputs,
    gate_log,
    beta,
    conv_weight,
    kda_out_weight,
    residual,
    norm_gain,
    latent_weight,
    latent_gain,
    query_weight,
    up_weight,
):
    length = residual.shape[0]
    edge_rows = kda_inputs[:, length - (CONV - 1) :, :]
    earlier_rows = passed_along(edge_rows, "ctx", 1)
    extended = jnp.concatenate([earlier_rows, kda_inputs], axis=1).astype(jnp.float32)
    running = jnp.zeros(kda_inputs.shape, jnp.float32)
    for tap_index in range(CONV):
        running = (
            running
            + conv_weight[:, tap_index, None, :] * extended[:, tap_index : tap_index + length, :]
        )
    activated = jax.nn.silu(running)
    kda_query = rounded(unit_heads(activated[0]) * DK ** (-0.5))
    kda_key = rounded(unit_heads(activated[1]))
    kda_value = rounded(activated[2])
    device_move, device_shift, span_data = delta_rule(kda_query, kda_key, kda_value, gate_log, beta)
    heads = device_move.shape[0]
    span_count = span_data[0].shape[0]
    emit_carry = (
        jnp.zeros((heads, DK, DK), jnp.float32),
        jnp.broadcast_to(jnp.eye(DK, dtype=jnp.float32), (heads, DK, DK)),
    )
    produced = []

    def run_emit(emit_carry):
        span_index = len(produced)
        emit_carry, emitted = emit_step(emit_carry, tuple(part[span_index] for part in span_data))
        produced.append(emitted)
        return emit_carry

    ctx_size = lax.axis_size("ctx")
    group_size = heads // 2
    moves = [device_move[:group_size], device_move[group_size:]]
    shifts = [device_shift[:group_size], device_shift[group_size:]]
    distance = 1
    while distance < ctx_size:
        for group in range(len(moves)):
            move, shift = moves[group], shifts[group]
            if 2 * distance < ctx_size:
                sent = jnp.stack([move, shift]).astype(jnp.bfloat16)
                both_in = passed_along(sent, "ctx", distance).astype(jnp.float32)
                next_shift = matmul_heads(move, both_in[1]) + shift
                next_move = matmul_heads(move, both_in[0])
            else:
                shift_in = passed_along(shift.astype(jnp.bfloat16), "ctx", distance)
                next_shift = matmul_heads(move, shift_in.astype(jnp.float32)) + shift
                next_move = move
            if group == 0 and len(produced) < span_count:
                emit_carry = run_emit(emit_carry)
                next_shift, next_move, emit_carry = lax.optimization_barrier(
                    (next_shift, next_move, emit_carry)
                )
            moves[group], shifts[group] = next_move, next_shift
        distance *= 2
    shift = jnp.concatenate(shifts, axis=0)
    while len(produced) < span_count:
        emit_carry = run_emit(emit_carry)
    local_outputs = token_major([emitted[0] for emitted in produced])
    start_queries = token_major([emitted[1] for emitted in produced])
    start_state = passed_along(shift.astype(jnp.bfloat16), "ctx", 1).astype(jnp.float32)
    kda_core = finish_spans(start_state, local_outputs, start_queries)
    partial_proj = jnp.dot(kda_core, kda_out_weight, preferred_element_type=jnp.float32)
    stream_out = stream_after_head_sum(partial_proj, residual)
    normed, latent = prepare(stream_out, norm_gain, latent_weight, latent_gain)
    mla_query = jnp.dot(normed, query_weight, preferred_element_type=jnp.float32).astype(
        jnp.bfloat16
    )
    query_heads = mla_query.reshape(length, -1, DH)
    heads_mla = query_heads.shape[1]
    flat_up = up_weight.reshape(up_weight.shape[0], -1)
    my_first = lax.axis_index("ctx") * length
    query_positions = my_first + jnp.arange(length, dtype=jnp.int32)
    piece = gathered_earlier(latent)
    piece_rows = piece.shape[0]
    paired = (
        jnp.dot(piece, flat_up, preferred_element_type=jnp.float32)
        .astype(jnp.bfloat16)
        .reshape(piece_rows, 2, heads_mla, DH)
    )
    scores = jnp.einsum(
        "qhd,khd->hqk", query_heads, paired[:, 0], preferred_element_type=jnp.float32
    ) * DH ** (-0.5)
    key_positions = jnp.arange(piece_rows, dtype=jnp.int32)
    allowed = key_positions[None, :] <= query_positions[:, None]
    final_peak = jnp.max(jnp.where(allowed, scores, -1e30), axis=-1)
    weights = jnp.where(allowed, jnp.exp(scores - final_peak[..., None]), 0.0)
    final_total = jnp.sum(weights, axis=-1)
    final_mixed = jnp.einsum(
        "hqk,khd->hqd",
        weights.astype(jnp.bfloat16),
        paired[:, 1],
        preferred_element_type=jnp.float32,
    )
    attention_out = (
        (final_mixed / final_total[..., None])
        .transpose(1, 0, 2)
        .reshape(length, heads_mla * DH)
        .astype(jnp.bfloat16)
    )
    return (stream_out, attention_out)


def solution(mesh):
    in_specs = (
        P(None, "ctx", "head"),
        P("ctx", "head"),
        P("ctx", "head"),
        P(None, None, "head"),
        P("head", None),
        P("ctx", None),
        P(),
        P(),
        P(),
        P(None, "head"),
        P(None, None, "head"),
    )
    out_specs = (P("ctx", None), P("ctx", "head"))
    return jax.shard_map(
        per_device, mesh=mesh, in_specs=in_specs, out_specs=out_specs, check_vma=False
    )
```

```python
import math

import jax
import jax.numpy as jnp
from jax import lax
from jax.sharding import PartitionSpec as P
from jax.experimental import pallas as pl
from jax.experimental.pallas import tpu as pltpu

DK = 128
CONV = 4
DH = 128


eps_norm = 1e-06
highest_precision = lax.Precision.HIGHEST


def passed_along(block, axis, distance):
    devices = range(lax.axis_size(axis))
    route = [(i - distance, i) for i in devices if i - distance in devices]
    return lax.ppermute(block, axis, route)


def stream_after_head_sum(partial, residual):
    size = lax.axis_size("head")
    core = lax.axis_index("head") % 2
    half = partial.shape[0] // 2
    pair_route = [(i, i ^ 1) for i in range(size)]
    chip_route = [(i, i ^ 2) for i in range(size)]
    kept = lax.dynamic_slice_in_dim(partial, core * half, half)
    given = lax.dynamic_slice_in_dim(partial, (1 - core) * half, half)
    pair_sum = kept + lax.ppermute(given, "head", pair_route)
    pair_rounded = lax.optimization_barrier(pair_sum.astype(jnp.bfloat16))
    partner_rounded = lax.ppermute(pair_rounded, "head", chip_route)
    total = pair_rounded.astype(jnp.float32) + partner_rounded.astype(jnp.float32)
    my_rows = lax.dynamic_slice_in_dim(residual, core * half, half)
    stream_half = (my_rows.astype(jnp.float32) + total).astype(jnp.bfloat16)
    other_half = lax.ppermute(stream_half, "head", pair_route)
    return jnp.where(
        core == 0,
        jnp.concatenate([stream_half, other_half], axis=0),
        jnp.concatenate([other_half, stream_half], axis=0),
    )


def gather_kernel(block_ref, out_ref, send_sems, recv_sems, forward_sems):
    me = lax.axis_index("ctx")
    head = lax.axis_index("head")
    core = head % 2
    sibling = head + 1 - 2 * core
    count = out_ref.shape[0]
    out_ref[me] = block_ref[...]

    def outgoing(peer):
        return pltpu.make_async_remote_copy(
            src_ref=block_ref,
            dst_ref=out_ref.at[me],
            send_sem=send_sems.at[peer],
            recv_sem=recv_sems.at[me],
            device_id={"ctx": peer, "head": head},
            device_id_type=pl.DeviceIdType.MESH,
        )

    def forwarded(origin):
        return pltpu.make_async_remote_copy(
            src_ref=out_ref.at[origin],
            dst_ref=out_ref.at[origin],
            send_sem=forward_sems.at[origin],
            recv_sem=recv_sems.at[origin],
            device_id={"ctx": me, "head": sibling},
            device_id_type=pl.DeviceIdType.MESH,
        )

    @pl.loop(me + 1, count)
    def _(peer):
        @pl.when((peer + me) % 2 == core)
        def _():
            outgoing(peer).start()

    @pl.loop(me + 1, count)
    def _(peer):
        out_ref[peer] = jnp.zeros(block_ref.shape, block_ref.dtype)

    @pl.loop(0, me)
    def _(step):
        origin = me - 1 - step

        @pl.when((origin + me) % 2 == core)
        def _():
            forwarded(origin).wait_recv()
            forwarded(origin).start()

    @pl.loop(0, me)
    def _(step):
        origin = me - 1 - step

        @pl.when((origin + me) % 2 != core)
        def _():
            forwarded(origin).wait_recv()

    @pl.loop(me + 1, count)
    def _(peer):
        @pl.when((peer + me) % 2 == core)
        def _():
            outgoing(peer).wait_send()

    @pl.loop(0, me)
    def _(origin):
        @pl.when((origin + me) % 2 == core)
        def _():
            forwarded(origin).wait_send()


def gathered_earlier(block):
    count = lax.axis_size("ctx")
    rows, width = block.shape
    stacked = pl.pallas_call(
        gather_kernel,
        out_shape=jax.ShapeDtypeStruct((count, rows, width), block.dtype),
        in_specs=[pl.BlockSpec(memory_space=pltpu.VMEM)],
        out_specs=pl.BlockSpec(memory_space=pltpu.VMEM),
        scratch_shapes=[pltpu.SemaphoreType.DMA((count,))] * 3,
        compiler_params=pltpu.CompilerParams(has_side_effects=True),
    )(block)
    return stacked.reshape(count * rows, width)


def rounded(values):
    return lax.optimization_barrier(values.astype(jnp.bfloat16))


def unit_heads(activated):
    grouped = activated.reshape(activated.shape[0], -1, DK)
    scaled = grouped * lax.rsqrt(jnp.sum(grouped * grouped, axis=-1, keepdims=True) + eps_norm)
    return scaled.reshape(activated.shape)


def prepare(stream, norm_gain, latent_weight, latent_gain):
    widened = stream.astype(jnp.float32)
    normed = (
        widened
        * lax.rsqrt(jnp.mean(widened * widened, axis=-1, keepdims=True) + eps_norm)
        * norm_gain
    ).astype(jnp.bfloat16)
    latent_pre = jnp.dot(normed, latent_weight, preferred_element_type=jnp.float32)
    latent = (
        latent_pre
        * lax.rsqrt(jnp.mean(latent_pre * latent_pre, axis=-1, keepdims=True) + eps_norm)
        * latent_gain
    ).astype(jnp.bfloat16)
    return (normed, latent)


def span_layout(values, span_rows):
    length, channel_count = values.shape
    return values.reshape(length // span_rows, span_rows, channel_count // DK, DK).transpose(
        0, 2, 1, 3
    )


def matmul_heads(left, right):
    return jnp.einsum("hij,hjk->hik", left, right, precision=highest_precision)


def matmul_batched(left, right):
    return jnp.einsum("...ij,...jk->...ik", left, right, precision=highest_precision)


def unit_lower_inverse(system):
    size = system.shape[-1]
    rows = jnp.arange(size)[:, None]
    cols = jnp.arange(size)[None, :]
    first_below = (rows // 2 == cols // 2) & (rows != cols)
    inverse = jnp.eye(size, dtype=system.dtype) - jnp.where(first_below, system, 0.0)
    width = 2
    while width < size:
        below = (rows // (2 * width) == cols // (2 * width)) & (rows // width != cols // width)
        off_block = jnp.where(below, system, 0.0)
        correction = matmul_batched(matmul_batched(inverse, off_block), inverse)
        inverse = inverse - lax.optimization_barrier(correction)
        width *= 2
    return inverse


def delta_rule(kda_query, kda_key, kda_value, gate_log, beta):
    span_rows = 32
    length, channel_count = gate_log.shape
    heads = channel_count // DK
    queries = span_layout(kda_query.astype(jnp.float32), span_rows)
    keys_unit = span_layout(kda_key.astype(jnp.float32), span_rows)
    values_new = span_layout(kda_value.astype(jnp.float32), span_rows)
    inclusive_ones = jnp.tril(jnp.ones((span_rows, span_rows), jnp.float32))
    cumulative = jnp.einsum(
        "ts,nhsc->nhtc", inclusive_ones, span_layout(gate_log, span_rows), precision=highest_precision
    )
    rates = beta.reshape(length // span_rows, span_rows, heads).transpose(0, 2, 1)[..., None]
    growth = jnp.exp(cumulative)
    final_log = cumulative[:, :, -1:, :]
    keys_grown = keys_unit * growth
    keys_shrunk = keys_unit * jnp.exp(-cumulative)
    queries_grown = queries * growth
    keys_final = keys_unit * jnp.exp(final_log - cumulative)
    strict = jnp.tril(jnp.ones((span_rows, span_rows), jnp.float32), -1)
    inclusive = jnp.tril(jnp.ones((span_rows, span_rows), jnp.float32))
    coupling = (
        jnp.einsum("nhtc,nhsc->nhts", keys_grown, keys_shrunk, precision=highest_precision)
        * jnp.swapaxes(rates, -1, -2)
        * strict
    )
    system = coupling + jnp.eye(span_rows, dtype=jnp.float32)
    solved = matmul_batched(
        unit_lower_inverse(system), jnp.concatenate([values_new, keys_grown], axis=-1)
    )
    fresh = solved[..., :DK] * rates
    carried = solved[..., DK:] * rates
    eye_key = jnp.eye(DK, dtype=jnp.float32)
    transition = jnp.exp(final_log[:, :, 0, :])[..., :, None] * eye_key - jnp.einsum(
        "nhsk,nhsv->nhkv", keys_final, carried, precision=highest_precision
    )
    offset = jnp.einsum("nhsk,nhsv->nhkv", keys_final, fresh, precision=highest_precision)
    mixing = (
        jnp.einsum("nhtc,nhsc->nhts", queries_grown, keys_shrunk, precision=highest_precision)
        * inclusive
    )

    moves, shifts = transition, offset
    while moves.shape[0] > 1:
        later_moves, earlier_moves = moves[1::2], moves[0::2]
        shifts = matmul_batched(later_moves, shifts[0::2]) + shifts[1::2]
        moves = matmul_batched(later_moves, earlier_moves)
    device_move, device_shift = moves[0], shifts[0]
    return (device_move, device_shift, (transition, offset, fresh, carried, queries_grown, mixing))


def emit_step(carried_parts, span_parts):
    recurrent_state, accumulated_move = carried_parts
    span_move, span_shift, fresh_state_term, carried_state_term, query_term, mixing_part = (
        span_parts
    )
    state_update = fresh_state_term - jnp.einsum(
        "orm,omj->orj", carried_state_term, recurrent_state, precision=highest_precision
    )
    produced_output = jnp.einsum(
        "fmb,fbi->fmi", query_term, recurrent_state, precision=highest_precision
    ) + jnp.einsum("hts,hsv->htv", mixing_part, state_update, precision=highest_precision)
    start_weight = query_term - jnp.einsum(
        "hts,hsv->htv", mixing_part, carried_state_term, precision=highest_precision
    )
    start_query = matmul_heads(start_weight, accumulated_move)
    next_parts = (
        matmul_heads(span_move, recurrent_state) + span_shift,
        matmul_heads(span_move, accumulated_move),
    )
    return (next_parts, (produced_output, start_query))


def token_major(span_values):
    stacked = jnp.stack(span_values)
    block_count, heads, span_rows, _ = stacked.shape
    return stacked.transpose(1, 0, 2, 3).reshape(heads, block_count * span_rows, DK)


def finish_spans(start_state, local_outputs, start_queries):
    outputs = local_outputs + matmul_heads(start_queries, start_state)
    heads, length, _ = outputs.shape
    return outputs.transpose(1, 0, 2).reshape(length, heads * DK).astype(jnp.bfloat16)


def per_device(
    kda_inputs,
    gate_log,
    beta,
    conv_weight,
    kda_out_weight,
    residual,
    norm_gain,
    latent_weight,
    latent_gain,
    query_weight,
    up_weight,
):
    length = residual.shape[0]
    edge_rows = kda_inputs[:, length - (CONV - 1) :, :]
    earlier_rows = passed_along(edge_rows, "ctx", 1)
    extended = jnp.concatenate([earlier_rows, kda_inputs], axis=1).astype(jnp.float32)
    running = jnp.zeros(kda_inputs.shape, jnp.float32)
    for tap_index in range(CONV):
        running = (
            running
            + conv_weight[:, tap_index, None, :] * extended[:, tap_index : tap_index + length, :]
        )
    activated = jax.nn.silu(running)
    kda_query = rounded(unit_heads(activated[0]) * DK ** (-0.5))
    kda_key = rounded(unit_heads(activated[1]))
    kda_value = rounded(activated[2])
    device_move, device_shift, span_data = delta_rule(kda_query, kda_key, kda_value, gate_log, beta)
    heads = device_move.shape[0]
    span_count = span_data[0].shape[0]
    emit_carry = (
        jnp.zeros((heads, DK, DK), jnp.float32),
        jnp.broadcast_to(jnp.eye(DK, dtype=jnp.float32), (heads, DK, DK)),
    )
    produced = []

    def run_emit(emit_carry):
        span_index = len(produced)
        emit_carry, emitted = emit_step(emit_carry, tuple(part[span_index] for part in span_data))
        produced.append(emitted)
        return emit_carry

    ctx_size = lax.axis_size("ctx")
    group_size = heads // 4
    starts = range(0, heads, group_size)
    moves = [device_move[first : first + group_size] for first in starts]
    shifts = [device_shift[first : first + group_size] for first in starts]
    distance = 1
    while distance < ctx_size:
        for group in range(len(moves)):
            move, shift = moves[group], shifts[group]
            if 2 * distance < ctx_size:
                sent = jnp.stack([move, shift]).astype(jnp.bfloat16)
                both_in = passed_along(sent, "ctx", distance).astype(jnp.float32)
                next_shift = matmul_heads(move, both_in[1]) + shift
                next_move = matmul_heads(move, both_in[0])
            else:
                shift_in = passed_along(shift.astype(jnp.bfloat16), "ctx", distance)
                next_shift = matmul_heads(move, shift_in.astype(jnp.float32)) + shift
                next_move = move
            if group == 0 and len(produced) < span_count:
                emit_carry = run_emit(emit_carry)
                next_shift, next_move, emit_carry = lax.optimization_barrier(
                    (next_shift, next_move, emit_carry)
                )
            moves[group], shifts[group] = next_move, next_shift
        distance *= 2
    shift = jnp.concatenate(shifts, axis=0)
    while len(produced) < span_count:
        emit_carry = run_emit(emit_carry)
    local_outputs = token_major([emitted[0] for emitted in produced])
    start_queries = token_major([emitted[1] for emitted in produced])
    start_state = passed_along(shift.astype(jnp.bfloat16), "ctx", 1).astype(jnp.float32)
    kda_core = finish_spans(start_state, local_outputs, start_queries)
    partial_proj = jnp.dot(kda_core, kda_out_weight, preferred_element_type=jnp.float32)
    stream_out = stream_after_head_sum(partial_proj, residual)
    normed, latent = prepare(stream_out, norm_gain, latent_weight, latent_gain)
    mla_query = jnp.dot(normed, query_weight, preferred_element_type=jnp.float32).astype(
        jnp.bfloat16
    )
    query_heads = mla_query.reshape(length, -1, DH)
    heads_mla = query_heads.shape[1]
    flat_up = up_weight.reshape(up_weight.shape[0], -1)
    my_first = lax.axis_index("ctx") * length
    query_positions = my_first + jnp.arange(length, dtype=jnp.int32)
    piece = gathered_earlier(latent)
    piece_rows = piece.shape[0]
    paired = (
        jnp.dot(piece, flat_up, preferred_element_type=jnp.float32)
        .astype(jnp.bfloat16)
        .reshape(piece_rows, 2, heads_mla, DH)
    )
    scores = jnp.einsum(
        "qhd,khd->hqk", query_heads, paired[:, 0], preferred_element_type=jnp.float32
    ) * DH ** (-0.5)
    key_positions = jnp.arange(piece_rows, dtype=jnp.int32)
    allowed = key_positions[None, :] <= query_positions[:, None]
    final_peak = jnp.max(jnp.where(allowed, scores, -1e30), axis=-1)
    weights = jnp.where(allowed, jnp.exp(scores - final_peak[..., None]), 0.0)
    final_total = jnp.sum(weights, axis=-1)
    final_mixed = jnp.einsum(
        "hqk,khd->hqd",
        weights.astype(jnp.bfloat16),
        paired[:, 1],
        preferred_element_type=jnp.float32,
    )
    attention_out = (
        (final_mixed / final_total[..., None])
        .transpose(1, 0, 2)
        .reshape(length, heads_mla * DH)
        .astype(jnp.bfloat16)
    )
    return (stream_out, attention_out)


def solution(mesh):
    in_specs = (
        P(None, "ctx", "head"),
        P("ctx", "head"),
        P("ctx", "head"),
        P(None, None, "head"),
        P("head", None),
        P("ctx", None),
        P(),
        P(),
        P(),
        P(None, "head"),
        P(None, None, "head"),
    )
    out_specs = (P("ctx", None), P("ctx", "head"))
    return jax.shard_map(
        per_device, mesh=mesh, in_specs=in_specs, out_specs=out_specs, check_vma=False
    )
```

```python
import math

import jax
import jax.numpy as jnp
from jax import lax
from jax.sharding import PartitionSpec as P
from jax.experimental import pallas as pl
from jax.experimental.pallas import tpu as pltpu

DK = 128
CONV = 4
DH = 128


eps_norm = 1e-06
highest_precision = lax.Precision.HIGHEST


def passed_along(block, axis, distance):
    devices = range(lax.axis_size(axis))
    route = [(i - distance, i) for i in devices if i - distance in devices]
    return lax.ppermute(block, axis, route)


def stream_after_head_sum(partial, residual):
    size = lax.axis_size("head")
    core = lax.axis_index("head") % 2
    half = partial.shape[0] // 2
    pair_route = [(i, i ^ 1) for i in range(size)]
    chip_route = [(i, i ^ 2) for i in range(size)]
    kept = lax.dynamic_slice_in_dim(partial, core * half, half)
    given = lax.dynamic_slice_in_dim(partial, (1 - core) * half, half)
    pair_sum = kept + lax.ppermute(given, "head", pair_route)
    pair_rounded = lax.optimization_barrier(pair_sum.astype(jnp.bfloat16))
    partner_rounded = lax.ppermute(pair_rounded, "head", chip_route)
    total = pair_rounded.astype(jnp.float32) + partner_rounded.astype(jnp.float32)
    my_rows = lax.dynamic_slice_in_dim(residual, core * half, half)
    stream_half = (my_rows.astype(jnp.float32) + total).astype(jnp.bfloat16)
    other_half = lax.ppermute(stream_half, "head", pair_route)
    return jnp.where(
        core == 0,
        jnp.concatenate([stream_half, other_half], axis=0),
        jnp.concatenate([other_half, stream_half], axis=0),
    )


def gather_kernel(block_ref, out_ref, send_sems, recv_sems, forward_sems):
    me = lax.axis_index("ctx")
    head = lax.axis_index("head")
    core = head % 2
    sibling = head + 1 - 2 * core
    count = out_ref.shape[0]
    out_ref[me] = block_ref[...]

    def outgoing(peer):
        return pltpu.make_async_remote_copy(
            src_ref=block_ref,
            dst_ref=out_ref.at[me],
            send_sem=send_sems.at[peer],
            recv_sem=recv_sems.at[me],
            device_id={"ctx": peer, "head": head},
            device_id_type=pl.DeviceIdType.MESH,
        )

    def forwarded(origin):
        return pltpu.make_async_remote_copy(
            src_ref=out_ref.at[origin],
            dst_ref=out_ref.at[origin],
            send_sem=forward_sems.at[origin],
            recv_sem=recv_sems.at[origin],
            device_id={"ctx": me, "head": sibling},
            device_id_type=pl.DeviceIdType.MESH,
        )

    @pl.loop(me + 1, count)
    def _(peer):
        @pl.when((peer + me) % 2 == core)
        def _():
            outgoing(peer).start()

    @pl.loop(me + 1, count)
    def _(peer):
        out_ref[peer] = jnp.zeros(block_ref.shape, block_ref.dtype)

    @pl.loop(0, me)
    def _(step):
        origin = me - 1 - step

        @pl.when((origin + me) % 2 == core)
        def _():
            forwarded(origin).wait_recv()
            forwarded(origin).start()

    @pl.loop(0, me)
    def _(step):
        origin = me - 1 - step

        @pl.when((origin + me) % 2 != core)
        def _():
            forwarded(origin).wait_recv()

    @pl.loop(me + 1, count)
    def _(peer):
        @pl.when((peer + me) % 2 == core)
        def _():
            outgoing(peer).wait_send()

    @pl.loop(0, me)
    def _(origin):
        @pl.when((origin + me) % 2 == core)
        def _():
            forwarded(origin).wait_send()


def gathered_earlier(block):
    count = lax.axis_size("ctx")
    rows, width = block.shape
    stacked = pl.pallas_call(
        gather_kernel,
        out_shape=jax.ShapeDtypeStruct((count, rows, width), block.dtype),
        in_specs=[pl.BlockSpec(memory_space=pltpu.VMEM)],
        out_specs=pl.BlockSpec(memory_space=pltpu.VMEM),
        scratch_shapes=[pltpu.SemaphoreType.DMA((count,))] * 3,
        compiler_params=pltpu.CompilerParams(has_side_effects=True),
    )(block)
    return stacked.reshape(count * rows, width)


def rounded(values):
    return lax.optimization_barrier(values.astype(jnp.bfloat16))


def unit_heads(activated):
    grouped = activated.reshape(activated.shape[0], -1, DK)
    scaled = grouped * lax.rsqrt(jnp.sum(grouped * grouped, axis=-1, keepdims=True) + eps_norm)
    return scaled.reshape(activated.shape)


def prepare(stream, norm_gain, latent_weight, latent_gain):
    widened = stream.astype(jnp.float32)
    normed = (
        widened
        * lax.rsqrt(jnp.mean(widened * widened, axis=-1, keepdims=True) + eps_norm)
        * norm_gain
    ).astype(jnp.bfloat16)
    latent_pre = jnp.dot(normed, latent_weight, preferred_element_type=jnp.float32)
    latent = (
        latent_pre
        * lax.rsqrt(jnp.mean(latent_pre * latent_pre, axis=-1, keepdims=True) + eps_norm)
        * latent_gain
    ).astype(jnp.bfloat16)
    return (normed, latent)


def span_layout(values, span_rows):
    length, channel_count = values.shape
    return values.reshape(length // span_rows, span_rows, channel_count // DK, DK).transpose(
        0, 2, 1, 3
    )


def matmul_heads(left, right):
    return jnp.einsum("hij,hjk->hik", left, right, precision=highest_precision)


def matmul_batched(left, right):
    return jnp.einsum("...ij,...jk->...ik", left, right, precision=highest_precision)


def unit_lower_inverse(system):
    size = system.shape[-1]
    rows = jnp.arange(size)[:, None]
    cols = jnp.arange(size)[None, :]
    first_below = (rows // 2 == cols // 2) & (rows != cols)
    inverse = jnp.eye(size, dtype=system.dtype) - jnp.where(first_below, system, 0.0)
    width = 2
    while width < size:
        below = (rows // (2 * width) == cols // (2 * width)) & (rows // width != cols // width)
        off_block = jnp.where(below, system, 0.0)
        correction = matmul_batched(matmul_batched(inverse, off_block), inverse)
        inverse = inverse - lax.optimization_barrier(correction)
        width *= 2
    return inverse


def delta_rule(kda_query, kda_key, kda_value, gate_log, beta):
    span_rows = 32
    length, channel_count = gate_log.shape
    heads = channel_count // DK
    queries = span_layout(kda_query.astype(jnp.float32), span_rows)
    keys_unit = span_layout(kda_key.astype(jnp.float32), span_rows)
    values_new = span_layout(kda_value.astype(jnp.float32), span_rows)
    inclusive_ones = jnp.tril(jnp.ones((span_rows, span_rows), jnp.float32))
    cumulative = jnp.einsum(
        "ts,nhsc->nhtc", inclusive_ones, span_layout(gate_log, span_rows), precision=highest_precision
    )
    rates = beta.reshape(length // span_rows, span_rows, heads).transpose(0, 2, 1)[..., None]
    growth = jnp.exp(cumulative)
    final_log = cumulative[:, :, -1:, :]
    keys_grown = keys_unit * growth
    keys_shrunk = keys_unit * jnp.exp(-cumulative)
    queries_grown = queries * growth
    keys_final = keys_unit * jnp.exp(final_log - cumulative)
    strict = jnp.tril(jnp.ones((span_rows, span_rows), jnp.float32), -1)
    inclusive = jnp.tril(jnp.ones((span_rows, span_rows), jnp.float32))
    coupling = (
        jnp.einsum("nhtc,nhsc->nhts", keys_grown, keys_shrunk, precision=highest_precision)
        * jnp.swapaxes(rates, -1, -2)
        * strict
    )
    system = coupling + jnp.eye(span_rows, dtype=jnp.float32)
    solved = matmul_batched(
        unit_lower_inverse(system), jnp.concatenate([values_new, keys_grown], axis=-1)
    )
    fresh = solved[..., :DK] * rates
    carried = solved[..., DK:] * rates
    eye_key = jnp.eye(DK, dtype=jnp.float32)
    transition = jnp.exp(final_log[:, :, 0, :])[..., :, None] * eye_key - jnp.einsum(
        "nhsk,nhsv->nhkv", keys_final, carried, precision=highest_precision
    )
    offset = jnp.einsum("nhsk,nhsv->nhkv", keys_final, fresh, precision=highest_precision)
    mixing = (
        jnp.einsum("nhtc,nhsc->nhts", queries_grown, keys_shrunk, precision=highest_precision)
        * inclusive
    )

    moves, shifts = transition, offset
    while moves.shape[0] > 1:
        later_moves, earlier_moves = moves[1::2], moves[0::2]
        shifts = matmul_batched(later_moves, shifts[0::2]) + shifts[1::2]
        moves = matmul_batched(later_moves, earlier_moves)
    device_move, device_shift = moves[0], shifts[0]
    return (device_move, device_shift, (transition, offset, fresh, carried, queries_grown, mixing))


def emit_step(carried_parts, span_parts):
    recurrent_state, accumulated_move = carried_parts
    span_move, span_shift, fresh_state_term, carried_state_term, query_term, mixing_part = (
        span_parts
    )
    state_update = fresh_state_term - jnp.einsum(
        "orm,omj->orj", carried_state_term, recurrent_state, precision=highest_precision
    )
    produced_output = jnp.einsum(
        "fmb,fbi->fmi", query_term, recurrent_state, precision=highest_precision
    ) + jnp.einsum("hts,hsv->htv", mixing_part, state_update, precision=highest_precision)
    start_weight = query_term - jnp.einsum(
        "hts,hsv->htv", mixing_part, carried_state_term, precision=highest_precision
    )
    start_query = matmul_heads(start_weight, accumulated_move)
    next_parts = (
        matmul_heads(span_move, recurrent_state) + span_shift,
        matmul_heads(span_move, accumulated_move),
    )
    return (next_parts, (produced_output, start_query))


def token_major(span_values):
    stacked = jnp.stack(span_values)
    block_count, heads, span_rows, _ = stacked.shape
    return stacked.transpose(1, 0, 2, 3).reshape(heads, block_count * span_rows, DK)


def finish_spans(start_state, local_outputs, start_queries):
    outputs = local_outputs + matmul_heads(start_queries, start_state)
    heads, length, _ = outputs.shape
    return outputs.transpose(1, 0, 2).reshape(length, heads * DK).astype(jnp.bfloat16)


def per_device(
    kda_inputs,
    gate_log,
    beta,
    conv_weight,
    kda_out_weight,
    residual,
    norm_gain,
    latent_weight,
    latent_gain,
    query_weight,
    up_weight,
):
    length = residual.shape[0]
    edge_rows = kda_inputs[:, length - (CONV - 1) :, :]
    earlier_rows = passed_along(edge_rows, "ctx", 1)
    extended = jnp.concatenate([earlier_rows, kda_inputs], axis=1).astype(jnp.float32)
    running = jnp.zeros(kda_inputs.shape, jnp.float32)
    for tap_index in range(CONV):
        running = (
            running
            + conv_weight[:, tap_index, None, :] * extended[:, tap_index : tap_index + length, :]
        )
    activated = jax.nn.silu(running)
    kda_query = rounded(unit_heads(activated[0]) * DK ** (-0.5))
    kda_key = rounded(unit_heads(activated[1]))
    kda_value = rounded(activated[2])
    device_move, device_shift, span_data = delta_rule(kda_query, kda_key, kda_value, gate_log, beta)
    heads = device_move.shape[0]
    span_count = span_data[0].shape[0]
    emit_carry = (
        jnp.zeros((heads, DK, DK), jnp.float32),
        jnp.broadcast_to(jnp.eye(DK, dtype=jnp.float32), (heads, DK, DK)),
    )
    produced = []

    def run_emit(emit_carry):
        span_index = len(produced)
        emit_carry, emitted = emit_step(emit_carry, tuple(part[span_index] for part in span_data))
        produced.append(emitted)
        return emit_carry

    ctx_size = lax.axis_size("ctx")
    group_size = heads // 2
    moves = [device_move[:group_size], device_move[group_size:]]
    shifts = [device_shift[:group_size], device_shift[group_size:]]
    distance = 1
    while distance < ctx_size:
        for group in range(len(moves)):
            move, shift = moves[group], shifts[group]
            if 2 * distance < ctx_size:
                sent = jnp.stack([move, shift]).astype(jnp.bfloat16)
                both_in = passed_along(sent, "ctx", distance).astype(jnp.float32)
                next_shift = matmul_heads(move, both_in[1]) + shift
                next_move = matmul_heads(move, both_in[0])
            else:
                shift_in = passed_along(shift.astype(jnp.bfloat16), "ctx", distance)
                next_shift = matmul_heads(move, shift_in.astype(jnp.float32)) + shift
                next_move = move
            if group == len(moves) - 1 and len(produced) < span_count:
                emit_carry = run_emit(emit_carry)
                next_shift, next_move, emit_carry = lax.optimization_barrier(
                    (next_shift, next_move, emit_carry)
                )
            moves[group], shifts[group] = next_move, next_shift
        distance *= 2
    shift = jnp.concatenate(shifts, axis=0)
    while len(produced) < span_count:
        emit_carry = run_emit(emit_carry)
    local_outputs = token_major([emitted[0] for emitted in produced])
    start_queries = token_major([emitted[1] for emitted in produced])
    start_state = passed_along(shift.astype(jnp.bfloat16), "ctx", 1).astype(jnp.float32)
    kda_core = finish_spans(start_state, local_outputs, start_queries)
    partial_proj = jnp.dot(kda_core, kda_out_weight, preferred_element_type=jnp.float32)
    stream_out = stream_after_head_sum(partial_proj, residual)
    normed, latent = prepare(stream_out, norm_gain, latent_weight, latent_gain)
    mla_query = jnp.dot(normed, query_weight, preferred_element_type=jnp.float32).astype(
        jnp.bfloat16
    )
    query_heads = mla_query.reshape(length, -1, DH)
    heads_mla = query_heads.shape[1]
    flat_up = up_weight.reshape(up_weight.shape[0], -1)
    my_first = lax.axis_index("ctx") * length
    query_positions = my_first + jnp.arange(length, dtype=jnp.int32)
    piece = gathered_earlier(latent)
    piece_rows = piece.shape[0]
    paired = (
        jnp.dot(piece, flat_up, preferred_element_type=jnp.float32)
        .astype(jnp.bfloat16)
        .reshape(piece_rows, 2, heads_mla, DH)
    )
    scores = jnp.einsum(
        "qhd,khd->hqk", query_heads, paired[:, 0], preferred_element_type=jnp.float32
    ) * DH ** (-0.5)
    key_positions = jnp.arange(piece_rows, dtype=jnp.int32)
    allowed = key_positions[None, :] <= query_positions[:, None]
    final_peak = jnp.max(jnp.where(allowed, scores, -1e30), axis=-1)
    weights = jnp.where(allowed, jnp.exp(scores - final_peak[..., None]), 0.0)
    final_total = jnp.sum(weights, axis=-1)
    final_mixed = jnp.einsum(
        "hqk,khd->hqd",
        weights.astype(jnp.bfloat16),
        paired[:, 1],
        preferred_element_type=jnp.float32,
    )
    attention_out = (
        (final_mixed / final_total[..., None])
        .transpose(1, 0, 2)
        .reshape(length, heads_mla * DH)
        .astype(jnp.bfloat16)
    )
    return (stream_out, attention_out)


def solution(mesh):
    in_specs = (
        P(None, "ctx", "head"),
        P("ctx", "head"),
        P("ctx", "head"),
        P(None, None, "head"),
        P("head", None),
        P("ctx", None),
        P(),
        P(),
        P(),
        P(None, "head"),
        P(None, None, "head"),
    )
    out_specs = (P("ctx", None), P("ctx", "head"))
    return jax.shard_map(
        per_device, mesh=mesh, in_specs=in_specs, out_specs=out_specs, check_vma=False
    )
```

```python
import math

import jax
import jax.numpy as jnp
from jax import lax
from jax.sharding import PartitionSpec as P
from jax.experimental import pallas as pl
from jax.experimental.pallas import tpu as pltpu

DK = 128
CONV = 4
DH = 128


eps_norm = 1e-06
highest_precision = lax.Precision.HIGHEST


def passed_along(block, axis, distance):
    devices = range(lax.axis_size(axis))
    route = [(i - distance, i) for i in devices if i - distance in devices]
    return lax.ppermute(block, axis, route)


def stream_after_head_sum(partial, residual):
    size = lax.axis_size("head")
    core = lax.axis_index("head") % 2
    half = partial.shape[0] // 2
    pair_route = [(i, i ^ 1) for i in range(size)]
    chip_route = [(i, i ^ 2) for i in range(size)]
    kept = lax.dynamic_slice_in_dim(partial, core * half, half)
    given = lax.dynamic_slice_in_dim(partial, (1 - core) * half, half)
    pair_sum = kept + lax.ppermute(given, "head", pair_route)
    pair_rounded = lax.optimization_barrier(pair_sum.astype(jnp.bfloat16))
    partner_rounded = lax.ppermute(pair_rounded, "head", chip_route)
    total = pair_rounded.astype(jnp.float32) + partner_rounded.astype(jnp.float32)
    my_rows = lax.dynamic_slice_in_dim(residual, core * half, half)
    stream_half = (my_rows.astype(jnp.float32) + total).astype(jnp.bfloat16)
    other_half = lax.ppermute(stream_half, "head", pair_route)
    return jnp.where(
        core == 0,
        jnp.concatenate([stream_half, other_half], axis=0),
        jnp.concatenate([other_half, stream_half], axis=0),
    )


def gather_kernel(block_ref, out_ref, send_sems, recv_sems, forward_sems):
    me = lax.axis_index("ctx")
    head = lax.axis_index("head")
    core = head % 2
    sibling = head + 1 - 2 * core
    count = out_ref.shape[0]
    out_ref[me] = block_ref[...]

    def outgoing(peer):
        return pltpu.make_async_remote_copy(
            src_ref=block_ref,
            dst_ref=out_ref.at[me],
            send_sem=send_sems.at[peer],
            recv_sem=recv_sems.at[me],
            device_id={"ctx": peer, "head": head},
            device_id_type=pl.DeviceIdType.MESH,
        )

    def forwarded(origin):
        return pltpu.make_async_remote_copy(
            src_ref=out_ref.at[origin],
            dst_ref=out_ref.at[origin],
            send_sem=forward_sems.at[origin],
            recv_sem=recv_sems.at[origin],
            device_id={"ctx": me, "head": sibling},
            device_id_type=pl.DeviceIdType.MESH,
        )

    @pl.loop(me + 1, count)
    def _(peer):
        @pl.when((peer + me) % 2 == core)
        def _():
            outgoing(peer).start()

    @pl.loop(me + 1, count)
    def _(peer):
        out_ref[peer] = jnp.zeros(block_ref.shape, block_ref.dtype)

    @pl.loop(0, me)
    def _(step):
        origin = me - 1 - step

        @pl.when((origin + me) % 2 == core)
        def _():
            forwarded(origin).wait_recv()
            forwarded(origin).start()

    @pl.loop(0, me)
    def _(step):
        origin = me - 1 - step

        @pl.when((origin + me) % 2 != core)
        def _():
            forwarded(origin).wait_recv()

    @pl.loop(me + 1, count)
    def _(peer):
        @pl.when((peer + me) % 2 == core)
        def _():
            outgoing(peer).wait_send()

    @pl.loop(0, me)
    def _(origin):
        @pl.when((origin + me) % 2 == core)
        def _():
            forwarded(origin).wait_send()


def gathered_earlier(block):
    count = lax.axis_size("ctx")
    rows, width = block.shape
    stacked = pl.pallas_call(
        gather_kernel,
        out_shape=jax.ShapeDtypeStruct((count, rows, width), block.dtype),
        in_specs=[pl.BlockSpec(memory_space=pltpu.VMEM)],
        out_specs=pl.BlockSpec(memory_space=pltpu.VMEM),
        scratch_shapes=[pltpu.SemaphoreType.DMA((count,))] * 3,
        compiler_params=pltpu.CompilerParams(has_side_effects=True),
    )(block)
    return stacked.reshape(count * rows, width)


def rounded(values):
    return lax.optimization_barrier(values.astype(jnp.bfloat16))


def unit_heads(activated):
    grouped = activated.reshape(activated.shape[0], -1, DK)
    scaled = grouped * lax.rsqrt(jnp.sum(grouped * grouped, axis=-1, keepdims=True) + eps_norm)
    return scaled.reshape(activated.shape)


def prepare(stream, norm_gain, latent_weight, latent_gain):
    widened = stream.astype(jnp.float32)
    normed = (
        widened
        * lax.rsqrt(jnp.mean(widened * widened, axis=-1, keepdims=True) + eps_norm)
        * norm_gain
    ).astype(jnp.bfloat16)
    latent_pre = jnp.dot(normed, latent_weight, preferred_element_type=jnp.float32)
    latent = (
        latent_pre
        * lax.rsqrt(jnp.mean(latent_pre * latent_pre, axis=-1, keepdims=True) + eps_norm)
        * latent_gain
    ).astype(jnp.bfloat16)
    return (normed, latent)


def span_layout(values, span_rows):
    length, channel_count = values.shape
    return values.reshape(length // span_rows, span_rows, channel_count // DK, DK).transpose(
        0, 2, 1, 3
    )


def matmul_heads(left, right):
    return jnp.einsum("hij,hjk->hik", left, right, precision=highest_precision)


def matmul_batched(left, right):
    return jnp.einsum("...ij,...jk->...ik", left, right, precision=highest_precision)


def unit_lower_inverse(system):
    size = system.shape[-1]
    rows = jnp.arange(size)[:, None]
    cols = jnp.arange(size)[None, :]
    first_below = (rows // 2 == cols // 2) & (rows != cols)
    inverse = jnp.eye(size, dtype=system.dtype) - jnp.where(first_below, system, 0.0)
    width = 2
    while width < size:
        below = (rows // (2 * width) == cols // (2 * width)) & (rows // width != cols // width)
        off_block = jnp.where(below, system, 0.0)
        correction = matmul_batched(matmul_batched(inverse, off_block), inverse)
        inverse = inverse - lax.optimization_barrier(correction)
        width *= 2
    return inverse


def delta_rule(kda_query, kda_key, kda_value, gate_log, beta):
    span_rows = 32
    length, channel_count = gate_log.shape
    heads = channel_count // DK
    queries = span_layout(kda_query.astype(jnp.float32), span_rows)
    keys_unit = span_layout(kda_key.astype(jnp.float32), span_rows)
    values_new = span_layout(kda_value.astype(jnp.float32), span_rows)
    inclusive_ones = jnp.tril(jnp.ones((span_rows, span_rows), jnp.float32))
    cumulative = jnp.einsum(
        "ts,nhsc->nhtc", inclusive_ones, span_layout(gate_log, span_rows), precision=highest_precision
    )
    rates = beta.reshape(length // span_rows, span_rows, heads).transpose(0, 2, 1)[..., None]
    growth = jnp.exp(cumulative)
    final_log = cumulative[:, :, -1:, :]
    keys_grown = keys_unit * growth
    keys_shrunk = keys_unit * jnp.exp(-cumulative)
    queries_grown = queries * growth
    keys_final = keys_unit * jnp.exp(final_log - cumulative)
    strict = jnp.tril(jnp.ones((span_rows, span_rows), jnp.float32), -1)
    inclusive = jnp.tril(jnp.ones((span_rows, span_rows), jnp.float32))
    coupling = (
        jnp.einsum("nhtc,nhsc->nhts", keys_grown, keys_shrunk, precision=highest_precision)
        * jnp.swapaxes(rates, -1, -2)
        * strict
    )
    system = coupling + jnp.eye(span_rows, dtype=jnp.float32)
    solved = matmul_batched(
        unit_lower_inverse(system), jnp.concatenate([values_new, keys_grown], axis=-1)
    )
    fresh = solved[..., :DK] * rates
    carried = solved[..., DK:] * rates
    eye_key = jnp.eye(DK, dtype=jnp.float32)
    transition = jnp.exp(final_log[:, :, 0, :])[..., :, None] * eye_key - jnp.einsum(
        "nhsk,nhsv->nhkv", keys_final, carried, precision=highest_precision
    )
    offset = jnp.einsum("nhsk,nhsv->nhkv", keys_final, fresh, precision=highest_precision)
    mixing = (
        jnp.einsum("nhtc,nhsc->nhts", queries_grown, keys_shrunk, precision=highest_precision)
        * inclusive
    )

    moves, shifts = transition, offset
    while moves.shape[0] > 1:
        later_moves, earlier_moves = moves[1::2], moves[0::2]
        shifts = matmul_batched(later_moves, shifts[0::2]) + shifts[1::2]
        moves = matmul_batched(later_moves, earlier_moves)
    device_move, device_shift = moves[0], shifts[0]
    return (device_move, device_shift, (transition, offset, fresh, carried, queries_grown, mixing))


def emit_step(carried_parts, span_parts):
    recurrent_state, accumulated_move = carried_parts
    span_move, span_shift, fresh_state_term, carried_state_term, query_term, mixing_part = (
        span_parts
    )
    state_update = fresh_state_term - jnp.einsum(
        "orm,omj->orj", carried_state_term, recurrent_state, precision=highest_precision
    )
    produced_output = jnp.einsum(
        "fmb,fbi->fmi", query_term, recurrent_state, precision=highest_precision
    ) + jnp.einsum("hts,hsv->htv", mixing_part, state_update, precision=highest_precision)
    start_weight = query_term - jnp.einsum(
        "hts,hsv->htv", mixing_part, carried_state_term, precision=highest_precision
    )
    start_query = matmul_heads(start_weight, accumulated_move)
    next_parts = (
        matmul_heads(span_move, recurrent_state) + span_shift,
        matmul_heads(span_move, accumulated_move),
    )
    return (next_parts, (produced_output, start_query))


def token_major(span_values):
    stacked = jnp.stack(span_values)
    block_count, heads, span_rows, _ = stacked.shape
    return stacked.transpose(1, 0, 2, 3).reshape(heads, block_count * span_rows, DK)


def finish_spans(start_state, local_outputs, start_queries):
    outputs = local_outputs + matmul_heads(start_queries, start_state)
    heads, length, _ = outputs.shape
    return outputs.transpose(1, 0, 2).reshape(length, heads * DK).astype(jnp.bfloat16)


def per_device(
    kda_inputs,
    gate_log,
    beta,
    conv_weight,
    kda_out_weight,
    residual,
    norm_gain,
    latent_weight,
    latent_gain,
    query_weight,
    up_weight,
):
    length = residual.shape[0]
    edge_rows = kda_inputs[:, length - (CONV - 1) :, :]
    earlier_rows = passed_along(edge_rows, "ctx", 1)
    extended = jnp.concatenate([earlier_rows, kda_inputs], axis=1).astype(jnp.float32)
    running = jnp.zeros(kda_inputs.shape, jnp.float32)
    for tap_index in range(CONV):
        running = (
            running
            + conv_weight[:, tap_index, None, :] * extended[:, tap_index : tap_index + length, :]
        )
    activated = jax.nn.silu(running)
    kda_query = rounded(unit_heads(activated[0]) * DK ** (-0.5))
    kda_key = rounded(unit_heads(activated[1]))
    kda_value = rounded(activated[2])
    device_move, device_shift, span_data = delta_rule(kda_query, kda_key, kda_value, gate_log, beta)
    heads = device_move.shape[0]
    span_count = span_data[0].shape[0]
    emit_carry = (
        jnp.zeros((heads, DK, DK), jnp.float32),
        jnp.broadcast_to(jnp.eye(DK, dtype=jnp.float32), (heads, DK, DK)),
    )
    produced = []

    def run_emit(emit_carry):
        span_index = len(produced)
        emit_carry, emitted = emit_step(emit_carry, tuple(part[span_index] for part in span_data))
        produced.append(emitted)
        return emit_carry

    ctx_size = lax.axis_size("ctx")
    group_size = heads // 2
    moves = [device_move[:group_size], device_move[group_size:]]
    shifts = [device_shift[:group_size], device_shift[group_size:]]
    distance = 1
    while distance < ctx_size:
        for group in range(len(moves)):
            move, shift = moves[group], shifts[group]
            if 2 * distance < ctx_size:
                sent = jnp.stack([move, shift]).astype(jnp.bfloat16)
                both_in = passed_along(sent, "ctx", distance).astype(jnp.float32)
                next_shift = matmul_heads(move, both_in[1]) + shift
                next_move = matmul_heads(move, both_in[0])
            else:
                shift_in = passed_along(shift.astype(jnp.bfloat16), "ctx", distance)
                next_shift = matmul_heads(move, shift_in.astype(jnp.float32)) + shift
                next_move = move
            if group == 0 and len(produced) < span_count:
                emit_carry = run_emit(emit_carry)
                next_shift, next_move, emit_carry = lax.optimization_barrier(
                    (next_shift, next_move, emit_carry)
                )
            moves[group], shifts[group] = next_move, next_shift
        distance *= 2
    shift = jnp.concatenate(shifts, axis=0)
    while len(produced) < span_count:
        emit_carry = run_emit(emit_carry)
    local_outputs = token_major([emitted[0] for emitted in produced])
    start_queries = token_major([emitted[1] for emitted in produced])
    start_state = jnp.concatenate(
        [passed_along(part.astype(jnp.bfloat16), "ctx", 1) for part in shifts], axis=0
    ).astype(jnp.float32)
    kda_core = finish_spans(start_state, local_outputs, start_queries)
    partial_proj = jnp.dot(kda_core, kda_out_weight, preferred_element_type=jnp.float32)
    stream_out = stream_after_head_sum(partial_proj, residual)
    normed, latent = prepare(stream_out, norm_gain, latent_weight, latent_gain)
    mla_query = jnp.dot(normed, query_weight, preferred_element_type=jnp.float32).astype(
        jnp.bfloat16
    )
    query_heads = mla_query.reshape(length, -1, DH)
    heads_mla = query_heads.shape[1]
    flat_up = up_weight.reshape(up_weight.shape[0], -1)
    my_first = lax.axis_index("ctx") * length
    query_positions = my_first + jnp.arange(length, dtype=jnp.int32)
    piece = gathered_earlier(latent)
    piece_rows = piece.shape[0]
    paired = (
        jnp.dot(piece, flat_up, preferred_element_type=jnp.float32)
        .astype(jnp.bfloat16)
        .reshape(piece_rows, 2, heads_mla, DH)
    )
    scores = jnp.einsum(
        "qhd,khd->hqk", query_heads, paired[:, 0], preferred_element_type=jnp.float32
    ) * DH ** (-0.5)
    key_positions = jnp.arange(piece_rows, dtype=jnp.int32)
    allowed = key_positions[None, :] <= query_positions[:, None]
    final_peak = jnp.max(jnp.where(allowed, scores, -1e30), axis=-1)
    weights = jnp.where(allowed, jnp.exp(scores - final_peak[..., None]), 0.0)
    final_total = jnp.sum(weights, axis=-1)
    final_mixed = jnp.einsum(
        "hqk,khd->hqd",
        weights.astype(jnp.bfloat16),
        paired[:, 1],
        preferred_element_type=jnp.float32,
    )
    attention_out = (
        (final_mixed / final_total[..., None])
        .transpose(1, 0, 2)
        .reshape(length, heads_mla * DH)
        .astype(jnp.bfloat16)
    )
    return (stream_out, attention_out)


def solution(mesh):
    in_specs = (
        P(None, "ctx", "head"),
        P("ctx", "head"),
        P("ctx", "head"),
        P(None, None, "head"),
        P("head", None),
        P("ctx", None),
        P(),
        P(),
        P(),
        P(None, "head"),
        P(None, None, "head"),
    )
    out_specs = (P("ctx", None), P("ctx", "head"))
    return jax.shard_map(
        per_device, mesh=mesh, in_specs=in_specs, out_specs=out_specs, check_vma=False
    )
```
